128 devices in a mesh: sector: 64 (over y, z, x_hi, core), lift: 2 (over x_lo).
Axes of the slice: x: 4 (x_hi: 2, x_lo: 2; x = x_hi * 2 + x_lo), y: 4, z: 4, core: 2. Of those that a mesh axis runs over, the one named last changes fastest.
Arguments:
- right_side: float32 [128, 262144], P('lift', 'sector'), may hold values from -40 to 40
- diagonal: float32 [262144], P('sector'), may hold values from 1.9 to 2.6
- coupling: float32 [262144], P('sector'), may hold values from 0.3 to 0.94
- local_inverse: bfloat16 [256, 1024, 2048], P('sector'), may hold values from -0.1 to 0.6
- coarse_basis: bfloat16 [256, 16, 1024], P('sector'), may hold values from -0.1875 to 0.1875
- coarse_inverse: float32 [4096, 4096], P('sector', 'lift'), may hold values from -8 to 12
Outputs:
- solution: float32 [128, 262144], P('lift', 'sector')
- residual: float32 [128, 262144], P('lift', 'sector')
The draws below stay inside these ranges and needn't reach their ends.
All inputs are finite; a program needn't handle non-finite values.
Results may differ from the reference program's by a relative error of at most 0.019.
Values may be sent and summed in bfloat16 or wider, within the bound.
No kernel may reach another device: no remote copies, remote signals or barrier semaphores. Data moves between devices by JAX's collectives and lax.ppermute only.
A program may use at most 128 MiB of HBM per device.

```python
import jax
import jax.numpy as jnp
from jax import lax

ORDER = 2048
OV = 512
MODES = 16
SWEEPS = 4
OUTER = 2
OWN = 1024
SUBS = 256
ROWS = 262144
NC = 4096
CASES = 128


def draw_right_side(key, part):
    keys = jax.random.split(key, 3)
    trend = jnp.exp(jnp.log(6.0) * (1.0 - jnp.arange(ROWS, dtype=jnp.float32) / ROWS)) / jnp.sqrt(6.0)
    rough = jnp.exp(jax.random.uniform(keys[1], (ROWS,), jnp.float32, jnp.log(0.5), jnp.log(2.0)))
    case_scale = jnp.exp(jax.random.uniform(keys[2], (CASES, 1), jnp.float32, jnp.log(0.2), jnp.log(2.0)))
    base = jnp.clip(jax.random.normal(keys[0], (CASES, ROWS), jnp.float32), -4.0, 4.0)
    return base * case_scale * trend[None, :] * rough[None, :]


def draw_local_inverse(key, part):
    keys = jax.random.split(key, 2)
    sigma = 0.1 / jnp.sqrt(float(ORDER))
    noise = jnp.clip(jax.random.normal(keys[0], (SUBS, OWN, ORDER), jnp.float32), -4.0, 4.0) * sigma
    level = 0.38 * jnp.exp(jax.random.uniform(keys[1], (SUBS, OWN, 1), jnp.float32, jnp.log(0.8), jnp.log(1.25)))
    placed = jnp.arange(ORDER)[None, None, :] == (jnp.arange(OWN) + OV)[None, :, None]
    return (noise + jnp.where(placed, level, 0.0)).astype(jnp.bfloat16)


def draw_coarse_inverse(key, part):
    keys = jax.random.split(key, 2)
    sigma = 1.0 / jnp.sqrt(float(NC))
    noise = jnp.clip(jax.random.normal(keys[0], (NC, NC), jnp.float32), -4.0, 4.0) * sigma
    level = jnp.exp(jax.random.uniform(keys[1], (NC,), jnp.float32, jnp.log(2.0), jnp.log(8.0)))
    return noise + jnp.diag(level)


def block_scale(key, shape, cuts, least, top_value):
    level = 1.0
    for axis_at, shards_of in cuts:
        steps = jax.random.uniform(jax.random.fold_in(jax.random.fold_in(key, 6), axis_at), (shards_of,), jnp.float32, least / len(cuts), top_value / len(cuts))
        level = level * jnp.repeat(jnp.exp(steps), shape[axis_at] // shards_of).reshape((-1,) + (1,) * (len(shape) - 1 - axis_at))
    return level


def normal_values(key, dims, deviation, bound, cuts=(), kind=jnp.bfloat16):
    drawn = jax.random.normal(key, dims, jnp.float32) * deviation
    if len(cuts) > 0:
        drawn = block_scale(key, dims, cuts, -0.22, 0.18) * drawn
    return jnp.clip(drawn, min=-bound, max=bound).astype(kind)


def setup_inputs(seed: int = 0) -> dict:
    key_list = jax.random.split(jax.random.key(seed), 7)
    return {
        "right_side": draw_right_side(jax.random.fold_in(key_list[6], 71), 0),
        "diagonal": jnp.clip(1.9 + 0.6999999 * jax.random.uniform(key_list[1], (ROWS,), jnp.float32) ** block_scale(key_list[1], (ROWS,), ((0, 64),), -0.2, 0.2), 1.9, 2.6),
        "coupling": jnp.clip(0.3 + 0.64 * jax.random.uniform(key_list[2], (ROWS,), jnp.float32) ** block_scale(key_list[2], (ROWS,), ((0, 64),), -0.2, 0.2), 0.3, 0.94),
        "local_inverse": draw_local_inverse(jax.random.fold_in(key_list[6], 71), 0),
        "coarse_basis": normal_values(key_list[4], (SUBS, MODES, OWN), OWN ** -0.5, 0.1875, ((0, 64),)),
        "coarse_inverse": draw_coarse_inverse(jax.random.fold_in(key_list[6], 71), 0),
    }


def apply_op(field, diagonal, coupling):
    return diagonal * field - coupling * (jnp.roll(field, 1, axis=1) + jnp.roll(field, -1, axis=1))


def reference(right_side, diagonal, coupling, local_inverse, coarse_basis, coarse_inverse):
    highest = lax.Precision.HIGHEST

    def correct(half_res):
        padded = jnp.concatenate([half_res[:, ROWS - OV:], half_res, half_res[:, :OV]], axis=1)

        def single(index):
            window = lax.dynamic_slice_in_dim(padded, index * OWN, ORDER, 1)
            inverse = lax.dynamic_index_in_dim(local_inverse, index, 0, keepdims=False)
            return jnp.dot(window.astype(jnp.float32), inverse.astype(jnp.float32).T, precision=highest)

        blocks = lax.map(single, jnp.arange(SUBS, dtype=jnp.int32))
        return jnp.transpose(blocks, (1, 0, 2)).reshape(CASES, ROWS)

    basis_wide = coarse_basis.astype(jnp.float32)
    solution = jnp.zeros_like(right_side)
    residual = right_side
    for outer_step in range(OUTER):
        update = correct(residual.astype(jnp.bfloat16))
        for sweep in range(SWEEPS - 1):
            sweep_res = (residual - apply_op(update, diagonal, coupling)).astype(jnp.bfloat16)
            update = update + correct(sweep_res)
        coarse_res = (residual - apply_op(update, diagonal, coupling)).astype(jnp.bfloat16)
        projected = jnp.einsum("cjk,jmk->cjm", coarse_res.reshape(CASES, SUBS, OWN).astype(jnp.float32), basis_wide, precision=highest).reshape(CASES, NC)
        coarse_sol = jnp.dot(projected, coarse_inverse.T, precision=highest)
        update = update + jnp.einsum("cjm,jmk->cjk", coarse_sol.reshape(CASES, SUBS, MODES), basis_wide, precision=highest).reshape(CASES, ROWS)
        image = apply_op(update, diagonal, coupling)
        alpha = jnp.sum(residual * image, axis=1) / (jnp.sum(image * image, axis=1) + 1e-6)
        solution = solution + alpha[:, None] * update
        residual = residual - alpha[:, None] * image
    return solution, residual
```

```python
import functools

import jax
import jax.numpy as jnp
from jax import lax
from jax.experimental import pallas as pl
from jax.experimental.pallas import tpu as pltpu
from jax.sharding import PartitionSpec as P

SWEEPS = 4
F32, BF16 = jnp.float32, jnp.bfloat16
CH = 512
TILE = 128


def lane_of(shape):
    return lax.broadcasted_iota(jnp.int32, shape, 1)


def dot_t(a, b):
    return lax.dot_general(a, b, (((1,), (1,)), ((), ())), preferred_element_type=F32)


def split(x):
    hi = x.astype(BF16)
    return hi, (x - hi.astype(F32)).astype(BF16)


def spread(x):
    hi = x.astype(BF16).astype(F32)
    lo = (x - hi).astype(BF16).astype(F32)
    lane = lane_of((x.shape[0], TILE))
    return jnp.where(lane == 0, hi, jnp.where(lane == 1, lo, 0.0)).astype(BF16)


def column(tile, at):
    return tile[:, at : at + 1].astype(F32) + tile[:, at + 1 : at + 2].astype(F32)


def op_chunk(cur, before, after, dg, cp):
    width = cur.shape[1]
    lane = lane_of(cur.shape)
    left = jnp.where(lane == 0, before, pltpu.roll(cur, 1, 1))
    right = jnp.where(lane == width - 1, after, pltpu.roll(cur, width - 1, 1))
    return dg * cur - cp * (left + right)


def parts(v_ref, u0_ref, u3_ref, own):
    total = v_ref.shape[1]

    def get(lo, hi):
        if hi <= own:
            return u0_ref[:, lo:hi]
        if lo >= total - own:
            return u3_ref[:, lo - (total - own) : hi - (total - own)]
        return v_ref[:, lo:hi]

    return get


def chunks_of(get, total):
    for lo in range(0, total, CH):
        hi = lo + CH
        before = get(lo - 1, lo) if lo > 0 else None
        after = get(hi, hi + 1) if hi < total else None
        yield lo, hi, get(lo, hi), before, after


def first_edges(r_ref, cp_ref, basis_ref, ci_ref, left_ref, right_ref):
    total = r_ref.shape[1]
    rows = r_ref.shape[0]
    lane = lane_of((16, TILE))
    for out, at, sub, tile_lo, shift, roll in (
        (left_ref, 0, 0, 0, 0, 2),
        (right_ref, total - CH, 3, 896, 127, 3),
    ):
        out[:, :CH] = r_ref[:, at : at + CH].astype(BF16)
        col = shift if at == 0 else TILE - 1
        coup = cp_ref[:, at : at + TILE] if at == 0 else cp_ref[:, total - TILE : total]
        one = coup[:, col : col + 1]
        meta = spread(jnp.broadcast_to(one, (rows, 1))).astype(F32)
        edge = basis_ref[sub][:, tile_lo : tile_lo + TILE].astype(F32)
        edge = pltpu.roll(edge, roll, 1) * one
        hi = edge.astype(BF16).astype(F32)
        lo = pltpu.roll(edge - hi, 1, 1)
        both = jnp.where(lane == 2, hi, jnp.where(lane == 3, lo, 0.0))
        out[:, CH : CH + TILE] = meta.astype(BF16)
        out[:16, CH : CH + TILE] = (meta[:16] + both).astype(BF16)
        weight = basis_ref[sub][:, tile_lo : tile_lo + TILE].astype(F32)[:, col : col + 1]
        line = jnp.sum(weight * ci_ref[sub * 16 : sub * 16 + 16, :], axis=0, keepdims=True)
        count = line.shape[1] // TILE
        out[:, CH + TILE :] = jnp.zeros((rows, TILE), BF16)
        out[:count, CH + TILE :] = jnp.concatenate(
            [line[:, k * TILE : (k + 1) * TILE] for k in range(count)], axis=0
        ).astype(BF16)


def products(s_ref, L_ref, own, order):
    total = s_ref.shape[1]
    margin = (order - own) // 2
    subs = L_ref.shape[0]
    for j in range(subs):
        lo, hi = j * own - margin, j * own - margin + order
        a = max(lo, TILE)
        b = min(hi, total - TILE)
        yield j, dot_t(s_ref[:, a:b], L_ref[j, :, a - lo : b - lo])


def middle_first(r_ref, L_ref, v_ref, s_ref):
    own, order = L_ref.shape[1], L_ref.shape[2]
    s_ref[...] = r_ref[...].astype(BF16)
    for j, p in products(s_ref, L_ref, own, order):
        v_ref[:, j * own : (j + 1) * own] = p


def middle(r_ref, v_ref, u0_ref, u3_ref, dg_ref, cp_ref, L_ref, out_ref, s_ref):
    own, order = L_ref.shape[1], L_ref.shape[2]
    get = parts(v_ref, u0_ref, u3_ref, own)
    for lo, hi, cur, before, after in chunks_of(get, r_ref.shape[1]):
        before = 0.0 if before is None else before
        after = 0.0 if after is None else after
        s = r_ref[:, lo:hi] - op_chunk(cur, before, after, dg_ref[:, lo:hi], cp_ref[:, lo:hi])
        s_ref[:, lo:hi] = s.astype(BF16)
    for j, p in products(s_ref, L_ref, own, order):
        out_ref[:, j * own : (j + 1) * own] = get(j * own, (j + 1) * own) + p


def edge_sends(r_ref, dg_ref, cp_ref, u0, u3, left_ref, right_ref):
    total = r_ref.shape[1]
    own = u0.shape[1]
    s = r_ref[:, :CH] - op_chunk(
        u0[:, :CH], 0.0, u0[:, CH : CH + 1], dg_ref[:, :CH], cp_ref[:, :CH]
    )
    left_ref[:, :CH] = s.astype(BF16)
    left_ref[:, CH : CH + TILE] = spread(u0[:, :1])
    at = total - CH
    s = r_ref[:, at:] - op_chunk(
        u3[:, own - CH :], u3[:, own - CH - 1 : own - CH], 0.0, dg_ref[:, at:], cp_ref[:, at:]
    )
    right_ref[:, :CH] = s.astype(BF16)
    right_ref[:, CH : CH + TILE] = spread(u3[:, own - 1 :])


def edges(first, send, *refs):
    (v_ref, gotl_ref, gotr_ref, ownl_ref, ownr_ref, metal_ref, metar_ref) = refs[:7]
    (r_ref, dg_ref, cp_ref, LhL_ref, LhR_ref) = refs[7:12]
    outs = refs[12:]
    total = v_ref.shape[1]
    own = LhL_ref.shape[0]
    tile_l, tile_r = ownl_ref[:, :TILE], ownr_ref[:, CH - TILE : CH]
    halo_l, halo_r = gotl_ref[:, :CH], gotr_ref[:, :CH]
    if not first:
        lane_t = lane_of(tile_l.shape)
        lane_h = lane_of(halo_l.shape)
        mine_l = column(ownl_ref[:, CH : CH + TILE], 0)
        mine_r = column(ownr_ref[:, CH : CH + TILE], 0)
        rim_l = column(gotl_ref[:, CH : CH + TILE], 0)
        rim_r = column(gotr_ref[:, CH : CH + TILE], 0)
        coup_l = column(metal_ref[...], 0)
        coup_r = column(metar_ref[...], 0)
        add = lambda x, lane, at, y: (x.astype(F32) + jnp.where(lane == at, y, 0.0)).astype(BF16)
        tile_l = add(tile_l, lane_t, 0, cp_ref[:, :1] * rim_l)
        tile_r = add(tile_r, lane_t, TILE - 1, cp_ref[:, total - 1 :] * rim_r)
        halo_l = add(halo_l, lane_h, CH - 1, coup_l * mine_l)
        halo_r = add(halo_r, lane_h, 0, coup_r * mine_r)
    u0 = v_ref[:, :own] + (
        dot_t(halo_l, LhL_ref[:, :CH]) + dot_t(tile_l, LhL_ref[:, CH:])
    )
    u3 = v_ref[:, total - own :] + (
        dot_t(halo_r, LhR_ref[:, TILE:]) + dot_t(tile_r, LhR_ref[:, :TILE])
    )
    outs[0][...] = u0
    outs[1][...] = u3
    if send:
        edge_sends(r_ref, dg_ref, cp_ref, u0, u3, outs[2], outs[3])


def project(v_ref, u0_ref, u3_ref, r_ref, dg_ref, cp_ref, basis_ref, metal_ref, metar_ref, out_ref):
    rows, total = r_ref.shape
    own = basis_ref.shape[2]
    get = parts(v_ref, u0_ref, u3_ref, own)
    lane = lane_of((rows, TILE))
    sums = []
    for lo, hi, cur, before, after in chunks_of(get, total):
        before = 0.0 if before is None else before
        after = 0.0 if after is None else after
        s = r_ref[:, lo:hi] - op_chunk(cur, before, after, dg_ref[:, lo:hi], cp_ref[:, lo:hi])
        j, k = lo // own, lo % own
        sums.append(dot_t(s.astype(BF16), basis_ref[j, :, k : k + CH]))
    per = own // CH
    pieces = []
    for j in range(total // own):
        p = sums[j * per]
        for k in range(1, per):
            p = p + sums[j * per + k]
        pieces.append(p)
    first, last = get(0, 1), get(total - 1, total)
    pick = (lane == 2) | (lane == 3)
    for value, meta in ((first, metal_ref), (last, metar_ref)):
        hi, lo = split(value)
        coef = meta[:16, :]
        pieces.append(
            dot_t(jnp.where(pick, hi.astype(F32), 0.0).astype(BF16), coef)
            + dot_t(jnp.where(pick, lo.astype(F32), 0.0).astype(BF16), coef)
        )
    rims = jnp.zeros((rows, 32), F32)
    lane32 = lane_of((rows, 32))
    for k, value in enumerate((first, last)):
        hi, lo = split(value)
        rims = jnp.where(lane32 == 2 * k, hi.astype(F32), rims)
        rims = jnp.where(lane32 == 2 * k + 1, lo.astype(F32), rims)
    chunk = jnp.concatenate(pieces + [rims], axis=1).astype(BF16)
    for d in range(out_ref.shape[0]):
        out_ref[d] = chunk


def coarse(at_ref, got_ref, W_ref, v_ref, u0_ref, u3_ref, r_ref, dg_ref, cp_ref, basis_ref,
           x_ref, image_ref, sums_ref, left_ref, right_ref):
    rows, total = r_ref.shape
    own = basis_ref.shape[2]
    modes = basis_ref.shape[1]
    get = parts(v_ref, u0_ref, u3_ref, own)
    c = jnp.zeros((rows, W_ref.shape[1]), F32)
    for d in range(got_ref.shape[0]):
        c = c + dot_t(got_ref[d], W_ref[d])
    subs = total // own
    for j in range(subs):
        hi, lo = split(c[:, j * modes : (j + 1) * modes])
        for k in range(0, own, CH):
            b = basis_ref[j, :, k : k + CH]
            at = j * own + k
            x_ref[:, at : at + CH] = get(at, at + CH) + (
                jnp.dot(hi, b, preferred_element_type=F32)
                + jnp.dot(lo, b, preferred_element_type=F32)
            )
    n = subs * modes
    before = got_ref[at_ref[0]]
    after = got_ref[at_ref[1]]
    rim_l = column(before, 98) + c[:, n : n + 1]
    rim_r = column(after, 96) + c[:, n + 1 : n + 2]
    num = jnp.zeros((rows, 1), F32)
    den = jnp.zeros((rows, 1), F32)
    read = lambda lo, hi: x_ref[:, lo:hi]
    for lo, hi, cur, b, a in chunks_of(read, total):
        b = rim_l if b is None else b
        a = rim_r if a is None else a
        image = op_chunk(cur, b, a, dg_ref[:, lo:hi], cp_ref[:, lo:hi])
        image_ref[:, lo:hi] = image
        num = num + jnp.sum(r_ref[:, lo:hi] * image, axis=1, keepdims=True)
        den = den + jnp.sum(image * image, axis=1, keepdims=True)
        if left_ref is not None and lo == 0:
            left_ref[...] = image.astype(BF16)
        if right_ref is not None and hi == total:
            right_ref[...] = image.astype(BF16)
    both = jnp.concatenate([num, den], axis=0)
    flat = jnp.transpose(jnp.broadcast_to(both, (2 * rows, 2 * rows)))
    sums_ref[...] = flat[: sums_ref.shape[0]]


def coarse_last(*refs):
    coarse(*refs, None, None)


def step_of(sums_ref, rows):
    s = jnp.sum(sums_ref[...], axis=0, keepdims=True)
    t = jnp.transpose(jnp.broadcast_to(s, (2 * rows, 2 * rows)))
    return t[:rows, :1] / (t[rows:, :1] + 1e-6)


def second(sums_ref, x_ref, image_ref, r_ref, hl0_ref, hr0_ref, hl_ref, hr_ref, dg_ref, cp_ref,
           L_ref, sol_ref, res_ref, u_ref, u0_ref, u3_ref, left_ref, right_ref, s_ref):
    rows, total = r_ref.shape
    own, order = L_ref.shape[1], L_ref.shape[2]
    alpha = step_of(sums_ref, rows)
    s_ref[:, :CH] = (hl0_ref[:, :CH].astype(F32) - alpha * hl_ref[...].astype(F32)).astype(BF16)
    s_ref[:, CH + total :] = (
        hr0_ref[:, :CH].astype(F32) - alpha * hr_ref[...].astype(F32)
    ).astype(BF16)
    for lo in range(0, total, CH):
        hi = lo + CH
        r = r_ref[:, lo:hi] - alpha * image_ref[:, lo:hi]
        res_ref[:, lo:hi] = r
        sol_ref[:, lo:hi] = alpha * x_ref[:, lo:hi]
        s_ref[:, CH + lo : CH + hi] = r.astype(BF16)
    subs = L_ref.shape[0]
    outer = []
    for j in range(subs):
        p = dot_t(s_ref[:, j * own : j * own + order], L_ref[j])
        u_ref[:, j * own : (j + 1) * own] = p
        if j == 0:
            u0_ref[...] = p
        if j == subs - 1:
            u3_ref[...] = p
    edge_sends(res_ref, dg_ref, cp_ref, u0_ref[...], u3_ref[...], left_ref, right_ref)


def finish(sums_ref, x_ref, image_ref, r_ref, sol_in_ref, sol_ref, res_ref):
    rows, total = r_ref.shape
    alpha = step_of(sums_ref, rows)
    for lo in range(0, total, CH):
        hi = lo + CH
        res_ref[:, lo:hi] = r_ref[:, lo:hi] - alpha * image_ref[:, lo:hi]
        sol_ref[:, lo:hi] = sol_in_ref[:, lo:hi] + alpha * x_ref[:, lo:hi]


def call(kernel, name, outs, args, scratch=(), limit=12, flops=0, smem=0):
    vmem = pl.BlockSpec(memory_space=pltpu.VMEM)
    size = sum(a.size * a.dtype.itemsize for a in args)
    return pl.pallas_call(
        kernel,
        out_shape=outs,
        in_specs=[pl.BlockSpec(memory_space=pltpu.SMEM)] * smem + [vmem] * (len(args) - smem),
        out_specs=jax.tree.map(lambda _: vmem, outs),
        scratch_shapes=list(scratch),
        compiler_params=pltpu.CompilerParams(vmem_limit_bytes=limit << 20),
        cost_estimate=pl.CostEstimate(flops=flops, bytes_accessed=size, transcendentals=0),
        name=name,
    )(*args)


def body(right_side, diagonal, coupling, local_inverse, coarse_basis, coarse_inverse):
    rows, total = right_side.shape
    subs, own, order = local_inverse.shape
    modes = coarse_basis.shape[1]
    sectors = lax.axis_size("sector")
    ring = [(i, (i + 1) % sectors) for i in range(sectors)]
    back = [(b, a) for a, b in ring]
    here = lax.axis_index("sector")
    around = jnp.stack([(here + sectors - 1) % sectors, (here + 1) % sectors]).astype(jnp.int32)
    L, basis = local_inverse, coarse_basis
    r = right_side
    dg, cp = diagonal.reshape(1, total), coupling.reshape(1, total)
    wide = CH + TILE
    shape = jax.ShapeDtypeStruct
    full = shape((rows, total), F32)
    sub = shape((rows, own), F32)
    send = shape((rows, wide), BF16)
    s_scratch = pltpu.VMEM((rows, total), BF16)
    work = 2 * rows * subs * own * order

    def exchange(to_left, to_right):
        got_left = lax.ppermute(to_right, "sector", ring)
        got_right = lax.ppermute(to_left, "sector", back)
        return got_left, got_right

    sl, sr = call(
        first_edges, "first_edges", [shape((rows, wide + TILE), BF16)] * 2,
        [r, cp, basis, coarse_inverse],
    )
    got_l, got_r = exchange(sl, sr)
    LhL, LhR = L[0, :, :wide], L[subs - 1, :, order - wide :]
    v = call(middle_first, "middle_first", full, [r, L], [s_scratch], 26, work)
    meta_l, meta_r = got_l[:, CH : CH + TILE], got_r[:, CH : CH + TILE]
    halo_l0, halo_r0 = got_l, got_r

    lines = jnp.concatenate(
        [
            coarse_inverse.astype(BF16),
            got_l[: coarse_inverse.shape[1] // TILE, CH + TILE :].reshape(1, -1),
            got_r[: coarse_inverse.shape[1] // TILE, CH + TILE :].reshape(1, -1),
            jnp.zeros((6, coarse_inverse.shape[1]), BF16),
        ],
        axis=0,
    )
    other = lax.ppermute(lines, "lift", [(0, 1), (1, 0)])
    low = lax.axis_index("lift") == 0
    both = jnp.stack([jnp.where(low, lines, other), jnp.where(low, other, lines)], axis=1)
    per = subs * modes
    grid = both.reshape(lines.shape[0], sectors, per).transpose(1, 0, 2)
    W = jnp.concatenate(
        [
            grid,
            jnp.roll(grid[:, :, per - modes :], 1, axis=0),
            jnp.roll(grid[:, :, :modes], -1, axis=0),
            jnp.zeros((sectors, lines.shape[0], TILE - per - 2 * modes), BF16),
        ],
        axis=2,
    )

    def sweeps(v, u0, u3, sl, sr, start):
        for sweep in range(start, SWEEPS):
            last = sweep == SWEEPS - 1
            if sweep == 0:
                vv, gl, gr = v, got_l, got_r
            else:
                gl, gr = exchange(sl, sr)
                vv = call(
                    middle, f"middle", full, [r, v, u0, u3, dg, cp, L], [s_scratch], 28, work
                )
            outs = call(
                functools.partial(edges, sweep == 0, not last), f"edges_{sweep}",
                [sub, sub] if last else [sub, sub, send, send],
                [vv, gl, gr, sl, sr, meta_l, meta_r, r, dg, cp, LhL, LhR],
                limit=14,
                flops=work // 8,
            )
            v, u0, u3 = vv, outs[0], outs[1]
            if not last:
                sl, sr = outs[2], outs[3]
        return v, u0, u3

    def coarse_step(v, u0, u3, kernel, extra):
        chunk = call(
            project, "project", shape((sectors, rows, TILE), BF16),
            [v, u0, u3, r, dg, cp, basis, meta_l, meta_r],
        )
        got = lax.all_to_all(chunk, "sector", 0, 0, tiled=True)
        return call(
            kernel, "coarse", [full, full, shape((sectors, 2 * rows), F32)] + extra,
            [around, got, W, v, u0, u3, r, dg, cp, basis], limit=16, smem=1,
        )

    v, u0, u3 = sweeps(v, None, None, sl, sr, 0)
    edge = shape((rows, CH), BF16)
    x, image, sums, il, ir = coarse_step(v, u0, u3, coarse, [edge, edge])
    halo_l, halo_r = exchange(il, ir)
    sums = lax.all_to_all(sums, "sector", 0, 0, tiled=True)
    sol, r, v, u0, u3, sl, sr = call(
        second, "second", [full, full, full, sub, sub, send, send],
        [sums, x, image, r, halo_l0, halo_r0, halo_l, halo_r, dg, cp, L],
        [pltpu.VMEM((rows, total + 2 * CH), BF16)], 30, work,
    )
    v, u0, u3 = sweeps(v, u0, u3, sl, sr, 1)
    x, image, sums = coarse_step(v, u0, u3, coarse_last, [])
    sums = lax.all_to_all(sums, "sector", 0, 0, tiled=True)
    sol, res = call(finish, "finish", [full, full], [sums, x, image, r, sol])
    return sol, res


def solution(mesh):
    in_specs = (
        P("lift", "sector"),
        P("sector"),
        P("sector"),
        P("sector", None, None),
        P("sector", None, None),
        P("sector", "lift"),
    )
    out_specs = (P("lift", "sector"), P("lift", "sector"))
    return jax.shard_map(body, mesh=mesh, in_specs=in_specs, out_specs=out_specs, check_vma=False)
```

```python
import functools

import jax
import jax.numpy as jnp
from jax import lax
from jax.experimental import pallas as pl
from jax.experimental.pallas import tpu as pltpu
from jax.sharding import PartitionSpec as P

SWEEPS = 4
F32, BF16 = jnp.float32, jnp.bfloat16
CH = 512
TILE = 128


def lane_of(shape):
    return lax.broadcasted_iota(jnp.int32, shape, 1)


def dot_t(a, b):
    return lax.dot_general(a, b, (((1,), (1,)), ((), ())), preferred_element_type=F32)


def split(x):
    hi = x.astype(BF16)
    return hi, (x - hi.astype(F32)).astype(BF16)


def spread(x):
    hi = x.astype(BF16).astype(F32)
    lo = (x - hi).astype(BF16).astype(F32)
    lane = lane_of((x.shape[0], TILE))
    return jnp.where(lane == 0, hi, jnp.where(lane == 1, lo, 0.0)).astype(BF16)


def column(tile, at):
    return tile[:, at : at + 1].astype(F32) + tile[:, at + 1 : at + 2].astype(F32)


def op_chunk(cur, before, after, dg, cp):
    width = cur.shape[1]
    lane = lane_of(cur.shape)
    left = jnp.where(lane == 0, before, pltpu.roll(cur, 1, 1))
    right = jnp.where(lane == width - 1, after, pltpu.roll(cur, width - 1, 1))
    return dg * cur - cp * (left + right)


def parts(v_ref, u0_ref, u3_ref, own):
    total = v_ref.shape[1]

    def get(lo, hi):
        if hi <= own:
            return u0_ref[:, lo:hi]
        if lo >= total - own:
            return u3_ref[:, lo - (total - own) : hi - (total - own)]
        return v_ref[:, lo:hi]

    return get


def chunks_of(get, total):
    for lo in range(0, total, CH):
        hi = lo + CH
        before = get(lo - 1, lo) if lo > 0 else None
        after = get(hi, hi + 1) if hi < total else None
        yield lo, hi, get(lo, hi), before, after


def pick(core_ref, a_ref, b_ref, left_ref, right_ref):
    @pl.when(core_ref[0] == 0)
    def _():
        left_ref[...] = b_ref[...]
        right_ref[...] = a_ref[...]

    @pl.when(core_ref[0] != 0)
    def _():
        left_ref[...] = a_ref[...]
        right_ref[...] = b_ref[...]


def first_edges(core_ref, r_hbm, cp_hbm, basis_hbm, ci_hbm, a_ref, b_ref,
                r_ref, cp_ref, basis_ref, ci_ref, left_ref, right_ref, sem):
    rows, total = r_hbm.shape
    subs, modes, own = basis_hbm.shape
    copies = []
    for k, (at, sub, tile_lo, cp_lo) in enumerate(
        ((0, 0, 0, 0), (total - CH, subs - 1, own - TILE, total - TILE))
    ):
        for n, (src, dst) in enumerate(
            (
                (r_hbm.at[:, pl.ds(at, CH)], r_ref.at[k]),
                (cp_hbm.at[:, pl.ds(cp_lo, TILE)], cp_ref.at[k]),
                (basis_hbm.at[sub, :, pl.ds(tile_lo, TILE)], basis_ref.at[k]),
                (ci_hbm.at[pl.ds(sub * modes, modes), :], ci_ref.at[k]),
            )
        ):
            copies.append(pltpu.make_async_copy(src, dst, sem.at[4 * k + n]))
    for c in copies:
        c.start()
    for c in copies:
        c.wait()
    lane = lane_of((modes, TILE))
    for k, (out, col, roll) in enumerate(((left_ref, 0, 2), (right_ref, TILE - 1, 3))):
        out[:, :CH] = r_ref[k].astype(BF16)
        one = cp_ref[k][:, col : col + 1]
        meta = spread(jnp.broadcast_to(one, (rows, 1))).astype(F32)
        weight = basis_ref[k].astype(F32)
        edge = pltpu.roll(weight, roll, 1) * one
        hi = edge.astype(BF16).astype(F32)
        lo = pltpu.roll(edge - hi, 1, 1)
        both = jnp.where(lane == 2, hi, jnp.where(lane == 3, lo, 0.0))
        out[:, CH : CH + TILE] = meta.astype(BF16)
        out[:modes, CH : CH + TILE] = (meta[:modes] + both).astype(BF16)
        line = jnp.sum(weight[:, col : col + 1] * ci_ref[k], axis=0, keepdims=True)
        count = line.shape[1] // TILE
        out[:, CH + TILE :] = jnp.zeros((rows, TILE), BF16)
        out[:count, CH + TILE :] = jnp.concatenate(
            [line[:, n * TILE : (n + 1) * TILE] for n in range(count)], axis=0
        ).astype(BF16)
    send_pair(core_ref, left_ref, right_ref, a_ref, b_ref)


def send_pair(core_ref, left_ref, right_ref, a_ref, b_ref):
    @pl.when(core_ref[0] == 0)
    def _():
        a_ref[...] = right_ref[...]
        b_ref[...] = left_ref[...]

    @pl.when(core_ref[0] != 0)
    def _():
        a_ref[...] = left_ref[...]
        b_ref[...] = right_ref[...]


def lines_of(core_ref, ci_ref, a_ref, b_ref, out_ref, left_ref, right_ref):
    pick(core_ref, a_ref, b_ref, left_ref, right_ref)
    rows, width = ci_ref.shape
    out_ref[:rows, :] = ci_ref[...].astype(BF16)
    extra = []
    for ref in (left_ref, right_ref):
        block = ref[:, CH + TILE :].astype(F32)
        extra.append(
            jnp.concatenate([block[k : k + 1, :] for k in range(width // TILE)], axis=1)
        )
    extra.append(jnp.zeros((6, width), F32))
    out_ref[rows:, :] = jnp.concatenate(extra, axis=0).astype(BF16)


def weave(core_ref, mine_ref, other_ref, out_ref, all_ref):
    rows, half = mine_ref.shape
    low = core_ref[3] == 0

    @pl.when(low)
    def _():
        all_ref[:, TILE : TILE + half] = mine_ref[...].astype(F32)
        all_ref[:, TILE + half : TILE + 2 * half] = other_ref[...].astype(F32)

    @pl.when(jnp.logical_not(low))
    def _():
        all_ref[:, TILE : TILE + half] = other_ref[...].astype(F32)
        all_ref[:, TILE + half : TILE + 2 * half] = mine_ref[...].astype(F32)

    all_ref[:, :TILE] = all_ref[:, 2 * half : 2 * half + TILE]
    all_ref[:, 2 * half + TILE :] = all_ref[:, TILE : 2 * TILE]
    lane = lane_of((rows, TILE))
    core = core_ref[0]
    zero = jnp.zeros((rows, TILE), F32)

    def step(k, carry):
        at = pl.multiple_of(k * TILE, TILE)
        prev = all_ref[:, pl.ds(at, TILE)]
        tile = all_ref[:, pl.ds(pl.multiple_of(at + TILE, TILE), TILE)]
        after = all_ref[:, pl.ds(pl.multiple_of(at + 2 * TILE, TILE), TILE)]
        near = pltpu.roll(tile, 16, 1)
        even = jnp.where(lane < 64, tile, jnp.where(lane < 80, pltpu.roll(prev, 80, 1), near))
        odd = jnp.where(lane < 64, pltpu.roll(tile, 64, 1), jnp.where(lane < 80, near, pltpu.roll(after, 80, 1)))
        at = 2 * k * TILE
        out_ref[:, pl.ds(pl.multiple_of(at + core * TILE, TILE), TILE)] = jnp.where(
            lane < 96, even, zero
        ).astype(BF16)
        out_ref[:, pl.ds(pl.multiple_of(at + (1 - core) * TILE, TILE), TILE)] = jnp.where(
            lane < 96, odd, zero
        ).astype(BF16)
        return carry

    lax.fori_loop(0, 2 * half // TILE, step, 0)


def products(s_ref, L_ref, own, order, store):
    total = s_ref.shape[1]
    margin = (order - own) // 2
    subs = L_ref.shape[0]
    part = own // 2

    def rows_at(k):
        return pl.ds(pl.multiple_of(k * part, part), part)

    def first(k, carry):
        p = dot_t(s_ref[:, TILE : order - margin], L_ref[0, rows_at(k), margin + TILE :])
        store(pl.multiple_of(k * part, part), part, p)
        return carry

    def last(k, carry):
        start = (subs - 1) * own - margin
        p = dot_t(
            s_ref[:, start : total - TILE], L_ref[subs - 1, rows_at(k), : total - TILE - start]
        )
        store(pl.multiple_of((subs - 1) * own + k * part, part), part, p)
        return carry

    def inner(n, carry):
        j, k = 1 + n // 2, n % 2
        start = pl.multiple_of(j * own - margin, TILE)
        p = dot_t(s_ref[:, pl.ds(start, order)], L_ref[j, rows_at(k), :])
        store(pl.multiple_of(j * own + k * part, part), part, p)
        return carry

    lax.fori_loop(0, 2, first, 0)
    lax.fori_loop(0, 2 * (subs - 2), inner, 0)
    lax.fori_loop(0, 2, last, 0)


def middle_first(r_ref, L_ref, v_ref, s_ref):
    own, order = L_ref.shape[1], L_ref.shape[2]
    s_ref[...] = r_ref[...].astype(BF16)

    def store(at, size, p):
        v_ref[:, pl.ds(at, size)] = p

    products(s_ref, L_ref, own, order, store)


def middle(r_ref, v_ref, u0_ref, u3_ref, dg_ref, cp_ref, L_ref, out_ref, s_ref):
    own, order = L_ref.shape[1], L_ref.shape[2]
    get = parts(v_ref, u0_ref, u3_ref, own)
    for lo, hi, cur, before, after in chunks_of(get, r_ref.shape[1]):
        before = 0.0 if before is None else before
        after = 0.0 if after is None else after
        s = r_ref[:, lo:hi] - op_chunk(cur, before, after, dg_ref[:, lo:hi], cp_ref[:, lo:hi])
        s_ref[:, lo:hi] = s.astype(BF16)
        out_ref[:, lo:hi] = cur

    def store(at, size, p):
        out_ref[:, pl.ds(at, size)] += p

    products(s_ref, L_ref, own, order, store)


def edge_sends(r_ref, dg_ref, cp_ref, u0, u3, left_ref, right_ref):
    total = r_ref.shape[1]
    own = u0.shape[1]
    s = r_ref[:, :CH] - op_chunk(
        u0[:, :CH], 0.0, u0[:, CH : CH + 1], dg_ref[:, :CH], cp_ref[:, :CH]
    )
    left_ref[:, :CH] = s.astype(BF16)
    left_ref[:, CH : CH + TILE] = spread(u0[:, :1])
    at = total - CH
    s = r_ref[:, at:] - op_chunk(
        u3[:, own - CH :], u3[:, own - CH - 1 : own - CH], 0.0, dg_ref[:, at:], cp_ref[:, at:]
    )
    right_ref[:, :CH] = s.astype(BF16)
    right_ref[:, CH : CH + TILE] = spread(u3[:, own - 1 :])


def edges(first, send, *refs):
    (core_ref, v_ref, gota_ref, gotb_ref, owna_ref, ownb_ref, metaa_ref, metab_ref) = refs[:8]
    (r_ref, dg_ref, cp_ref, L_ref) = refs[8:12]
    outs = refs[12 : 16 if send else 14]
    (gotl_ref, gotr_ref, ownl_ref, ownr_ref, metal_ref, metar_ref, sl_ref, sr_ref) = refs[-8:]
    total = v_ref.shape[1]
    subs, own, order = L_ref.shape
    wide = CH + TILE
    pick(core_ref, gota_ref, gotb_ref, gotl_ref, gotr_ref)
    pick(core_ref, owna_ref, ownb_ref, ownl_ref, ownr_ref)
    tile_l, tile_r = ownl_ref[:, :TILE], ownr_ref[:, CH - TILE : CH]
    halo_l, halo_r = gotl_ref[:, :CH], gotr_ref[:, :CH]
    if not first:
        pick(core_ref, metaa_ref, metab_ref, metal_ref, metar_ref)
        lane_t = lane_of(tile_l.shape)
        lane_h = lane_of(halo_l.shape)
        mine_l = column(ownl_ref[:, CH : CH + TILE], 0)
        mine_r = column(ownr_ref[:, CH : CH + TILE], 0)
        rim_l = column(gotl_ref[:, CH : CH + TILE], 0)
        rim_r = column(gotr_ref[:, CH : CH + TILE], 0)
        coup_l = column(metal_ref[:, CH : CH + TILE], 0)
        coup_r = column(metar_ref[:, CH : CH + TILE], 0)
        add = lambda x, lane, at, y: (x.astype(F32) + jnp.where(lane == at, y, 0.0)).astype(BF16)
        tile_l = add(tile_l, lane_t, 0, cp_ref[:, :1] * rim_l)
        tile_r = add(tile_r, lane_t, TILE - 1, cp_ref[:, total - 1 :] * rim_r)
        halo_l = add(halo_l, lane_h, CH - 1, coup_l * mine_l)
        halo_r = add(halo_r, lane_h, 0, coup_r * mine_r)
    u0 = v_ref[:, :own] + (
        dot_t(halo_l, L_ref[0, :, :CH]) + dot_t(tile_l, L_ref[0, :, CH:wide])
    )
    u3 = v_ref[:, total - own :] + (
        dot_t(halo_r, L_ref[subs - 1, :, order - CH :])
        + dot_t(tile_r, L_ref[subs - 1, :, order - wide : order - CH])
    )
    outs[0][...] = u0
    outs[1][...] = u3
    if send:
        edge_sends(r_ref, dg_ref, cp_ref, u0, u3, sl_ref, sr_ref)
        send_pair(core_ref, sl_ref, sr_ref, outs[2], outs[3])


def project(core_ref, v_ref, u0_ref, u3_ref, r_ref, dg_ref, cp_ref, basis_ref, metaa_ref, metab_ref,
            out_ref, metal_ref, metar_ref):
    rows, total = r_ref.shape
    own = basis_ref.shape[2]
    modes = basis_ref.shape[1]
    get = parts(v_ref, u0_ref, u3_ref, own)
    lane = lane_of((rows, TILE))
    pick(core_ref, metaa_ref, metab_ref, metal_ref, metar_ref)
    sums = []
    for lo, hi, cur, before, after in chunks_of(get, total):
        before = 0.0 if before is None else before
        after = 0.0 if after is None else after
        s = r_ref[:, lo:hi] - op_chunk(cur, before, after, dg_ref[:, lo:hi], cp_ref[:, lo:hi])
        j, k = lo // own, lo % own
        sums.append(dot_t(s.astype(BF16), basis_ref[j, :, k : k + CH]))
    per = own // CH
    pieces = []
    for j in range(total // own):
        p = sums[j * per]
        for k in range(1, per):
            p = p + sums[j * per + k]
        pieces.append(p)
    first, last = get(0, 1), get(total - 1, total)
    chosen = (lane == 2) | (lane == 3)
    for value, meta in ((first, metal_ref), (last, metar_ref)):
        hi, lo = split(value)
        coef = meta[:modes, CH : CH + TILE]
        pieces.append(
            dot_t(jnp.where(chosen, hi.astype(F32), 0.0).astype(BF16), coef)
            + dot_t(jnp.where(chosen, lo.astype(F32), 0.0).astype(BF16), coef)
        )
    rims = jnp.zeros((rows, 32), F32)
    lane32 = lane_of((rows, 32))
    for k, value in enumerate((first, last)):
        hi, lo = split(value)
        rims = jnp.where(lane32 == 2 * k, hi.astype(F32), rims)
        rims = jnp.where(lane32 == 2 * k + 1, lo.astype(F32), rims)
    chunk = jnp.concatenate(pieces + [rims], axis=1).astype(BF16)
    for d in range(out_ref.shape[0]):
        out_ref[d] = chunk


def coarse(send, core_ref, mine_ref, other_ref, W_ref, v_ref, u0_ref, u3_ref, r_ref, dg_ref, cp_ref,
           basis_ref, x_ref, image_ref, sums_ref, *rest):
    rows, total = r_ref.shape
    own = basis_ref.shape[2]
    modes = basis_ref.shape[1]
    get = parts(v_ref, u0_ref, u3_ref, own)
    count = mine_ref.shape[0]
    group = min(8, count)
    c = None
    for k in range(0, count, group):
        tiles = []
        for d in range(k, k + group):
            tiles += [mine_ref[d], other_ref[d]]
        p = dot_t(
            jnp.concatenate(tiles, axis=1), W_ref[:, 2 * k * TILE : 2 * (k + group) * TILE]
        )
        c = p if c is None else c + p
    subs = total // own
    for j in range(subs):
        hi, lo = split(c[:, j * modes : (j + 1) * modes])
        both = jnp.concatenate([hi, lo], axis=1)
        for k in range(0, own, CH):
            b = basis_ref[j, :, k : k + CH]
            at = j * own + k
            x_ref[:, at : at + CH] = get(at, at + CH) + jnp.dot(
                both, jnp.concatenate([b, b], axis=0), preferred_element_type=F32
            )
    n = subs * modes
    before = other_ref[core_ref[1]]
    after = other_ref[core_ref[2]]
    rim_l = column(before, 98) + c[:, n : n + 1]
    rim_r = column(after, 96) + c[:, n + 1 : n + 2]
    num = jnp.zeros((rows, 1), F32)
    den = jnp.zeros((rows, 1), F32)
    read = lambda lo, hi: x_ref[:, lo:hi]
    for lo, hi, cur, b, a in chunks_of(read, total):
        b = rim_l if b is None else b
        a = rim_r if a is None else a
        image = op_chunk(cur, b, a, dg_ref[:, lo:hi], cp_ref[:, lo:hi])
        image_ref[:, lo:hi] = image
        num = num + jnp.sum(r_ref[:, lo:hi] * image, axis=1, keepdims=True)
        den = den + jnp.sum(image * image, axis=1, keepdims=True)
    both = jnp.concatenate([num, den], axis=0)
    flat = jnp.transpose(jnp.broadcast_to(both, (2 * rows, 2 * rows)))
    sums_ref[...] = flat[: sums_ref.shape[0]]
    if send:
        a_ref, b_ref, left_ref, right_ref = rest
        left_ref[...] = image_ref[:, :CH].astype(BF16)
        right_ref[...] = image_ref[:, total - CH :].astype(BF16)
        send_pair(core_ref, left_ref, right_ref, a_ref, b_ref)


def step_of(sums_ref, rows):
    s = jnp.sum(sums_ref[...], axis=0, keepdims=True)
    t = jnp.transpose(jnp.broadcast_to(s, (2 * rows, 2 * rows)))
    return t[:rows, :1] / (t[rows:, :1] + 1e-6)


def second(core_ref, sums_ref, x_ref, image_ref, r_ref, ha0_ref, hb0_ref, ha_ref, hb_ref,
           dg_ref, cp_ref, L_ref, sol_ref, res_ref, u_ref, u0_ref, u3_ref, a_ref, b_ref,
           s_ref, sl_ref, sr_ref, hl0_ref, hr0_ref, hl_ref, hr_ref):
    rows, total = r_ref.shape
    own, order = L_ref.shape[1], L_ref.shape[2]
    alpha = step_of(sums_ref, rows)
    pick(core_ref, ha0_ref, hb0_ref, hl0_ref, hr0_ref)
    pick(core_ref, ha_ref, hb_ref, hl_ref, hr_ref)
    s_ref[:, :CH] = (hl0_ref[:, :CH].astype(F32) - alpha * hl_ref[...].astype(F32)).astype(BF16)
    s_ref[:, CH + total :] = (
        hr0_ref[:, :CH].astype(F32) - alpha * hr_ref[...].astype(F32)
    ).astype(BF16)
    for lo in range(0, total, CH):
        hi = lo + CH
        r = r_ref[:, lo:hi] - alpha * image_ref[:, lo:hi]
        res_ref[:, lo:hi] = r
        sol_ref[:, lo:hi] = alpha * x_ref[:, lo:hi]
        s_ref[:, CH + lo : CH + hi] = r.astype(BF16)
    subs = L_ref.shape[0]
    part = own // 2

    def step(n, carry):
        j, k = n // 2, n % 2
        p = dot_t(
            s_ref[:, pl.ds(pl.multiple_of(j * own, own), order)],
            L_ref[j, pl.ds(pl.multiple_of(k * part, part), part), :],
        )
        u_ref[:, pl.ds(pl.multiple_of(n * part, part), part)] = p
        return carry

    lax.fori_loop(0, 2 * subs, step, 0)
    u0 = u_ref[:, :own]
    u3 = u_ref[:, total - own :]
    u0_ref[...] = u0
    u3_ref[...] = u3
    edge_sends(res_ref, dg_ref, cp_ref, u0, u3, sl_ref, sr_ref)
    send_pair(core_ref, sl_ref, sr_ref, a_ref, b_ref)


def finish(sums_ref, x_ref, image_ref, r_ref, sol_in_ref, sol_ref, res_ref):
    rows, total = r_ref.shape
    alpha = step_of(sums_ref, rows)
    for lo in range(0, total, CH):
        hi = lo + CH
        res_ref[:, lo:hi] = r_ref[:, lo:hi] - alpha * image_ref[:, lo:hi]
        sol_ref[:, lo:hi] = sol_in_ref[:, lo:hi] + alpha * x_ref[:, lo:hi]


def call(kernel, name, outs, args, scratch=(), limit=8, flops=0, smem=1, specs=None):
    vmem = pl.BlockSpec(memory_space=pltpu.VMEM)
    size = sum(a.size * a.dtype.itemsize for a in args)
    return pl.pallas_call(
        kernel,
        out_shape=outs,
        in_specs=specs
        or [pl.BlockSpec(memory_space=pltpu.SMEM)] * smem + [vmem] * (len(args) - smem),
        out_specs=jax.tree.map(lambda _: vmem, outs),
        scratch_shapes=list(scratch),
        compiler_params=pltpu.CompilerParams(vmem_limit_bytes=limit << 20),
        cost_estimate=pl.CostEstimate(flops=flops, bytes_accessed=size, transcendentals=0),
        name=name,
    )(*args)


def body(right_side, diagonal, coupling, local_inverse, coarse_basis, coarse_inverse):
    rows, total = right_side.shape
    subs, own, order = local_inverse.shape
    modes = coarse_basis.shape[1]
    sectors = lax.axis_size("sector")
    chip = [(i, i ^ 1) for i in range(sectors)]
    side = [(i, (i + 1 if i % 2 else i - 1) % sectors) for i in range(sectors)]
    planes = [[2 * k + c for k in range(sectors // 2)] for c in range(2)]
    here = lax.axis_index("sector")
    core = jnp.stack(
        [
            here % 2,
            (here + sectors - 1) % sectors // 2,
            (here + 1) % sectors // 2,
            lax.axis_index("lift"),
        ]
    ).astype(jnp.int32)
    L, basis = local_inverse, coarse_basis
    r = right_side
    dg, cp = diagonal.reshape(1, total), coupling.reshape(1, total)
    wide = CH + TILE
    shape = jax.ShapeDtypeStruct
    full = shape((rows, total), F32)
    sub = shape((rows, own), F32)
    send = shape((rows, wide), BF16)
    long = shape((rows, wide + TILE), BF16)
    s_scratch = pltpu.VMEM((rows, total), BF16)
    pair = lambda like: [pltpu.VMEM(like.shape, like.dtype)] * 2
    work = 2 * rows * subs * own * order

    def exchange(a, b):
        got_b = lax.ppermute(b, "sector", side)
        got_a = lax.ppermute(a, "sector", chip)
        return got_a, got_b

    hbm = pl.BlockSpec(memory_space=pltpu.HBM)
    sa, sb = call(
        first_edges, "first_edges", [long, long], [core, r, cp, basis, coarse_inverse],
        [
            pltpu.VMEM((2, rows, CH), F32),
            pltpu.VMEM((2, 1, TILE), F32),
            pltpu.VMEM((2, modes, TILE), BF16),
            pltpu.VMEM((2, modes, coarse_inverse.shape[1]), F32),
        ]
        + pair(long)
        + [pltpu.SemaphoreType.DMA((8,))],
        specs=[pl.BlockSpec(memory_space=pltpu.SMEM)] + [hbm] * 4,
    )
    got_a0, got_b0 = exchange(sa, sb)
    v = call(middle_first, "middle_first", full, [r, L], [s_scratch], 8, work, 0)
    weights = []

    def sweeps(v, u0, u3, sa, sb, start):
        for sweep in range(start, SWEEPS):
            last = sweep == SWEEPS - 1
            if sweep == 0:
                vv, ga, gb = v, got_a0, got_b0
            else:
                ga, gb = exchange(sa, sb)
                vv = call(
                    middle, "middle", full, [r, v, u0, u3, dg, cp, L], [s_scratch], 8, work, 0
                )
            if sweep == 1 and not weights:
                ci, _ = lax.optimization_barrier((coarse_inverse, vv))
                lines = call(
                    lines_of, "lines", shape((ci.shape[0] + 8, ci.shape[1]), BF16),
                    [core, ci, got_a0, got_b0], pair(long),
                )
                other = lax.ppermute(lines, "lift", [(0, 1), (1, 0)])
                weights.append((lines, other))
            if sweep == 2 and len(weights) == 1:
                lines, other = weights[0]
                other, _ = lax.optimization_barrier((other, vv))
                weights.append(
                    call(
                        weave, "weave", shape((lines.shape[0], sectors * TILE), BF16),
                        [core, lines, other],
                        [pltpu.VMEM((lines.shape[0], 2 * lines.shape[1] + 2 * TILE), F32)],
                    )
                )
            first = sweep == 0
            outs = call(
                functools.partial(edges, first, not last), f"edges_{sweep}",
                [sub, sub] if last else [sub, sub, send, send],
                [core, vv, ga, gb, sa, sb, got_a0, got_b0, r, dg, cp, L],
                (pair(long) * 2 if first else pair(send) * 2) + pair(long) + pair(send),
                8, work // 8,
            )
            v, u0, u3 = vv, outs[0], outs[1]
            if not last:
                sa, sb = outs[2], outs[3]
        return v, u0, u3

    edge = shape((rows, CH), BF16)

    def coarse_step(v, u0, u3, sending):
        W = weights[1]
        chunk = call(
            project, "project", shape((sectors // 2, rows, TILE), BF16),
            [core, v, u0, u3, r, dg, cp, basis, got_a0, got_b0], pair(long),
        )
        chunk, W = lax.optimization_barrier((chunk, W))
        mine = lax.all_to_all(
            chunk, "sector", 0, 0, axis_index_groups=planes, tiled=True
        )
        other = lax.ppermute(mine, "sector", chip)
        return call(
            functools.partial(coarse, sending), "coarse",
            [full, full, shape((sectors, 2 * rows), F32)] + ([edge, edge] if sending else []),
            [core, mine, other, W, v, u0, u3, r, dg, cp, basis],
            pair(edge) if sending else (),
        )

    v, u0, u3 = sweeps(v, None, None, sa, sb, 0)
    x, image, sums, ia, ib = coarse_step(v, u0, u3, True)
    halo_a, halo_b = exchange(ia, ib)
    sums = lax.all_to_all(sums, "sector", 0, 0, tiled=True)
    sol, r, v, u0, u3, sa, sb = call(
        second, "second", [full, full, full, sub, sub, send, send],
        [core, sums, x, image, r, got_a0, got_b0, halo_a, halo_b, dg, cp, L],
        [pltpu.VMEM((rows, total + 2 * CH), BF16)] + pair(send) + pair(long) + pair(edge), 8, work,
    )
    v, u0, u3 = sweeps(v, u0, u3, sa, sb, 1)
    x, image, sums = coarse_step(v, u0, u3, False)
    sums = lax.all_to_all(sums, "sector", 0, 0, tiled=True)
    sol, res = call(finish, "finish", [full, full], [sums, x, image, r, sol], smem=0)
    return sol, res


def solution(mesh):
    in_specs = (
        P("lift", "sector"),
        P("sector"),
        P("sector"),
        P("sector", None, None),
        P("sector", None, None),
        P("sector", "lift"),
    )
    out_specs = (P("lift", "sector"), P("lift", "sector"))
    return jax.shard_map(body, mesh=mesh, in_specs=in_specs, out_specs=out_specs, check_vma=False)
```

```python
import functools

import jax
import jax.numpy as jnp
from jax import lax
from jax.experimental import pallas as pl
from jax.experimental.pallas import tpu as pltpu
from jax.sharding import PartitionSpec as P

SWEEPS = 4
F32, BF16 = jnp.float32, jnp.bfloat16
CH = 512
TILE = 128
EDGE_LIMIT = 57
FIRST_LIMIT = 20


def lane_of(shape):
    return lax.broadcasted_iota(jnp.int32, shape, 1)


def dot_t(a, b):
    return lax.dot_general(a, b, (((1,), (1,)), ((), ())), preferred_element_type=F32)


def split(x):
    hi = x.astype(BF16)
    return hi, (x - hi.astype(F32)).astype(BF16)


def spread(x):
    hi = x.astype(BF16).astype(F32)
    lo = (x - hi).astype(BF16).astype(F32)
    lane = lane_of((x.shape[0], TILE))
    return jnp.where(lane == 0, hi, jnp.where(lane == 1, lo, 0.0)).astype(BF16)


def column(tile, at):
    return tile[:, at : at + 1].astype(F32) + tile[:, at + 1 : at + 2].astype(F32)


GROUP = 16


def by_rows(rows, run):
    def step(g, carry):
        run(pl.ds(pl.multiple_of(g * GROUP, GROUP), GROUP))
        return carry

    lax.fori_loop(0, rows // GROUP, step, 0)


def operator(read, first, last, total, coefs, before, after, emit):
    dg_ref, cp_ref = coefs
    lane = lane_of((GROUP, TILE))
    cur = read(first)
    down = pltpu.roll(cur, TILE - 1, 1)
    prev = before if before is not None else pltpu.roll(read(first - 1), 1, 1)
    for t in range(first, last):
        up = pltpu.roll(cur, 1, 1)
        if t + 1 < last or after is None:
            ahead = read(t + 1)
            ahead_down = pltpu.roll(ahead, TILE - 1, 1)
        else:
            ahead, ahead_down = None, after
        left = jnp.where(lane == 0, prev, up)
        right = jnp.where(lane == TILE - 1, ahead_down, down)
        cols = slice(total + t * TILE, total + (t + 1) * TILE)
        emit(t, cur, dg_ref[:, cols] * cur - cp_ref[:, cols] * (left + right))
        cur, down, prev = ahead, ahead_down, up


def parts(v_ref, u0_ref, u3_ref, own):
    tiles, outer = v_ref.shape[1] // TILE, own // TILE

    def get(rows, t):
        if t < outer:
            return u0_ref[rows, t * TILE : (t + 1) * TILE]
        if t >= tiles - outer:
            t = t - (tiles - outer)
            return u3_ref[rows, t * TILE : (t + 1) * TILE]
        return v_ref[rows, t * TILE : (t + 1) * TILE]

    return get


def sweep_residual(r_ref, get, coefs, s_ref):
    rows, total = r_ref.shape

    def run(group):
        def emit(t, cur, image):
            cols = slice(t * TILE, (t + 1) * TILE)
            s_ref[group, cols] = (r_ref[group, cols] - image).astype(BF16)

        operator(lambda t: get(group, t), 0, total // TILE, 0, coefs, 0.0, 0.0, emit)

    by_rows(rows, run)


def pick(core_ref, a_ref, b_ref, left_ref, right_ref):
    @pl.when(core_ref[0] == 0)
    def _():
        left_ref[...] = b_ref[...]
        right_ref[...] = a_ref[...]

    @pl.when(core_ref[0] != 0)
    def _():
        left_ref[...] = a_ref[...]
        right_ref[...] = b_ref[...]


def first_edges(core_ref, r_hbm, cp_hbm, basis_hbm, ci_hbm, a_ref, b_ref,
                r_ref, cp_ref, basis_ref, ci_ref, left_ref, right_ref, sem):
    rows, total = r_hbm.shape
    subs, modes, own = basis_hbm.shape
    copies = []
    for k, (at, sub, tile_lo, cp_lo) in enumerate(
        ((0, 0, 0, 0), (total - CH, subs - 1, own - TILE, total - TILE))
    ):
        for n, (src, dst) in enumerate(
            (
                (r_hbm.at[:, pl.ds(at, CH)], r_ref.at[k]),
                (cp_hbm.at[:, pl.ds(cp_lo, TILE)], cp_ref.at[k]),
                (basis_hbm.at[sub, :, pl.ds(tile_lo, TILE)], basis_ref.at[k]),
                (ci_hbm.at[pl.ds(sub * modes, modes), :], ci_ref.at[k]),
            )
        ):
            copies.append(pltpu.make_async_copy(src, dst, sem.at[4 * k + n]))
    for c in copies:
        c.start()
    for c in copies:
        c.wait()
    lane = lane_of((modes, TILE))
    for k, (out, col, roll) in enumerate(((left_ref, 0, 2), (right_ref, TILE - 1, 3))):
        out[:, :CH] = r_ref[k].astype(BF16)
        one = cp_ref[k][:, col : col + 1]
        meta = spread(jnp.broadcast_to(one, (rows, 1))).astype(F32)
        weight = basis_ref[k].astype(F32)
        edge = pltpu.roll(weight, roll, 1) * one
        hi = edge.astype(BF16).astype(F32)
        lo = pltpu.roll(edge - hi, 1, 1)
        both = jnp.where(lane == 2, hi, jnp.where(lane == 3, lo, 0.0))
        out[:, CH : CH + TILE] = meta.astype(BF16)
        out[:modes, CH : CH + TILE] = (meta[:modes] + both).astype(BF16)
        line = jnp.sum(weight[:, col : col + 1] * ci_ref[k], axis=0, keepdims=True)
        count = line.shape[1] // TILE
        out[:, CH + TILE :] = jnp.zeros((rows, TILE), BF16)
        out[:count, CH + TILE :] = jnp.concatenate(
            [line[:, n * TILE : (n + 1) * TILE] for n in range(count)], axis=0
        ).astype(BF16)
    def send(even):
        a_ref[...] = (right_ref if even else left_ref)[...]
        b_ref[...] = (left_ref if even else right_ref)[...]

    by_side(core_ref, send)


def by_side(core_ref, run):
    pl.when(core_ref[0] == 0)(lambda: run(True))
    pl.when(core_ref[0] != 0)(lambda: run(False))


def lines_of(core_ref, ci_ref, a_ref, b_ref, out_ref, left_ref, right_ref):
    pick(core_ref, a_ref, b_ref, left_ref, right_ref)
    rows, width = ci_ref.shape
    out_ref[:rows, :] = ci_ref[...].astype(BF16)
    extra = []
    for ref in (left_ref, right_ref):
        block = ref[:, CH + TILE :].astype(F32)
        extra.append(
            jnp.concatenate([block[k : k + 1, :] for k in range(width // TILE)], axis=1)
        )
    extra.append(jnp.zeros((6, width), F32))
    out_ref[rows:, :] = jnp.concatenate(extra, axis=0).astype(BF16)


def weave(core_ref, mine_ref, other_ref, out_ref, all_ref):
    rows, half = mine_ref.shape
    low = core_ref[3] == 0

    @pl.when(low)
    def _():
        all_ref[:, TILE : TILE + half] = mine_ref[...].astype(F32)
        all_ref[:, TILE + half : TILE + 2 * half] = other_ref[...].astype(F32)

    @pl.when(jnp.logical_not(low))
    def _():
        all_ref[:, TILE : TILE + half] = other_ref[...].astype(F32)
        all_ref[:, TILE + half : TILE + 2 * half] = mine_ref[...].astype(F32)

    all_ref[:, :TILE] = all_ref[:, 2 * half : 2 * half + TILE]
    all_ref[:, 2 * half + TILE :] = all_ref[:, TILE : 2 * TILE]
    lane = lane_of((rows, TILE))
    core = core_ref[0]
    zero = jnp.zeros((rows, TILE), F32)

    def step(k, carry):
        at = pl.multiple_of(k * TILE, TILE)
        prev = all_ref[:, pl.ds(at, TILE)]
        tile = all_ref[:, pl.ds(pl.multiple_of(at + TILE, TILE), TILE)]
        after = all_ref[:, pl.ds(pl.multiple_of(at + 2 * TILE, TILE), TILE)]
        near = pltpu.roll(tile, 16, 1)
        even = jnp.where(lane < 64, tile, jnp.where(lane < 80, pltpu.roll(prev, 80, 1), near))
        odd = jnp.where(lane < 64, pltpu.roll(tile, 64, 1), jnp.where(lane < 80, near, pltpu.roll(after, 80, 1)))
        at = 2 * k * TILE
        out_ref[:, pl.ds(pl.multiple_of(at + core * TILE, TILE), TILE)] = jnp.where(
            lane < 96, even, zero
        ).astype(BF16)
        out_ref[:, pl.ds(pl.multiple_of(at + (1 - core) * TILE, TILE), TILE)] = jnp.where(
            lane < 96, odd, zero
        ).astype(BF16)
        return carry

    lax.fori_loop(0, 2 * half // TILE, step, 0, unroll=min(4, 2 * half // TILE))


def products(s_ref, L_ref, own, order, store, ready=None):
    total = s_ref.shape[1]
    margin = (order - own) // 2
    subs = L_ref.shape[0]
    part = own // 2

    def rows_at(k):
        return pl.ds(pl.multiple_of(k * part, part), part)

    def first(k, carry):
        p = dot_t(s_ref[:, TILE : order - margin], L_ref[0, rows_at(k), margin + TILE :])
        store(pl.multiple_of(k * part, part), part, p)
        return carry

    def last(k, carry):
        start = (subs - 1) * own - margin
        p = dot_t(
            s_ref[:, start : total - TILE], L_ref[subs - 1, rows_at(k), : total - TILE - start]
        )
        store(pl.multiple_of((subs - 1) * own + k * part, part), part, p)
        return carry

    def inner(n, carry):
        j, k = 1 + n // 2, n % 2
        if ready is not None:
            pl.when(k == 0)(lambda: ready(j))
        start = pl.multiple_of(j * own - margin, TILE)
        p = dot_t(s_ref[:, pl.ds(start, order)], L_ref[j, rows_at(k), :])
        store(pl.multiple_of(j * own + k * part, part), part, p)
        return carry

    if ready is not None:
        ready(0)
    lax.fori_loop(0, 2, first, 0)
    lax.fori_loop(0, 2 * (subs - 2), inner, 0)
    if ready is not None:
        ready(subs - 1)
    lax.fori_loop(0, 2, last, 0)


def middle_first(r_ref, L_hbm, v_ref, L_ref, s_ref, sem):
    subs, own, order = L_ref.shape

    def copy(j):
        return pltpu.make_async_copy(L_hbm.at[j], L_ref.at[j], sem.at[j])

    for j in range(subs):
        copy(j).start()
    s_ref[...] = r_ref[...].astype(BF16)

    def store(at, size, p):
        v_ref[:, pl.ds(at, size)] = p

    products(s_ref, L_ref, own, order, store, lambda j: copy(j).wait())


def middle(r_ref, v_ref, u0_ref, u3_ref, dg_ref, cp_ref, L_ref, out_ref, s_ref):
    subs, own, order = L_ref.shape
    total = r_ref.shape[1]
    margin = (order - own) // 2
    sweep_residual(r_ref, parts(v_ref, u0_ref, u3_ref, own), (dg_ref, cp_ref), s_ref)

    def inner(j, carry):
        at = pl.multiple_of(j * own, own)
        p = dot_t(s_ref[:, pl.ds(pl.multiple_of(at - margin, TILE), order)], L_ref[j])
        out_ref[:, pl.ds(at, own)] = v_ref[:, pl.ds(at, own)] + p
        return carry

    lax.fori_loop(1, subs - 1, inner, 0)
    for j, u_ref in ((0, u0_ref), (subs - 1, u3_ref)):
        at = j * own
        lo = at - margin
        a, b = max(lo, TILE), min(lo + order, total - TILE)
        out_ref[:, at : at + own] = u_ref[...] + dot_t(
            s_ref[:, a:b], L_ref[j, :, a - lo : b - lo]
        )


def edge_sends(r_ref, dg_ref, cp_ref, u0_ref, u3_ref, left_ref, right_ref):
    rows, total = r_ref.shape
    own = u0_ref.shape[1]
    count, tiles = CH // TILE, own // TILE
    shift = total - own

    def run(group):
        def left(t, cur, image):
            cols = slice(t * TILE, (t + 1) * TILE)
            left_ref[group, cols] = (r_ref[group, cols] - image).astype(BF16)

        def right(t, cur, image):
            cols = slice(shift + t * TILE, shift + (t + 1) * TILE)
            k = (t - (tiles - count)) * TILE
            right_ref[group, k : k + TILE] = (r_ref[group, cols] - image).astype(BF16)

        read = lambda ref: lambda t: ref[group, t * TILE : (t + 1) * TILE]
        operator(read(u0_ref), 0, count, 0, (dg_ref, cp_ref), 0.0, None, left)
        operator(
            read(u3_ref), tiles - count, tiles, shift, (dg_ref, cp_ref), None, 0.0, right
        )

    by_rows(rows, run)
    left_ref[:, CH : CH + TILE] = spread(u0_ref[:, :1])
    right_ref[:, CH : CH + TILE] = spread(u3_ref[:, own - 1 :])


def edges(first, *refs):
    (core_ref, v_ref, gota_ref, gotb_ref, owna_ref, ownb_ref, metaa_ref, metab_ref) = refs[:8]
    (r_ref, dg_ref, cp_ref, L_ref, u0_ref, u3_ref, senda_ref, sendb_ref) = refs[8:]
    total = v_ref.shape[1]
    subs, own, order = L_ref.shape
    wide = CH + TILE

    def run(even):
        order_of = (lambda a, b: (b, a)) if even else (lambda a, b: (a, b))
        gotl_ref, gotr_ref = order_of(gota_ref, gotb_ref)
        ownl_ref, ownr_ref = order_of(owna_ref, ownb_ref)
        metal_ref, metar_ref = order_of(metaa_ref, metab_ref)
        tile_l, tile_r = ownl_ref[:, :TILE], ownr_ref[:, CH - TILE : CH]
        halo_l, halo_r = gotl_ref[:, :CH], gotr_ref[:, :CH]
        if not first:
            lane_t = lane_of(tile_l.shape)
            mine_l = column(ownl_ref[:, CH : CH + TILE], 0)
            mine_r = column(ownr_ref[:, CH : CH + TILE], 0)
            rim_l = column(gotl_ref[:, CH : CH + TILE], 0)
            rim_r = column(gotr_ref[:, CH : CH + TILE], 0)
            coup_l = column(metal_ref[:, CH : CH + TILE], 0)
            coup_r = column(metar_ref[:, CH : CH + TILE], 0)
            add = lambda x, at, y: (
                x.astype(F32) + jnp.where(lane_t == at, y, 0.0)
            ).astype(BF16)
            tile_l = add(tile_l, 0, cp_ref[:, :1] * rim_l)
            tile_r = add(tile_r, TILE - 1, cp_ref[:, total - 1 :] * rim_r)
            halo_l = jnp.concatenate(
                [halo_l[:, : CH - TILE], add(halo_l[:, CH - TILE :], TILE - 1, coup_l * mine_l)],
                axis=1,
            )
            halo_r = jnp.concatenate(
                [add(halo_r[:, :TILE], 0, coup_r * mine_r), halo_r[:, TILE:]], axis=1
            )
        u0_ref[...] = v_ref[:, :own] + dot_t(
            jnp.concatenate([halo_l, tile_l], axis=1), L_ref[0, :, :wide]
        )
        u3_ref[...] = v_ref[:, total - own :] + dot_t(
            jnp.concatenate([tile_r, halo_r], axis=1), L_ref[subs - 1, :, order - wide :]
        )
        edge_sends(r_ref, dg_ref, cp_ref, u0_ref, u3_ref, *order_of(senda_ref, sendb_ref))

    by_side(core_ref, run)


def project(core_ref, v_ref, u0_ref, u3_ref, r_ref, dg_ref, cp_ref, basis_ref, metaa_ref, metab_ref,
            unused_a, unused_b, out_ref, s_ref, metal_ref, metar_ref):
    rows, total = r_ref.shape
    own = basis_ref.shape[2]
    modes = basis_ref.shape[1]
    get = parts(v_ref, u0_ref, u3_ref, own)
    lane = lane_of((rows, TILE))

    def meta_of(even):
        metal_ref[...] = (metab_ref if even else metaa_ref)[:modes, CH : CH + TILE]
        metar_ref[...] = (metaa_ref if even else metab_ref)[:modes, CH : CH + TILE]

    by_side(core_ref, meta_of)
    sweep_residual(r_ref, get, (dg_ref, cp_ref), s_ref)
    pieces = [
        dot_t(s_ref[:, j * own : (j + 1) * own], basis_ref[j]) for j in range(total // own)
    ]
    first, last = u0_ref[:, :1], u3_ref[:, own - 1 :]
    chosen = (lane == 2) | (lane == 3)
    for value, meta in ((first, metal_ref), (last, metar_ref)):
        hi, lo = split(value)
        coef = meta[...]
        pieces.append(
            dot_t(jnp.where(chosen, hi.astype(F32), 0.0).astype(BF16), coef)
            + dot_t(jnp.where(chosen, lo.astype(F32), 0.0).astype(BF16), coef)
        )
    rims = jnp.zeros((rows, 32), F32)
    lane32 = lane_of((rows, 32))
    for k, value in enumerate((first, last)):
        hi, lo = split(value)
        rims = jnp.where(lane32 == 2 * k, hi.astype(F32), rims)
        rims = jnp.where(lane32 == 2 * k + 1, lo.astype(F32), rims)
    chunk = jnp.concatenate(pieces + [rims], axis=1).astype(BF16)
    for d in range(out_ref.shape[0]):
        out_ref[d] = chunk


def coarse(core_ref, mine_ref, other_ref, W_ref, v_ref, u0_ref, u3_ref, r_ref, dg_ref, cp_ref,
           basis_ref, x_ref, image_ref, sums_ref, a_ref, b_ref, both_ref, rims_ref):
    rows, total = r_ref.shape
    own = basis_ref.shape[2]
    modes = basis_ref.shape[1]
    count = mine_ref.shape[0]
    group = min(8, count)
    c = None
    for k in range(0, count, group):
        tiles = []
        for d in range(k, k + group):
            tiles += [mine_ref[d], other_ref[d]]
        p = dot_t(
            jnp.concatenate(tiles, axis=1), W_ref[:, 2 * k * TILE : 2 * (k + group) * TILE]
        )
        c = p if c is None else c + p
    subs = total // own
    for j in range(subs):
        hi, lo = split(c[:, j * modes : (j + 1) * modes])
        both = jnp.concatenate([hi, lo], axis=1)
        at = j * own
        b = basis_ref[j]
        u = u0_ref[...] if j == 0 else u3_ref[...] if j == subs - 1 else v_ref[:, at : at + own]
        x_ref[:, at : at + own] = u + jnp.dot(
            both, jnp.concatenate([b, b], axis=0), preferred_element_type=F32
        )
    n = subs * modes
    before = other_ref[core_ref[1]]
    after = other_ref[core_ref[2]]
    rim_l = column(before, 98) + c[:, n : n + 1]
    rim_r = column(after, 96) + c[:, n + 1 : n + 2]
    rims_ref[0] = jnp.broadcast_to(rim_l, (rows, TILE))
    rims_ref[1] = jnp.broadcast_to(rim_r, (rows, TILE))

    def run(group):
        acc = [jnp.zeros((GROUP, TILE), F32)] * 2

        def emit(t, cur, image):
            cols = slice(t * TILE, (t + 1) * TILE)
            image_ref[group, cols] = image
            acc[0] = acc[0] + r_ref[group, cols] * image
            acc[1] = acc[1] + image * image

        operator(
            lambda t: x_ref[group, t * TILE : (t + 1) * TILE], 0, total // TILE, 0,
            (dg_ref, cp_ref), rims_ref[0, group, :], rims_ref[1, group, :], emit,
        )
        for k in range(2):
            both_ref[k, group, :] = jnp.broadcast_to(
                jnp.sum(acc[k], axis=1, keepdims=True), (GROUP, TILE)
            )

    by_rows(rows, run)
    flat = jnp.transpose(jnp.concatenate([both_ref[0], both_ref[1]], axis=0))
    sums_ref[...] = flat[: sums_ref.shape[0]]

    def send(even):
        (b_ref if even else a_ref)[...] = image_ref[:, :CH].astype(BF16)
        (a_ref if even else b_ref)[...] = image_ref[:, total - CH :].astype(BF16)

    by_side(core_ref, send)


def step_of(sums_ref, rows):
    s = jnp.sum(sums_ref[...], axis=0, keepdims=True)
    t = jnp.transpose(jnp.broadcast_to(s, (2 * rows, 2 * rows)))
    return t[:rows, :1] / (t[rows:, :1] + 1e-6)


def second(core_ref, sums_ref, x_ref, image_ref, r_ref, ha0_ref, hb0_ref, ha_ref, hb_ref,
           dg_ref, cp_ref, L_ref, sol_ref, res_ref, u_ref, u0_ref, u3_ref, a_ref, b_ref,
           s_ref, sl_ref, sr_ref):
    rows, total = r_ref.shape
    own, order = L_ref.shape[1], L_ref.shape[2]
    alpha = step_of(sums_ref, rows)

    def halo(even):
        for at, one in ((0, even), (CH + total, not even)):
            old, new = (hb0_ref, hb_ref) if one else (ha0_ref, ha_ref)
            s_ref[:, at : at + CH] = (
                old[:, :CH].astype(F32) - alpha * new[...].astype(F32)
            ).astype(BF16)

    by_side(core_ref, halo)

    def update(k, carry):
        cols = pl.ds(pl.multiple_of(k * CH, CH), CH)
        r = r_ref[:, cols] - alpha * image_ref[:, cols]
        res_ref[:, cols] = r
        sol_ref[:, cols] = alpha * x_ref[:, cols]
        s_ref[:, pl.ds(pl.multiple_of((k + 1) * CH, CH), CH)] = r.astype(BF16)
        return carry

    lax.fori_loop(0, total // CH, update, 0)
    subs = L_ref.shape[0]

    def step(j, carry):
        at = pl.multiple_of(j * own, own)
        u_ref[:, pl.ds(at, own)] = dot_t(s_ref[:, pl.ds(at, order)], L_ref[j])
        return carry

    lax.fori_loop(0, subs, step, 0)
    u0_ref[...] = u_ref[:, :own]
    u3_ref[...] = u_ref[:, total - own :]
    edge_sends(res_ref, dg_ref, cp_ref, u0_ref, u3_ref, sl_ref, sr_ref)

    def send(even):
        a_ref[...] = (sr_ref if even else sl_ref)[...]
        b_ref[...] = (sl_ref if even else sr_ref)[...]

    by_side(core_ref, send)


def finish(sums_ref, x_ref, image_ref, r_ref, sol_in_ref, unused_a, unused_b, sol_ref, res_ref):
    rows, total = r_ref.shape
    alpha = step_of(sums_ref, rows)
    for lo in range(0, total, CH):
        hi = lo + CH
        res_ref[:, lo:hi] = r_ref[:, lo:hi] - alpha * image_ref[:, lo:hi]
        sol_ref[:, lo:hi] = sol_in_ref[:, lo:hi] + alpha * x_ref[:, lo:hi]


def call(kernel, name, outs, args, scratch=(), limit=8, flops=0, smem=1, specs=None):
    vmem = pl.BlockSpec(memory_space=pltpu.VMEM)
    size = sum(a.size * a.dtype.itemsize for a in args)
    return pl.pallas_call(
        kernel,
        out_shape=outs,
        in_specs=specs
        or [pl.BlockSpec(memory_space=pltpu.SMEM)] * smem + [vmem] * (len(args) - smem),
        out_specs=jax.tree.map(lambda _: vmem, outs),
        scratch_shapes=list(scratch),
        compiler_params=pltpu.CompilerParams(vmem_limit_bytes=limit << 20),
        cost_estimate=pl.CostEstimate(flops=flops, bytes_accessed=size, transcendentals=0),
        name=name,
    )(*args)


def body(right_side, diagonal, coupling, local_inverse, coarse_basis, coarse_inverse):
    rows, total = right_side.shape
    subs, own, order = local_inverse.shape
    modes = coarse_basis.shape[1]
    sectors = lax.axis_size("sector")
    chip = [(i, i ^ 1) for i in range(sectors)]
    side = [(i, (i + 1 if i % 2 else i - 1) % sectors) for i in range(sectors)]
    planes = [[2 * k + c for k in range(sectors // 2)] for c in range(2)]
    here = lax.axis_index("sector")
    core = jnp.stack(
        [
            here % 2,
            (here + sectors - 1) % sectors // 2,
            (here + 1) % sectors // 2,
            lax.axis_index("lift"),
        ]
    ).astype(jnp.int32)
    L, basis = local_inverse, coarse_basis
    r = right_side
    dg, cp = diagonal.reshape(1, total), coupling.reshape(1, total)
    wide = CH + TILE
    shape = jax.ShapeDtypeStruct
    full = shape((rows, total), F32)
    sub = shape((rows, own), F32)
    send = shape((rows, wide), BF16)
    long = shape((rows, wide + TILE), BF16)
    s_scratch = pltpu.VMEM((rows, total), BF16)
    pair = lambda like: [pltpu.VMEM(like.shape, like.dtype)] * 2
    work = 2 * rows * subs * own * order

    def exchange(a, b):
        got_b = lax.ppermute(b, "sector", side)
        got_a = lax.ppermute(a, "sector", chip)
        return got_a, got_b

    hbm = pl.BlockSpec(memory_space=pltpu.HBM)
    sa, sb = call(
        first_edges, "first_edges", [long, long], [core, r, cp, basis, coarse_inverse],
        [
            pltpu.VMEM((2, rows, CH), F32),
            pltpu.VMEM((2, 1, TILE), F32),
            pltpu.VMEM((2, modes, TILE), BF16),
            pltpu.VMEM((2, modes, coarse_inverse.shape[1]), F32),
        ]
        + pair(long)
        + [pltpu.SemaphoreType.DMA((8,))],
        EDGE_LIMIT,
        specs=[pl.BlockSpec(memory_space=pltpu.SMEM)] + [hbm] * 4,
    )
    got_a0, got_b0 = exchange(sa, sb)
    v, L = call(
        middle_first, "middle_first", [full, shape(L.shape, L.dtype)], [r, L],
        [s_scratch, pltpu.SemaphoreType.DMA((subs,))],
        FIRST_LIMIT, work, specs=[pl.BlockSpec(memory_space=pltpu.VMEM), hbm],
    )
    weights = []

    def sweeps(v, u0, u3, sa, sb, start):
        for sweep in range(start, SWEEPS):
            last = sweep == SWEEPS - 1
            if sweep == 0:
                vv, ga, gb = v, got_a0, got_b0
            else:
                ga, gb = exchange(sa, sb)
                vv = call(
                    middle, "middle", full, [r, v, u0, u3, dg, cp, L], [s_scratch], 8, work, 0
                )
            if sweep == 1 and not weights:
                ci, _ = lax.optimization_barrier((coarse_inverse, vv))
                lines = call(
                    lines_of, "lines", shape((ci.shape[0] + 8, ci.shape[1]), BF16),
                    [core, ci, got_a0, got_b0], pair(long),
                )
                other = lax.ppermute(lines, "lift", [(0, 1), (1, 0)])
                weights.append((lines, other))
            if sweep == 2 and len(weights) == 1:
                lines, other = weights[0]
                other, _ = lax.optimization_barrier((other, vv))
                weights.append(
                    call(
                        weave, "weave", shape((lines.shape[0], sectors * TILE), BF16),
                        [core, lines, other],
                        [pltpu.VMEM((lines.shape[0], 2 * lines.shape[1] + 2 * TILE), F32)],
                    )
                )
            first = sweep == 0
            if last and start == 0:
                vv, weights[1] = lax.optimization_barrier((vv, weights[1]))
            u0, u3, sa, sb = call(
                functools.partial(edges, first), "edges_first" if first else "edges",
                [sub, sub, send, send],
                [core, vv, ga, gb, sa, sb, got_a0, got_b0, r, dg, cp, L],
                flops=work // 8,
            )
            v = vv
        return v, u0, u3, sa, sb

    edge = shape((rows, CH), BF16)

    def coarse_step(v, u0, u3, sa, sb):
        W = weights[1]
        chunk = call(
            project, "project", shape((sectors // 2, rows, TILE), BF16),
            [core, v, u0, u3, r, dg, cp, basis, got_a0, got_b0, sa, sb],
            [s_scratch] + [pltpu.VMEM((modes, TILE), BF16)] * 2,
        )
        chunk, W = lax.optimization_barrier((chunk, W))
        mine = lax.all_to_all(
            chunk, "sector", 0, 0, axis_index_groups=planes, tiled=True
        )
        other = lax.ppermute(mine, "sector", chip)
        return call(
            coarse, "coarse", [full, full, shape((sectors, 2 * rows), F32), edge, edge],
            [core, mine, other, W, v, u0, u3, r, dg, cp, basis],
            [pltpu.VMEM((2, rows, TILE), F32)] * 2,
        )

    v, u0, u3, sa, sb = sweeps(v, None, None, sa, sb, 0)
    x, image, sums, ia, ib = coarse_step(v, u0, u3, sa, sb)
    halo_a, halo_b = exchange(ia, ib)
    sums = lax.all_to_all(sums, "sector", 0, 0, tiled=True)
    sol, r, v, u0, u3, sa, sb = call(
        second, "second", [full, full, full, sub, sub, send, send],
        [core, sums, x, image, r, got_a0, got_b0, halo_a, halo_b, dg, cp, L],
        [pltpu.VMEM((rows, total + 2 * CH), BF16)] + pair(send), 8, work,
    )
    v, u0, u3, sa, sb = sweeps(v, u0, u3, sa, sb, 1)
    x, image, sums, ia, ib = coarse_step(v, u0, u3, sa, sb)
    sums = lax.all_to_all(sums, "sector", 0, 0, tiled=True)
    sol, res = call(finish, "finish", [full, full], [sums, x, image, r, sol, ia, ib], smem=0)
    return sol, res


def solution(mesh):
    in_specs = (
        P("lift", "sector"),
        P("sector"),
        P("sector"),
        P("sector", None, None),
        P("sector", None, None),
        P("sector", "lift"),
    )
    out_specs = (P("lift", "sector"), P("lift", "sector"))
    return jax.shard_map(body, mesh=mesh, in_specs=in_specs, out_specs=out_specs, check_vma=False)
```

```python
import functools

import jax
import jax.numpy as jnp
from jax import lax
from jax.experimental import pallas as pl
from jax.experimental.pallas import tpu as pltpu
from jax.sharding import PartitionSpec as P

SWEEPS = 4
F32, BF16 = jnp.float32, jnp.bfloat16
CH = 512
TILE = 128
EDGE_LIMIT = 57
FIRST_LIMIT = 20


def lane_of(shape):
    return lax.broadcasted_iota(jnp.int32, shape, 1)


def dot_t(a, b):
    return lax.dot_general(a, b, (((1,), (1,)), ((), ())), preferred_element_type=F32)


def split(x):
    hi = x.astype(BF16)
    return hi, (x - hi.astype(F32)).astype(BF16)


def spread(x):
    hi = x.astype(BF16).astype(F32)
    lo = (x - hi).astype(BF16).astype(F32)
    lane = lane_of((x.shape[0], TILE))
    return jnp.where(lane == 0, hi, jnp.where(lane == 1, lo, 0.0)).astype(BF16)


def column(tile, at):
    return tile[:, at : at + 1].astype(F32) + tile[:, at + 1 : at + 2].astype(F32)


GROUP = 16


def by_rows(rows, run):
    for at in range(0, rows, GROUP):
        run(slice(at, at + GROUP))


def operator(read, first, last, total, coefs, before, after, emit):
    dg_ref, cp_ref = coefs
    lane = lane_of((GROUP, TILE))
    cur = read(first)
    down = pltpu.roll(cur, TILE - 1, 1)
    prev = before if before is not None else pltpu.roll(read(first - 1), 1, 1)
    for t in range(first, last):
        up = pltpu.roll(cur, 1, 1)
        if t + 1 < last or after is None:
            ahead = read(t + 1)
            ahead_down = pltpu.roll(ahead, TILE - 1, 1)
        else:
            ahead, ahead_down = None, after
        left = jnp.where(lane == 0, prev, up)
        right = jnp.where(lane == TILE - 1, ahead_down, down)
        cols = slice(total + t * TILE, total + (t + 1) * TILE)
        emit(t, cur, dg_ref[:, cols] * cur - cp_ref[:, cols] * (left + right))
        cur, down, prev = ahead, ahead_down, up


def parts(v_ref, u0_ref, u3_ref, own):
    tiles, outer = v_ref.shape[1] // TILE, own // TILE

    def get(rows, t):
        if t < outer:
            return u0_ref[rows, t * TILE : (t + 1) * TILE]
        if t >= tiles - outer:
            t = t - (tiles - outer)
            return u3_ref[rows, t * TILE : (t + 1) * TILE]
        return v_ref[rows, t * TILE : (t + 1) * TILE]

    return get


def sweep_residual(r_ref, get, coefs, s_ref):
    rows, total = r_ref.shape

    def run(group):
        def emit(t, cur, image):
            cols = slice(t * TILE, (t + 1) * TILE)
            s_ref[group, cols] = (r_ref[group, cols] - image).astype(BF16)

        operator(lambda t: get(group, t), 0, total // TILE, 0, coefs, 0.0, 0.0, emit)

    by_rows(rows, run)


def pick(core_ref, a_ref, b_ref, left_ref, right_ref):
    @pl.when(core_ref[0] == 0)
    def _():
        left_ref[...] = b_ref[...]
        right_ref[...] = a_ref[...]

    @pl.when(core_ref[0] != 0)
    def _():
        left_ref[...] = a_ref[...]
        right_ref[...] = b_ref[...]


def first_edges(core_ref, r_hbm, cp_hbm, basis_hbm, ci_hbm, a_ref, b_ref,
                r_ref, cp_ref, basis_ref, ci_ref, left_ref, right_ref, sem):
    rows, total = r_hbm.shape
    subs, modes, own = basis_hbm.shape
    copies = []
    for k, (at, sub, tile_lo, cp_lo) in enumerate(
        ((0, 0, 0, 0), (total - CH, subs - 1, own - TILE, total - TILE))
    ):
        for n, (src, dst) in enumerate(
            (
                (r_hbm.at[:, pl.ds(at, CH)], r_ref.at[k]),
                (cp_hbm.at[:, pl.ds(cp_lo, TILE)], cp_ref.at[k]),
                (basis_hbm.at[sub, :, pl.ds(tile_lo, TILE)], basis_ref.at[k]),
                (ci_hbm.at[pl.ds(sub * modes, modes), :], ci_ref.at[k]),
            )
        ):
            copies.append(pltpu.make_async_copy(src, dst, sem.at[4 * k + n]))
    for c in copies:
        c.start()
    for c in copies:
        c.wait()
    lane = lane_of((modes, TILE))
    for k, (out, col, roll) in enumerate(((left_ref, 0, 2), (right_ref, TILE - 1, 3))):
        out[:, :CH] = r_ref[k].astype(BF16)
        one = cp_ref[k][:, col : col + 1]
        meta = spread(jnp.broadcast_to(one, (rows, 1))).astype(F32)
        weight = basis_ref[k].astype(F32)
        edge = pltpu.roll(weight, roll, 1) * one
        hi = edge.astype(BF16).astype(F32)
        lo = pltpu.roll(edge - hi, 1, 1)
        both = jnp.where(lane == 2, hi, jnp.where(lane == 3, lo, 0.0))
        out[:, CH : CH + TILE] = meta.astype(BF16)
        out[:modes, CH : CH + TILE] = (meta[:modes] + both).astype(BF16)
        line = jnp.sum(weight[:, col : col + 1] * ci_ref[k], axis=0, keepdims=True)
        count = line.shape[1] // TILE
        out[:, CH + TILE :] = jnp.zeros((rows, TILE), BF16)
        out[:count, CH + TILE :] = jnp.concatenate(
            [line[:, n * TILE : (n + 1) * TILE] for n in range(count)], axis=0
        ).astype(BF16)
    def send(even):
        a_ref[...] = (right_ref if even else left_ref)[...]
        b_ref[...] = (left_ref if even else right_ref)[...]

    by_side(core_ref, send)


def by_side(core_ref, run):
    pl.when(core_ref[0] == 0)(lambda: run(True))
    pl.when(core_ref[0] != 0)(lambda: run(False))


def lines_of(core_ref, ci_ref, a_ref, b_ref, out_ref, left_ref, right_ref):
    pick(core_ref, a_ref, b_ref, left_ref, right_ref)
    rows, width = ci_ref.shape
    out_ref[:rows, :] = ci_ref[...].astype(BF16)
    extra = []
    for ref in (left_ref, right_ref):
        block = ref[:, CH + TILE :].astype(F32)
        extra.append(
            jnp.concatenate([block[k : k + 1, :] for k in range(width // TILE)], axis=1)
        )
    extra.append(jnp.zeros((6, width), F32))
    out_ref[rows:, :] = jnp.concatenate(extra, axis=0).astype(BF16)


def weave(core_ref, mine_ref, other_ref, out_ref, all_ref):
    rows, half = mine_ref.shape
    low = core_ref[3] == 0

    @pl.when(low)
    def _():
        all_ref[:, TILE : TILE + half] = mine_ref[...].astype(F32)
        all_ref[:, TILE + half : TILE + 2 * half] = other_ref[...].astype(F32)

    @pl.when(jnp.logical_not(low))
    def _():
        all_ref[:, TILE : TILE + half] = other_ref[...].astype(F32)
        all_ref[:, TILE + half : TILE + 2 * half] = mine_ref[...].astype(F32)

    all_ref[:, :TILE] = all_ref[:, 2 * half : 2 * half + TILE]
    all_ref[:, 2 * half + TILE :] = all_ref[:, TILE : 2 * TILE]
    lane = lane_of((rows, TILE))
    core = core_ref[0]
    zero = jnp.zeros((rows, TILE), F32)

    def step(k, carry):
        at = pl.multiple_of(k * TILE, TILE)
        prev = all_ref[:, pl.ds(at, TILE)]
        tile = all_ref[:, pl.ds(pl.multiple_of(at + TILE, TILE), TILE)]
        after = all_ref[:, pl.ds(pl.multiple_of(at + 2 * TILE, TILE), TILE)]
        near = pltpu.roll(tile, 16, 1)
        even = jnp.where(lane < 64, tile, jnp.where(lane < 80, pltpu.roll(prev, 80, 1), near))
        odd = jnp.where(lane < 64, pltpu.roll(tile, 64, 1), jnp.where(lane < 80, near, pltpu.roll(after, 80, 1)))
        at = 2 * k * TILE
        out_ref[:, pl.ds(pl.multiple_of(at + core * TILE, TILE), TILE)] = jnp.where(
            lane < 96, even, zero
        ).astype(BF16)
        out_ref[:, pl.ds(pl.multiple_of(at + (1 - core) * TILE, TILE), TILE)] = jnp.where(
            lane < 96, odd, zero
        ).astype(BF16)
        return carry

    lax.fori_loop(0, 2 * half // TILE, step, 0, unroll=min(4, 2 * half // TILE))


def products(s_ref, L_ref, own, order, store, ready=None):
    total = s_ref.shape[1]
    margin = (order - own) // 2
    subs = L_ref.shape[0]
    part = own // 2

    def rows_at(k):
        return pl.ds(pl.multiple_of(k * part, part), part)

    def first(k, carry):
        p = dot_t(s_ref[:, TILE : order - margin], L_ref[0, rows_at(k), margin + TILE :])
        store(pl.multiple_of(k * part, part), part, p)
        return carry

    def last(k, carry):
        start = (subs - 1) * own - margin
        p = dot_t(
            s_ref[:, start : total - TILE], L_ref[subs - 1, rows_at(k), : total - TILE - start]
        )
        store(pl.multiple_of((subs - 1) * own + k * part, part), part, p)
        return carry

    def inner(n, carry):
        j, k = 1 + n // 2, n % 2
        if ready is not None:
            pl.when(k == 0)(lambda: ready(j))
        start = pl.multiple_of(j * own - margin, TILE)
        p = dot_t(s_ref[:, pl.ds(start, order)], L_ref[j, rows_at(k), :])
        store(pl.multiple_of(j * own + k * part, part), part, p)
        return carry

    if ready is not None:
        ready(0)
    lax.fori_loop(0, 2, first, 0)
    lax.fori_loop(0, 2 * (subs - 2), inner, 0)
    if ready is not None:
        ready(subs - 1)
    lax.fori_loop(0, 2, last, 0)


def middle_first(r_ref, L_hbm, v_ref, L_ref, s_ref, sem):
    subs, own, order = L_ref.shape

    def copy(j):
        return pltpu.make_async_copy(L_hbm.at[j], L_ref.at[j], sem.at[j])

    for j in range(subs):
        copy(j).start()
    s_ref[...] = r_ref[...].astype(BF16)

    def store(at, size, p):
        v_ref[:, pl.ds(at, size)] = p

    products(s_ref, L_ref, own, order, store, lambda j: copy(j).wait())


def middle(r_ref, v_ref, u0_ref, u3_ref, dg_ref, cp_ref, L_ref, out_ref, s_ref):
    subs, own, order = L_ref.shape
    total = r_ref.shape[1]
    margin = (order - own) // 2
    sweep_residual(r_ref, parts(v_ref, u0_ref, u3_ref, own), (dg_ref, cp_ref), s_ref)

    for j, u_ref in ((0, u0_ref), (subs - 1, u3_ref)):
        at = j * own
        lo = at - margin
        a, b = max(lo, TILE), min(lo + order, total - TILE)
        out_ref[:, at : at + own] = u_ref[...] + dot_t(
            s_ref[:, a:b], L_ref[j, :, a - lo : b - lo]
        )

    def inner(j, carry):
        at = pl.multiple_of(j * own, own)
        p = dot_t(s_ref[:, pl.ds(pl.multiple_of(at - margin, TILE), order)], L_ref[j])
        out_ref[:, pl.ds(at, own)] = v_ref[:, pl.ds(at, own)] + p
        return carry

    lax.fori_loop(1, subs - 1, inner, 0)


def edge_sends(r_ref, dg_ref, cp_ref, u0_ref, u3_ref, left_ref, right_ref):
    rows, total = r_ref.shape
    own = u0_ref.shape[1]
    count, tiles = CH // TILE, own // TILE
    shift = total - own

    def run(group):
        def left(t, cur, image):
            cols = slice(t * TILE, (t + 1) * TILE)
            left_ref[group, cols] = (r_ref[group, cols] - image).astype(BF16)

        def right(t, cur, image):
            cols = slice(shift + t * TILE, shift + (t + 1) * TILE)
            k = (t - (tiles - count)) * TILE
            right_ref[group, k : k + TILE] = (r_ref[group, cols] - image).astype(BF16)

        read = lambda ref: lambda t: ref[group, t * TILE : (t + 1) * TILE]
        operator(read(u0_ref), 0, count, 0, (dg_ref, cp_ref), 0.0, None, left)
        operator(
            read(u3_ref), tiles - count, tiles, shift, (dg_ref, cp_ref), None, 0.0, right
        )

    by_rows(rows, run)
    left_ref[:, CH : CH + TILE] = spread(u0_ref[:, :1])
    right_ref[:, CH : CH + TILE] = spread(u3_ref[:, own - 1 :])


def edges(first, *refs):
    (core_ref, v_ref, gota_ref, gotb_ref, owna_ref, ownb_ref, metaa_ref, metab_ref) = refs[:8]
    (r_ref, dg_ref, cp_ref, L_ref, u0_ref, u3_ref, senda_ref, sendb_ref) = refs[8:16]
    (wl_ref, wr_ref, info_ref, sl_ref, sr_ref) = refs[16:]
    total = v_ref.shape[1]
    subs, own, order = L_ref.shape
    wide = CH + TILE
    spreads = slice(CH, wide)

    def gather(even):
        a, b = (gota_ref, owna_ref, metaa_ref), (gotb_ref, ownb_ref, metab_ref)
        (gl, ol, ml), (gr, orr, mr) = (b, a) if even else (a, b)
        wl_ref[:, :CH] = gl[:, :CH]
        wl_ref[:, CH:] = ol[:, :TILE]
        wr_ref[:, :TILE] = orr[:, CH - TILE : CH]
        wr_ref[:, TILE:] = gr[:, :CH]
        if not first:
            for k, ref in enumerate((gl, gr, ol, orr, ml, mr)):
                info_ref[k] = ref[:, spreads]

    by_side(core_ref, gather)
    if not first:
        rim_l, rim_r, mine_l, mine_r, coup_l, coup_r = (
            column(info_ref[k], 0) for k in range(6)
        )
        lane = lane_of((v_ref.shape[0], TILE))
        for ref, lo, at, y in (
            (wl_ref, CH, 0, cp_ref[:, :1] * rim_l),
            (wr_ref, 0, TILE - 1, cp_ref[:, total - 1 :] * rim_r),
            (wl_ref, CH - TILE, TILE - 1, coup_l * mine_l),
            (wr_ref, TILE, 0, coup_r * mine_r),
        ):
            x = ref[:, lo : lo + TILE].astype(F32)
            ref[:, lo : lo + TILE] = (x + jnp.where(lane == at, y, 0.0)).astype(BF16)
    u0_ref[...] = v_ref[:, :own] + dot_t(wl_ref[...], L_ref[0, :, :wide])
    u3_ref[...] = v_ref[:, total - own :] + dot_t(
        wr_ref[...], L_ref[subs - 1, :, order - wide :]
    )
    edge_sends(r_ref, dg_ref, cp_ref, u0_ref, u3_ref, sl_ref, sr_ref)

    def send(even):
        senda_ref[...] = (sr_ref if even else sl_ref)[...]
        sendb_ref[...] = (sl_ref if even else sr_ref)[...]

    by_side(core_ref, send)


def project(core_ref, v_ref, u0_ref, u3_ref, r_ref, dg_ref, cp_ref, basis_ref, metaa_ref, metab_ref,
            unused_a, unused_b, out_ref, s_ref, metal_ref, metar_ref):
    rows, total = r_ref.shape
    own = basis_ref.shape[2]
    modes = basis_ref.shape[1]
    get = parts(v_ref, u0_ref, u3_ref, own)
    lane = lane_of((rows, TILE))

    def meta_of(even):
        metal_ref[...] = (metab_ref if even else metaa_ref)[:modes, CH : CH + TILE]
        metar_ref[...] = (metaa_ref if even else metab_ref)[:modes, CH : CH + TILE]

    by_side(core_ref, meta_of)
    sweep_residual(r_ref, get, (dg_ref, cp_ref), s_ref)
    pieces = [
        dot_t(s_ref[:, j * own : (j + 1) * own], basis_ref[j]) for j in range(total // own)
    ]
    first, last = u0_ref[:, :1], u3_ref[:, own - 1 :]
    chosen = (lane == 2) | (lane == 3)
    for value, meta in ((first, metal_ref), (last, metar_ref)):
        hi, lo = split(value)
        coef = meta[...]
        pieces.append(
            dot_t(jnp.where(chosen, hi.astype(F32), 0.0).astype(BF16), coef)
            + dot_t(jnp.where(chosen, lo.astype(F32), 0.0).astype(BF16), coef)
        )
    rims = jnp.zeros((rows, 32), F32)
    lane32 = lane_of((rows, 32))
    for k, value in enumerate((first, last)):
        hi, lo = split(value)
        rims = jnp.where(lane32 == 2 * k, hi.astype(F32), rims)
        rims = jnp.where(lane32 == 2 * k + 1, lo.astype(F32), rims)
    chunk = jnp.concatenate(pieces + [rims], axis=1).astype(BF16)
    for d in range(out_ref.shape[0]):
        out_ref[d] = chunk


def coarse(core_ref, mine_ref, other_ref, W_ref, v_ref, u0_ref, u3_ref, r_ref, dg_ref, cp_ref,
           basis_ref, x_ref, image_ref, sums_ref, a_ref, b_ref, both_ref, rims_ref):
    rows, total = r_ref.shape
    own = basis_ref.shape[2]
    modes = basis_ref.shape[1]
    count = mine_ref.shape[0]
    group = min(8, count)
    c = None
    for k in range(0, count, group):
        tiles = []
        for d in range(k, k + group):
            tiles += [mine_ref[d], other_ref[d]]
        p = dot_t(
            jnp.concatenate(tiles, axis=1), W_ref[:, 2 * k * TILE : 2 * (k + group) * TILE]
        )
        c = p if c is None else c + p
    subs = total // own
    for j in range(subs):
        hi, lo = split(c[:, j * modes : (j + 1) * modes])
        both = jnp.concatenate([hi, lo], axis=1)
        at = j * own
        b = basis_ref[j]
        u = u0_ref[...] if j == 0 else u3_ref[...] if j == subs - 1 else v_ref[:, at : at + own]
        x_ref[:, at : at + own] = u + jnp.dot(
            both, jnp.concatenate([b, b], axis=0), preferred_element_type=F32
        )
    n = subs * modes
    before = other_ref[core_ref[1]]
    after = other_ref[core_ref[2]]
    rim_l = column(before, 98) + c[:, n : n + 1]
    rim_r = column(after, 96) + c[:, n + 1 : n + 2]
    rims_ref[0] = jnp.broadcast_to(rim_l, (rows, TILE))
    rims_ref[1] = jnp.broadcast_to(rim_r, (rows, TILE))

    def run(group):
        acc = [jnp.zeros((GROUP, TILE), F32)] * 2

        def emit(t, cur, image):
            cols = slice(t * TILE, (t + 1) * TILE)
            image_ref[group, cols] = image
            acc[0] = acc[0] + r_ref[group, cols] * image
            acc[1] = acc[1] + image * image

        operator(
            lambda t: x_ref[group, t * TILE : (t + 1) * TILE], 0, total // TILE, 0,
            (dg_ref, cp_ref), rims_ref[0, group, :], rims_ref[1, group, :], emit,
        )
        for k in range(2):
            both_ref[k, group, :] = jnp.broadcast_to(
                jnp.sum(acc[k], axis=1, keepdims=True), (GROUP, TILE)
            )

    by_rows(rows, run)
    flat = jnp.transpose(jnp.concatenate([both_ref[0], both_ref[1]], axis=0))
    sums_ref[...] = flat[: sums_ref.shape[0]]

    def send(even):
        (b_ref if even else a_ref)[...] = image_ref[:, :CH].astype(BF16)
        (a_ref if even else b_ref)[...] = image_ref[:, total - CH :].astype(BF16)

    by_side(core_ref, send)


def step_of(sums_ref, rows):
    s = jnp.sum(sums_ref[...], axis=0, keepdims=True)
    t = jnp.transpose(jnp.broadcast_to(s, (2 * rows, 2 * rows)))
    return t[:rows, :1] / (t[rows:, :1] + 1e-6)


def second(core_ref, sums_ref, x_ref, image_ref, r_ref, ha0_ref, hb0_ref, ha_ref, hb_ref,
           dg_ref, cp_ref, L_ref, sol_ref, res_ref, u_ref, u0_ref, u3_ref, a_ref, b_ref,
           s_ref, sl_ref, sr_ref):
    rows, total = r_ref.shape
    own, order = L_ref.shape[1], L_ref.shape[2]
    alpha = step_of(sums_ref, rows)

    def halo(even):
        for at, one in ((0, even), (CH + total, not even)):
            old, new = (hb0_ref, hb_ref) if one else (ha0_ref, ha_ref)
            s_ref[:, at : at + CH] = (
                old[:, :CH].astype(F32) - alpha * new[...].astype(F32)
            ).astype(BF16)

    by_side(core_ref, halo)
    for lo in range(0, total, TILE):
        cols = slice(lo, lo + TILE)
        r = r_ref[:, cols] - alpha * image_ref[:, cols]
        res_ref[:, cols] = r
        sol_ref[:, cols] = alpha * x_ref[:, cols]
        s_ref[:, CH + lo : CH + lo + TILE] = r.astype(BF16)
    subs = L_ref.shape[0]

    u0_ref[...] = dot_t(s_ref[:, :order], L_ref[0])
    u3_ref[...] = dot_t(s_ref[:, total - own :], L_ref[subs - 1])
    u_ref[:, :own] = u0_ref[...]
    u_ref[:, total - own :] = u3_ref[...]

    def step(j, carry):
        at = pl.multiple_of(j * own, own)
        u_ref[:, pl.ds(at, own)] = dot_t(s_ref[:, pl.ds(at, order)], L_ref[j])
        return carry

    lax.fori_loop(1, subs - 1, step, 0)
    edge_sends(res_ref, dg_ref, cp_ref, u0_ref, u3_ref, sl_ref, sr_ref)

    def send(even):
        a_ref[...] = (sr_ref if even else sl_ref)[...]
        b_ref[...] = (sl_ref if even else sr_ref)[...]

    by_side(core_ref, send)


def finish(sums_ref, x_ref, image_ref, r_ref, sol_in_ref, unused_a, unused_b, sol_ref, res_ref):
    rows, total = r_ref.shape
    alpha = step_of(sums_ref, rows)
    for lo in range(0, total, CH):
        hi = lo + CH
        res_ref[:, lo:hi] = r_ref[:, lo:hi] - alpha * image_ref[:, lo:hi]
        sol_ref[:, lo:hi] = sol_in_ref[:, lo:hi] + alpha * x_ref[:, lo:hi]


def call(kernel, name, outs, args, scratch=(), limit=8, flops=0, smem=1, specs=None):
    vmem = pl.BlockSpec(memory_space=pltpu.VMEM)
    size = sum(a.size * a.dtype.itemsize for a in args)
    return pl.pallas_call(
        kernel,
        out_shape=outs,
        in_specs=specs
        or [pl.BlockSpec(memory_space=pltpu.SMEM)] * smem + [vmem] * (len(args) - smem),
        out_specs=jax.tree.map(lambda _: vmem, outs),
        scratch_shapes=list(scratch),
        compiler_params=pltpu.CompilerParams(vmem_limit_bytes=limit << 20),
        cost_estimate=pl.CostEstimate(flops=flops, bytes_accessed=size, transcendentals=0),
        name=name,
    )(*args)


def body(right_side, diagonal, coupling, local_inverse, coarse_basis, coarse_inverse):
    rows, total = right_side.shape
    subs, own, order = local_inverse.shape
    modes = coarse_basis.shape[1]
    sectors = lax.axis_size("sector")
    chip = [(i, i ^ 1) for i in range(sectors)]
    side = [(i, (i + 1 if i % 2 else i - 1) % sectors) for i in range(sectors)]
    planes = [[2 * k + c for k in range(sectors // 2)] for c in range(2)]
    here = lax.axis_index("sector")
    core = jnp.stack(
        [
            here % 2,
            (here + sectors - 1) % sectors // 2,
            (here + 1) % sectors // 2,
            lax.axis_index("lift"),
        ]
    ).astype(jnp.int32)
    L, basis = local_inverse, coarse_basis
    r = right_side
    dg, cp = diagonal.reshape(1, total), coupling.reshape(1, total)
    wide = CH + TILE
    shape = jax.ShapeDtypeStruct
    full = shape((rows, total), F32)
    sub = shape((rows, own), F32)
    send = shape((rows, wide), BF16)
    long = shape((rows, wide + TILE), BF16)
    s_scratch = pltpu.VMEM((rows, total), BF16)
    pair = lambda like: [pltpu.VMEM(like.shape, like.dtype)] * 2
    work = 2 * rows * subs * own * order

    def exchange(a, b):
        got_b = lax.ppermute(b, "sector", side)
        got_a = lax.ppermute(a, "sector", chip)
        return got_a, got_b

    hbm = pl.BlockSpec(memory_space=pltpu.HBM)
    sa, sb = call(
        first_edges, "first_edges", [long, long], [core, r, cp, basis, coarse_inverse],
        [
            pltpu.VMEM((2, rows, CH), F32),
            pltpu.VMEM((2, 1, TILE), F32),
            pltpu.VMEM((2, modes, TILE), BF16),
            pltpu.VMEM((2, modes, coarse_inverse.shape[1]), F32),
        ]
        + pair(long)
        + [pltpu.SemaphoreType.DMA((8,))],
        EDGE_LIMIT,
        specs=[pl.BlockSpec(memory_space=pltpu.SMEM)] + [hbm] * 4,
    )
    got_a0, got_b0 = exchange(sa, sb)
    v, L = call(
        middle_first, "middle_first", [full, shape(L.shape, L.dtype)], [r, L],
        [s_scratch, pltpu.SemaphoreType.DMA((subs,))],
        FIRST_LIMIT, work, specs=[pl.BlockSpec(memory_space=pltpu.VMEM), hbm],
    )
    weights = []

    def sweeps(v, u0, u3, sa, sb, start):
        for sweep in range(start, SWEEPS):
            last = sweep == SWEEPS - 1
            if sweep == 0:
                vv, ga, gb = v, got_a0, got_b0
            else:
                ga, gb = exchange(sa, sb)
                vv = call(
                    middle, "middle", full, [r, v, u0, u3, dg, cp, L], [s_scratch], 8, work, 0
                )
            if sweep == 1 and not weights:
                ci, _ = lax.optimization_barrier((coarse_inverse, vv))
                lines = call(
                    lines_of, "lines", shape((ci.shape[0] + 8, ci.shape[1]), BF16),
                    [core, ci, got_a0, got_b0], pair(long),
                )
                other = lax.ppermute(lines, "lift", [(0, 1), (1, 0)])
                weights.append((lines, other))
            if sweep == 2 and len(weights) == 1:
                lines, other = weights[0]
                other, _ = lax.optimization_barrier((other, vv))
                weights.append(
                    call(
                        weave, "weave", shape((lines.shape[0], sectors * TILE), BF16),
                        [core, lines, other],
                        [pltpu.VMEM((lines.shape[0], 2 * lines.shape[1] + 2 * TILE), F32)],
                    )
                )
            first = sweep == 0
            if last and start == 0:
                vv, weights[1] = lax.optimization_barrier((vv, weights[1]))
            u0, u3, sa, sb = call(
                functools.partial(edges, first), "edges_first" if first else "edges",
                [sub, sub, send, send],
                [core, vv, ga, gb, sa, sb, got_a0, got_b0, r, dg, cp, L],
                pair(send) + [pltpu.VMEM((6, rows, TILE), BF16)] + pair(send),
                flops=work // 8,
            )
            v = vv
        return v, u0, u3, sa, sb

    edge = shape((rows, CH), BF16)

    def coarse_step(v, u0, u3, sa, sb):
        W = weights[1]
        chunk = call(
            project, "project", shape((sectors // 2, rows, TILE), BF16),
            [core, v, u0, u3, r, dg, cp, basis, got_a0, got_b0, sa, sb],
            [s_scratch] + [pltpu.VMEM((modes, TILE), BF16)] * 2,
        )
        chunk, W = lax.optimization_barrier((chunk, W))
        mine = lax.all_to_all(
            chunk, "sector", 0, 0, axis_index_groups=planes, tiled=True
        )
        other = lax.ppermute(mine, "sector", chip)
        return call(
            coarse, "coarse", [full, full, shape((sectors, 2 * rows), F32), edge, edge],
            [core, mine, other, W, v, u0, u3, r, dg, cp, basis],
            [pltpu.VMEM((2, rows, TILE), F32)] * 2,
        )

    v, u0, u3, sa, sb = sweeps(v, None, None, sa, sb, 0)
    x, image, sums, ia, ib = coarse_step(v, u0, u3, sa, sb)
    halo_a, halo_b = exchange(ia, ib)
    sums = lax.all_to_all(sums, "sector", 0, 0, tiled=True)
    sol, r, v, u0, u3, sa, sb = call(
        second, "second", [full, full, full, sub, sub, send, send],
        [core, sums, x, image, r, got_a0, got_b0, halo_a, halo_b, dg, cp, L],
        [pltpu.VMEM((rows, total + 2 * CH), BF16)] + pair(send), 8, work,
    )
    v, u0, u3, sa, sb = sweeps(v, u0, u3, sa, sb, 1)
    x, image, sums, ia, ib = coarse_step(v, u0, u3, sa, sb)
    sums = lax.all_to_all(sums, "sector", 0, 0, tiled=True)
    sol, res = call(finish, "finish", [full, full], [sums, x, image, r, sol, ia, ib], smem=0)
    return sol, res


def solution(mesh):
    in_specs = (
        P("lift", "sector"),
        P("sector"),
        P("sector"),
        P("sector", None, None),
        P("sector", None, None),
        P("sector", "lift"),
    )
    out_specs = (P("lift", "sector"), P("lift", "sector"))
    return jax.shard_map(body, mesh=mesh, in_specs=in_specs, out_specs=out_specs, check_vma=False)
```

```python
import functools

import jax
import jax.numpy as jnp
from jax import lax
from jax.experimental import pallas as pl
from jax.experimental.pallas import tpu as pltpu
from jax.sharding import PartitionSpec as P

SWEEPS = 4
F32, BF16 = jnp.float32, jnp.bfloat16
CH = 512
TILE = 128
EDGE_LIMIT = 57
FIRST_LIMIT = 20


def lane_of(shape):
    return lax.broadcasted_iota(jnp.int32, shape, 1)


def dot_t(a, b):
    return lax.dot_general(a, b, (((1,), (1,)), ((), ())), preferred_element_type=F32)


def split(x):
    hi = x.astype(BF16)
    return hi, (x - hi.astype(F32)).astype(BF16)


def spread(x):
    hi = x.astype(BF16).astype(F32)
    lo = (x - hi).astype(BF16).astype(F32)
    lane = lane_of((x.shape[0], TILE))
    return jnp.where(lane == 0, hi, jnp.where(lane == 1, lo, 0.0)).astype(BF16)


def column(tile, at):
    return tile[:, at : at + 1].astype(F32) + tile[:, at + 1 : at + 2].astype(F32)


GROUP = 16


def by_rows(rows, run):
    for at in range(0, rows, GROUP):
        run(slice(at, at + GROUP))


def operator(read, first, last, total, coefs, before, after, emit):
    dg_ref, cp_ref = coefs
    lane = lane_of((GROUP, TILE))
    cur = read(first)
    down = pltpu.roll(cur, TILE - 1, 1)
    prev = before if before is not None else pltpu.roll(read(first - 1), 1, 1)
    for t in range(first, last):
        up = pltpu.roll(cur, 1, 1)
        if t + 1 < last or after is None:
            ahead = read(t + 1)
            ahead_down = pltpu.roll(ahead, TILE - 1, 1)
        else:
            ahead, ahead_down = None, after
        left = jnp.where(lane == 0, prev, up)
        right = jnp.where(lane == TILE - 1, ahead_down, down)
        cols = slice(total + t * TILE, total + (t + 1) * TILE)
        emit(t, cur, dg_ref[:, cols] * cur - cp_ref[:, cols] * (left + right))
        cur, down, prev = ahead, ahead_down, up


def parts(v_ref, u0_ref, u3_ref, own):
    tiles, outer = v_ref.shape[1] // TILE, own // TILE

    def get(rows, t):
        if t < outer:
            return u0_ref[rows, t * TILE : (t + 1) * TILE]
        if t >= tiles - outer:
            t = t - (tiles - outer)
            return u3_ref[rows, t * TILE : (t + 1) * TILE]
        return v_ref[rows, t * TILE : (t + 1) * TILE]

    return get


def sweep_residual(r_ref, get, coefs, s_ref):
    rows, total = r_ref.shape

    def run(group):
        def emit(t, cur, image):
            cols = slice(t * TILE, (t + 1) * TILE)
            s_ref[group, cols] = (r_ref[group, cols] - image).astype(BF16)

        operator(lambda t: get(group, t), 0, total // TILE, 0, coefs, 0.0, 0.0, emit)

    by_rows(rows, run)


def pick(core_ref, a_ref, b_ref, left_ref, right_ref):
    @pl.when(core_ref[0] == 0)
    def _():
        left_ref[...] = b_ref[...]
        right_ref[...] = a_ref[...]

    @pl.when(core_ref[0] != 0)
    def _():
        left_ref[...] = a_ref[...]
        right_ref[...] = b_ref[...]


def first_edges(core_ref, r_hbm, cp_hbm, basis_hbm, ci_hbm, a_ref, b_ref,
                r_ref, cp_ref, basis_ref, ci_ref, left_ref, right_ref, sem):
    rows, total = r_hbm.shape
    subs, modes, own = basis_hbm.shape
    copies = []
    for k, (at, sub, tile_lo, cp_lo) in enumerate(
        ((0, 0, 0, 0), (total - CH, subs - 1, own - TILE, total - TILE))
    ):
        for n, (src, dst) in enumerate(
            (
                (r_hbm.at[:, pl.ds(at, CH)], r_ref.at[k]),
                (cp_hbm.at[:, pl.ds(cp_lo, TILE)], cp_ref.at[k]),
                (basis_hbm.at[sub, :, pl.ds(tile_lo, TILE)], basis_ref.at[k]),
                (ci_hbm.at[pl.ds(sub * modes, modes), :], ci_ref.at[k]),
            )
        ):
            copies.append(pltpu.make_async_copy(src, dst, sem.at[4 * k + n]))
    for c in copies:
        c.start()
    for c in copies:
        c.wait()
    lane = lane_of((modes, TILE))
    for k, (out, col, roll) in enumerate(((left_ref, 0, 2), (right_ref, TILE - 1, 3))):
        out[:, :CH] = r_ref[k].astype(BF16)
        one = cp_ref[k][:, col : col + 1]
        meta = spread(jnp.broadcast_to(one, (rows, 1))).astype(F32)
        weight = basis_ref[k].astype(F32)
        edge = pltpu.roll(weight, roll, 1) * one
        hi = edge.astype(BF16).astype(F32)
        lo = pltpu.roll(edge - hi, 1, 1)
        both = jnp.where(lane == 2, hi, jnp.where(lane == 3, lo, 0.0))
        out[:, CH : CH + TILE] = meta.astype(BF16)
        out[:modes, CH : CH + TILE] = (meta[:modes] + both).astype(BF16)
        line = jnp.sum(weight[:, col : col + 1] * ci_ref[k], axis=0, keepdims=True)
        count = line.shape[1] // TILE
        out[:, CH + TILE :] = jnp.zeros((rows, TILE), BF16)
        out[:count, CH + TILE :] = jnp.concatenate(
            [line[:, n * TILE : (n + 1) * TILE] for n in range(count)], axis=0
        ).astype(BF16)
    def send(even):
        a_ref[...] = (right_ref if even else left_ref)[...]
        b_ref[...] = (left_ref if even else right_ref)[...]

    by_side(core_ref, send)


def by_side(core_ref, run):
    pl.when(core_ref[0] == 0)(lambda: run(True))
    pl.when(core_ref[0] != 0)(lambda: run(False))


def lines_of(core_ref, ci_ref, a_ref, b_ref, out_ref, left_ref, right_ref):
    pick(core_ref, a_ref, b_ref, left_ref, right_ref)
    rows, width = ci_ref.shape
    out_ref[:rows, :] = ci_ref[...].astype(BF16)
    extra = []
    for ref in (left_ref, right_ref):
        block = ref[:, CH + TILE :].astype(F32)
        extra.append(
            jnp.concatenate([block[k : k + 1, :] for k in range(width // TILE)], axis=1)
        )
    extra.append(jnp.zeros((6, width), F32))
    out_ref[rows:, :] = jnp.concatenate(extra, axis=0).astype(BF16)


def weave(core_ref, mine_ref, other_ref, out_ref, all_ref):
    rows, half = mine_ref.shape
    low = core_ref[3] == 0

    @pl.when(low)
    def _():
        all_ref[:, TILE : TILE + half] = mine_ref[...].astype(F32)
        all_ref[:, TILE + half : TILE + 2 * half] = other_ref[...].astype(F32)

    @pl.when(jnp.logical_not(low))
    def _():
        all_ref[:, TILE : TILE + half] = other_ref[...].astype(F32)
        all_ref[:, TILE + half : TILE + 2 * half] = mine_ref[...].astype(F32)

    all_ref[:, :TILE] = all_ref[:, 2 * half : 2 * half + TILE]
    all_ref[:, 2 * half + TILE :] = all_ref[:, TILE : 2 * TILE]
    lane = lane_of((rows, TILE))
    core = core_ref[0]
    zero = jnp.zeros((rows, TILE), F32)

    def step(k, carry):
        at = pl.multiple_of(k * TILE, TILE)
        prev = all_ref[:, pl.ds(at, TILE)]
        tile = all_ref[:, pl.ds(pl.multiple_of(at + TILE, TILE), TILE)]
        after = all_ref[:, pl.ds(pl.multiple_of(at + 2 * TILE, TILE), TILE)]
        near = pltpu.roll(tile, 16, 1)
        even = jnp.where(lane < 64, tile, jnp.where(lane < 80, pltpu.roll(prev, 80, 1), near))
        odd = jnp.where(lane < 64, pltpu.roll(tile, 64, 1), jnp.where(lane < 80, near, pltpu.roll(after, 80, 1)))
        at = 2 * k * TILE
        out_ref[:, pl.ds(pl.multiple_of(at + core * TILE, TILE), TILE)] = jnp.where(
            lane < 96, even, zero
        ).astype(BF16)
        out_ref[:, pl.ds(pl.multiple_of(at + (1 - core) * TILE, TILE), TILE)] = jnp.where(
            lane < 96, odd, zero
        ).astype(BF16)
        return carry

    lax.fori_loop(0, 2 * half // TILE, step, 0, unroll=min(4, 2 * half // TILE))


def products(s_ref, L_ref, own, order, store, ready=None):
    total = s_ref.shape[1]
    margin = (order - own) // 2
    subs = L_ref.shape[0]
    part = own // 2
    quarter = own // 4

    def rows_at(k, part=part):
        return pl.ds(pl.multiple_of(k * part, part), part)

    def first(k, carry):
        p = dot_t(s_ref[:, TILE : order - margin], L_ref[0, rows_at(k, quarter), margin + TILE :])
        store(pl.multiple_of(k * quarter, quarter), quarter, p)
        return carry

    def last(k, carry):
        start = (subs - 1) * own - margin
        p = dot_t(
            s_ref[:, start : total - TILE],
            L_ref[subs - 1, rows_at(k, quarter), : total - TILE - start],
        )
        store(pl.multiple_of((subs - 1) * own + k * quarter, quarter), quarter, p)
        return carry

    def inner(n, carry):
        j, k = 1 + n // 2, n % 2
        if ready is not None:
            pl.when(k == 0)(lambda: ready(j))
        start = pl.multiple_of(j * own - margin, TILE)
        p = dot_t(s_ref[:, pl.ds(start, order)], L_ref[j, rows_at(k), :])
        store(pl.multiple_of(j * own + k * part, part), part, p)
        return carry

    if ready is not None:
        ready(0)
    lax.fori_loop(0, 4, first, 0)
    lax.fori_loop(0, 2 * (subs - 2), inner, 0)
    if ready is not None:
        ready(subs - 1)
    lax.fori_loop(0, 4, last, 0)


def middle_first(r_ref, L_hbm, v_ref, L_ref, s_ref, sem):
    subs, own, order = L_ref.shape

    def copy(j):
        return pltpu.make_async_copy(L_hbm.at[j], L_ref.at[j], sem.at[j])

    for j in range(subs):
        copy(j).start()
    s_ref[...] = r_ref[...].astype(BF16)

    def store(at, size, p):
        v_ref[:, pl.ds(at, size)] = p

    products(s_ref, L_ref, own, order, store, lambda j: copy(j).wait())


def complete(v_ref, near_l_ref, near_r_ref, wl_ref, wr_ref, L_ref, u0_ref, u3_ref):
    subs, own, order = L_ref.shape
    total, wide = v_ref.shape[1], wl_ref.shape[1]
    u0_ref[:, :wide] = near_l_ref[...]
    u0_ref[:, wide:] = v_ref[:, wide:own] + dot_t(wl_ref[...], L_ref[0, wide:, :wide])
    u3_ref[:, own - wide :] = near_r_ref[...]
    u3_ref[:, : own - wide] = v_ref[:, total - own : total - wide] + dot_t(
        wr_ref[...], L_ref[subs - 1, : own - wide, order - wide :]
    )


def middle_near(r_ref, v_ref, near_l_ref, near_r_ref, wl_ref, wr_ref, dg_ref, cp_ref, L_ref,
                out_ref, s_ref, u0_ref, u3_ref):
    complete(v_ref, near_l_ref, near_r_ref, wl_ref, wr_ref, L_ref, u0_ref, u3_ref)
    middle(r_ref, v_ref, u0_ref, u3_ref, dg_ref, cp_ref, L_ref, out_ref, s_ref)


def middle(r_ref, v_ref, u0_ref, u3_ref, dg_ref, cp_ref, L_ref, out_ref, s_ref):
    subs, own, order = L_ref.shape
    total = r_ref.shape[1]
    margin = (order - own) // 2
    sweep_residual(r_ref, parts(v_ref, u0_ref, u3_ref, own), (dg_ref, cp_ref), s_ref)

    for j, u_ref in ((0, u0_ref), (subs - 1, u3_ref)):
        at = j * own
        lo = at - margin
        a, b = max(lo, TILE), min(lo + order, total - TILE)
        out_ref[:, at : at + own] = u_ref[...] + dot_t(
            s_ref[:, a:b], L_ref[j, :, a - lo : b - lo]
        )

    def inner(j, carry):
        at = pl.multiple_of(j * own, own)
        p = dot_t(s_ref[:, pl.ds(pl.multiple_of(at - margin, TILE), order)], L_ref[j])
        out_ref[:, pl.ds(at, own)] = v_ref[:, pl.ds(at, own)] + p
        return carry

    lax.fori_loop(1, subs - 1, inner, 0)


def edge_sends(r_ref, dg_ref, cp_ref, u0_ref, u3_ref, left_ref, right_ref):
    rows, total = r_ref.shape
    own = u0_ref.shape[1]
    count, tiles = CH // TILE, own // TILE
    shift = total - own

    def run(group):
        def left(t, cur, image):
            cols = slice(t * TILE, (t + 1) * TILE)
            left_ref[group, cols] = (r_ref[group, cols] - image).astype(BF16)

        def right(t, cur, image):
            cols = slice(shift + t * TILE, shift + (t + 1) * TILE)
            k = (t - (tiles - count)) * TILE
            right_ref[group, k : k + TILE] = (r_ref[group, cols] - image).astype(BF16)

        read = lambda ref: lambda t: ref[group, t * TILE : (t + 1) * TILE]
        operator(read(u0_ref), 0, count, 0, (dg_ref, cp_ref), 0.0, None, left)
        operator(
            read(u3_ref), tiles - count, tiles, shift, (dg_ref, cp_ref), None, 0.0, right
        )

    by_rows(rows, run)
    left_ref[:, CH : CH + TILE] = spread(u0_ref[:, :1])
    right_ref[:, CH : CH + TILE] = spread(u3_ref[:, own - 1 :])


def edges(first, *refs):
    (core_ref, v_ref, gota_ref, gotb_ref, owna_ref, ownb_ref, metaa_ref, metab_ref) = refs[:8]
    (r_ref, dg_ref, cp_ref, L_ref, u0_ref, u3_ref, wl_ref, wr_ref) = refs[8:16]
    (senda_ref, sendb_ref, info_ref, sl_ref, sr_ref) = refs[16:]
    total = v_ref.shape[1]
    subs, own, order = L_ref.shape
    wide = CH + TILE
    spreads = slice(CH, wide)

    def gather(even):
        a, b = (gota_ref, owna_ref, metaa_ref), (gotb_ref, ownb_ref, metab_ref)
        (gl, ol, ml), (gr, orr, mr) = (b, a) if even else (a, b)
        wl_ref[:, :CH] = gl[:, :CH]
        wl_ref[:, CH:] = ol[:, :TILE]
        wr_ref[:, :TILE] = orr[:, CH - TILE : CH]
        wr_ref[:, TILE:] = gr[:, :CH]
        if not first:
            for k, ref in enumerate((gl, gr, ol, orr, ml, mr)):
                info_ref[k] = ref[:, spreads]

    by_side(core_ref, gather)
    if not first:
        rim_l, rim_r, mine_l, mine_r, coup_l, coup_r = (
            column(info_ref[k], 0) for k in range(6)
        )
        lane = lane_of((v_ref.shape[0], TILE))
        for ref, lo, at, y in (
            (wl_ref, CH, 0, cp_ref[:, :1] * rim_l),
            (wr_ref, 0, TILE - 1, cp_ref[:, total - 1 :] * rim_r),
            (wl_ref, CH - TILE, TILE - 1, coup_l * mine_l),
            (wr_ref, TILE, 0, coup_r * mine_r),
        ):
            x = ref[:, lo : lo + TILE].astype(F32)
            ref[:, lo : lo + TILE] = (x + jnp.where(lane == at, y, 0.0)).astype(BF16)
    u0_ref[...] = v_ref[:, :wide] + dot_t(wl_ref[...], L_ref[0, :wide, :wide])
    u3_ref[...] = v_ref[:, total - wide :] + dot_t(
        wr_ref[...], L_ref[subs - 1, own - wide :, order - wide :]
    )
    edge_sends(r_ref, dg_ref, cp_ref, u0_ref, u3_ref, sl_ref, sr_ref)

    def send(even):
        senda_ref[...] = (sr_ref if even else sl_ref)[...]
        sendb_ref[...] = (sl_ref if even else sr_ref)[...]

    by_side(core_ref, send)


def project(core_ref, v_ref, near_l_ref, near_r_ref, wl_ref, wr_ref, L_ref, r_ref, dg_ref, cp_ref,
            basis_ref, metaa_ref, metab_ref, unused_a, unused_b, out_ref, u0_ref, u3_ref,
            s_ref, metal_ref, metar_ref):
    complete(v_ref, near_l_ref, near_r_ref, wl_ref, wr_ref, L_ref, u0_ref, u3_ref)
    rows, total = r_ref.shape
    own = basis_ref.shape[2]
    modes = basis_ref.shape[1]
    get = parts(v_ref, u0_ref, u3_ref, own)
    lane = lane_of((rows, TILE))

    def meta_of(even):
        metal_ref[...] = (metab_ref if even else metaa_ref)[:modes, CH : CH + TILE]
        metar_ref[...] = (metaa_ref if even else metab_ref)[:modes, CH : CH + TILE]

    by_side(core_ref, meta_of)
    sweep_residual(r_ref, get, (dg_ref, cp_ref), s_ref)
    pieces = [
        dot_t(s_ref[:, j * own : (j + 1) * own], basis_ref[j]) for j in range(total // own)
    ]
    first, last = u0_ref[:, :1], u3_ref[:, own - 1 :]
    chosen = (lane == 2) | (lane == 3)
    for value, meta in ((first, metal_ref), (last, metar_ref)):
        hi, lo = split(value)
        coef = meta[...]
        pieces.append(
            dot_t(jnp.where(chosen, hi.astype(F32), 0.0).astype(BF16), coef)
            + dot_t(jnp.where(chosen, lo.astype(F32), 0.0).astype(BF16), coef)
        )
    rims = jnp.zeros((rows, 32), F32)
    lane32 = lane_of((rows, 32))
    for k, value in enumerate((first, last)):
        hi, lo = split(value)
        rims = jnp.where(lane32 == 2 * k, hi.astype(F32), rims)
        rims = jnp.where(lane32 == 2 * k + 1, lo.astype(F32), rims)
    chunk = jnp.concatenate(pieces + [rims], axis=1).astype(BF16)
    for d in range(out_ref.shape[0]):
        out_ref[d] = chunk


def coarse(core_ref, mine_ref, other_ref, W_ref, v_ref, u0_ref, u3_ref, r_ref, dg_ref, cp_ref,
           basis_ref, x_ref, image_ref, sums_ref, a_ref, b_ref, both_ref, rims_ref):
    rows, total = r_ref.shape
    own = basis_ref.shape[2]
    modes = basis_ref.shape[1]
    count = mine_ref.shape[0]
    group = min(8, count)
    c = None
    for k in range(0, count, group):
        tiles = []
        for d in range(k, k + group):
            tiles += [mine_ref[d], other_ref[d]]
        p = dot_t(
            jnp.concatenate(tiles, axis=1), W_ref[:, 2 * k * TILE : 2 * (k + group) * TILE]
        )
        c = p if c is None else c + p
    subs = total // own
    for j in range(subs):
        hi, lo = split(c[:, j * modes : (j + 1) * modes])
        both = jnp.concatenate([hi, lo], axis=1)
        at = j * own
        b = basis_ref[j]
        u = u0_ref[...] if j == 0 else u3_ref[...] if j == subs - 1 else v_ref[:, at : at + own]
        x_ref[:, at : at + own] = u + jnp.dot(
            both, jnp.concatenate([b, b], axis=0), preferred_element_type=F32
        )
    n = subs * modes
    before = other_ref[core_ref[1]]
    after = other_ref[core_ref[2]]
    rim_l = column(before, 98) + c[:, n : n + 1]
    rim_r = column(after, 96) + c[:, n + 1 : n + 2]
    rims_ref[0] = jnp.broadcast_to(rim_l, (rows, TILE))
    rims_ref[1] = jnp.broadcast_to(rim_r, (rows, TILE))

    def run(group):
        acc = [jnp.zeros((GROUP, TILE), F32)] * 2

        def emit(t, cur, image):
            cols = slice(t * TILE, (t + 1) * TILE)
            image_ref[group, cols] = image
            acc[0] = acc[0] + r_ref[group, cols] * image
            acc[1] = acc[1] + image * image

        operator(
            lambda t: x_ref[group, t * TILE : (t + 1) * TILE], 0, total // TILE, 0,
            (dg_ref, cp_ref), rims_ref[0, group, :], rims_ref[1, group, :], emit,
        )
        for k in range(2):
            both_ref[k, group, :] = jnp.broadcast_to(
                jnp.sum(acc[k], axis=1, keepdims=True), (GROUP, TILE)
            )

    by_rows(rows, run)
    flat = jnp.transpose(jnp.concatenate([both_ref[0], both_ref[1]], axis=0))
    sums_ref[...] = flat[: sums_ref.shape[0]]

    def send(even):
        (b_ref if even else a_ref)[...] = image_ref[:, :CH].astype(BF16)
        (a_ref if even else b_ref)[...] = image_ref[:, total - CH :].astype(BF16)

    by_side(core_ref, send)


def step_of(sums_ref, rows):
    s = jnp.sum(sums_ref[...], axis=0, keepdims=True)
    t = jnp.transpose(jnp.broadcast_to(s, (2 * rows, 2 * rows)))
    return t[:rows, :1] / (t[rows:, :1] + 1e-6)


def second(core_ref, sums_ref, x_ref, image_ref, r_ref, ha0_ref, hb0_ref, ha_ref, hb_ref,
           dg_ref, cp_ref, L_ref, sol_ref, res_ref, u_ref, u0_ref, u3_ref, a_ref, b_ref,
           s_ref, sl_ref, sr_ref):
    rows, total = r_ref.shape
    own, order = L_ref.shape[1], L_ref.shape[2]
    alpha = step_of(sums_ref, rows)

    def halo(even):
        for at, one in ((0, even), (CH + total, not even)):
            old, new = (hb0_ref, hb_ref) if one else (ha0_ref, ha_ref)
            s_ref[:, at : at + CH] = (
                old[:, :CH].astype(F32) - alpha * new[...].astype(F32)
            ).astype(BF16)

    by_side(core_ref, halo)
    for lo in range(0, total, TILE):
        cols = slice(lo, lo + TILE)
        r = r_ref[:, cols] - alpha * image_ref[:, cols]
        res_ref[:, cols] = r
        sol_ref[:, cols] = alpha * x_ref[:, cols]
        s_ref[:, CH + lo : CH + lo + TILE] = r.astype(BF16)
    subs = L_ref.shape[0]

    u0_ref[...] = dot_t(s_ref[:, :order], L_ref[0])
    u3_ref[...] = dot_t(s_ref[:, total - own :], L_ref[subs - 1])
    u_ref[:, :own] = u0_ref[...]
    u_ref[:, total - own :] = u3_ref[...]

    def step(j, carry):
        at = pl.multiple_of(j * own, own)
        u_ref[:, pl.ds(at, own)] = dot_t(s_ref[:, pl.ds(at, order)], L_ref[j])
        return carry

    lax.fori_loop(1, subs - 1, step, 0)
    edge_sends(res_ref, dg_ref, cp_ref, u0_ref, u3_ref, sl_ref, sr_ref)

    def send(even):
        a_ref[...] = (sr_ref if even else sl_ref)[...]
        b_ref[...] = (sl_ref if even else sr_ref)[...]

    by_side(core_ref, send)


def finish(sums_ref, x_ref, image_ref, r_ref, sol_in_ref, unused_a, unused_b, sol_ref, res_ref):
    rows, total = r_ref.shape
    alpha = step_of(sums_ref, rows)
    width = total // 2

    def half(k, carry):
        cols = pl.ds(pl.multiple_of(k * width, width), width)
        res_ref[:, cols] = r_ref[:, cols] - alpha * image_ref[:, cols]
        sol_ref[:, cols] = sol_in_ref[:, cols] + alpha * x_ref[:, cols]
        return carry

    lax.fori_loop(0, 2, half, 0)


def call(kernel, name, outs, args, scratch=(), limit=8, flops=0, smem=1, specs=None):
    vmem = pl.BlockSpec(memory_space=pltpu.VMEM)
    size = sum(a.size * a.dtype.itemsize for a in args)
    return pl.pallas_call(
        kernel,
        out_shape=outs,
        in_specs=specs
        or [pl.BlockSpec(memory_space=pltpu.SMEM)] * smem + [vmem] * (len(args) - smem),
        out_specs=jax.tree.map(lambda _: vmem, outs),
        scratch_shapes=list(scratch),
        compiler_params=pltpu.CompilerParams(vmem_limit_bytes=limit << 20),
        cost_estimate=pl.CostEstimate(flops=flops, bytes_accessed=size, transcendentals=0),
        name=name,
    )(*args)


def body(right_side, diagonal, coupling, local_inverse, coarse_basis, coarse_inverse):
    rows, total = right_side.shape
    subs, own, order = local_inverse.shape
    modes = coarse_basis.shape[1]
    sectors = lax.axis_size("sector")
    chip = [(i, i ^ 1) for i in range(sectors)]
    side = [(i, (i + 1 if i % 2 else i - 1) % sectors) for i in range(sectors)]
    planes = [[2 * k + c for k in range(sectors // 2)] for c in range(2)]
    here = lax.axis_index("sector")
    core = jnp.stack(
        [
            here % 2,
            (here + sectors - 1) % sectors // 2,
            (here + 1) % sectors // 2,
            lax.axis_index("lift"),
        ]
    ).astype(jnp.int32)
    L, basis = local_inverse, coarse_basis
    r = right_side
    dg, cp = diagonal.reshape(1, total), coupling.reshape(1, total)
    wide = CH + TILE
    shape = jax.ShapeDtypeStruct
    full = shape((rows, total), F32)
    sub = shape((rows, own), F32)
    near = shape((rows, wide), F32)
    send = shape((rows, wide), BF16)
    long = shape((rows, wide + TILE), BF16)
    s_scratch = pltpu.VMEM((rows, total), BF16)
    pair = lambda like: [pltpu.VMEM(like.shape, like.dtype)] * 2
    work = 2 * rows * subs * own * order

    def exchange(a, b):
        got_b = lax.ppermute(b, "sector", side)
        got_a = lax.ppermute(a, "sector", chip)
        return got_a, got_b

    hbm = pl.BlockSpec(memory_space=pltpu.HBM)
    sa, sb = call(
        first_edges, "first_edges", [long, long], [core, r, cp, basis, coarse_inverse],
        [
            pltpu.VMEM((2, rows, CH), F32),
            pltpu.VMEM((2, 1, TILE), F32),
            pltpu.VMEM((2, modes, TILE), BF16),
            pltpu.VMEM((2, modes, coarse_inverse.shape[1]), F32),
        ]
        + pair(long)
        + [pltpu.SemaphoreType.DMA((8,))],
        EDGE_LIMIT,
        specs=[pl.BlockSpec(memory_space=pltpu.SMEM)] + [hbm] * 4,
    )
    got_a0, got_b0 = exchange(sa, sb)
    v, L = call(
        middle_first, "middle_first", [full, shape(L.shape, L.dtype)], [r, L],
        [s_scratch, pltpu.SemaphoreType.DMA((subs,))],
        FIRST_LIMIT, work, specs=[pl.BlockSpec(memory_space=pltpu.VMEM), hbm],
    )
    weights = []

    def sweeps(v, u, sa, sb, start):
        for sweep in range(start, SWEEPS):
            last = sweep == SWEEPS - 1
            if sweep == 0:
                vv, ga, gb = v, got_a0, got_b0
            else:
                ga, gb = exchange(sa, sb)
                if len(u) == 2:
                    vv = call(
                        middle, "middle", full, [r, v, *u, dg, cp, L], [s_scratch], 8, work, 0
                    )
                else:
                    vv = call(
                        middle_near, "middle_near", full, [r, v, *u, dg, cp, L],
                        [s_scratch] + pair(sub), 8, work, 0,
                    )
            if sweep == 1 and not weights:
                ci, _ = lax.optimization_barrier((coarse_inverse, vv))
                lines = call(
                    lines_of, "lines", shape((ci.shape[0] + 8, ci.shape[1]), BF16),
                    [core, ci, got_a0, got_b0], pair(long),
                )
                other = lax.ppermute(lines, "lift", [(0, 1), (1, 0)])
                weights.append([lines, other])
            if sweep == 2 and len(weights) == 1:
                vv, *weights[0] = lax.optimization_barrier((vv, *weights[0]))
            first = sweep == 0
            *u, sa, sb = call(
                functools.partial(edges, first), "edges_first" if first else "edges",
                [near, near, send, send, send, send],
                [core, vv, ga, gb, sa, sb, got_a0, got_b0, r, dg, cp, L],
                [pltpu.VMEM((6, rows, TILE), BF16)] + pair(send),
                flops=work // 8,
            )
            v = vv
        return v, u, sa, sb

    edge = shape((rows, CH), BF16)

    def coarse_step(v, u, sa, sb):
        chunk, u0, u3 = call(
            project, "project", [shape((sectors // 2, rows, TILE), BF16), sub, sub],
            [core, v, *u, L, r, dg, cp, basis, got_a0, got_b0, sa, sb],
            [s_scratch] + [pltpu.VMEM((modes, TILE), BF16)] * 2,
        )
        mine = lax.all_to_all(
            chunk, "sector", 0, 0, axis_index_groups=planes, tiled=True
        )
        other = lax.ppermute(mine, "sector", chip)
        if len(weights) == 1:
            lines, swapped = weights[0]
            lines, swapped, _ = lax.optimization_barrier((lines, swapped, mine))
            weights.append(
                call(
                    weave, "weave", shape((lines.shape[0], sectors * TILE), BF16),
                    [core, lines, swapped],
                    [pltpu.VMEM((lines.shape[0], 2 * lines.shape[1] + 2 * TILE), F32)],
                    flops=1 << 26,
                )
            )
        W = weights[1]
        return call(
            coarse, "coarse", [full, full, shape((sectors, 2 * rows), F32), edge, edge],
            [core, mine, other, W, v, u0, u3, r, dg, cp, basis],
            [pltpu.VMEM((2, rows, TILE), F32)] * 2,
        )

    v, u, sa, sb = sweeps(v, None, sa, sb, 0)
    x, image, sums, ia, ib = coarse_step(v, u, sa, sb)
    halo_a, halo_b = exchange(ia, ib)
    sums = lax.all_to_all(sums, "sector", 0, 0, tiled=True)
    sol, r, v, u0, u3, sa, sb = call(
        second, "second", [full, full, full, sub, sub, send, send],
        [core, sums, x, image, r, got_a0, got_b0, halo_a, halo_b, dg, cp, L],
        [pltpu.VMEM((rows, total + 2 * CH), BF16)] + pair(send), 8, work,
    )
    v, u, sa, sb = sweeps(v, (u0, u3), sa, sb, 1)
    x, image, sums, ia, ib = coarse_step(v, u, sa, sb)
    sums = lax.all_to_all(sums, "sector", 0, 0, tiled=True)
    sol, res = call(finish, "finish", [full, full], [sums, x, image, r, sol, ia, ib], smem=0)
    return sol, res


def solution(mesh):
    in_specs = (
        P("lift", "sector"),
        P("sector"),
        P("sector"),
        P("sector", None, None),
        P("sector", None, None),
        P("sector", "lift"),
    )
    out_specs = (P("lift", "sector"), P("lift", "sector"))
    return jax.shard_map(body, mesh=mesh, in_specs=in_specs, out_specs=out_specs, check_vma=False)
```

```python
import functools

import jax
import jax.numpy as jnp
from jax import lax
from jax.experimental import pallas as pl
from jax.experimental.pallas import tpu as pltpu
from jax.sharding import PartitionSpec as P

SWEEPS = 4
F32, BF16 = jnp.float32, jnp.bfloat16
CH = 512
TILE = 128
EDGE_LIMIT = 57
FIRST_LIMIT = 20


def lane_of(shape):
    return lax.broadcasted_iota(jnp.int32, shape, 1)


def dot_t(a, b):
    return lax.dot_general(a, b, (((1,), (1,)), ((), ())), preferred_element_type=F32)


def split(x):
    hi = x.astype(BF16)
    return hi, (x - hi.astype(F32)).astype(BF16)


def spread(x):
    hi = x.astype(BF16).astype(F32)
    lo = (x - hi).astype(BF16).astype(F32)
    lane = lane_of((x.shape[0], TILE))
    return jnp.where(lane == 0, hi, jnp.where(lane == 1, lo, 0.0)).astype(BF16)


def column(tile, at):
    return tile[:, at : at + 1].astype(F32) + tile[:, at + 1 : at + 2].astype(F32)


GROUP = 16


def by_rows(rows, run):
    for at in range(0, rows, GROUP):
        run(slice(at, at + GROUP))


def operator(read, first, last, total, coefs, before, after, emit):
    dg_ref, cp_ref = coefs
    lane = lane_of((GROUP, TILE))
    cur = read(first)
    down = pltpu.roll(cur, TILE - 1, 1)
    prev = before if before is not None else pltpu.roll(read(first - 1), 1, 1)
    for t in range(first, last):
        up = pltpu.roll(cur, 1, 1)
        if t + 1 < last or after is None:
            ahead = read(t + 1)
            ahead_down = pltpu.roll(ahead, TILE - 1, 1)
        else:
            ahead, ahead_down = None, after
        left = jnp.where(lane == 0, prev, up)
        right = jnp.where(lane == TILE - 1, ahead_down, down)
        cols = slice(total + t * TILE, total + (t + 1) * TILE)
        emit(t, cur, dg_ref[:, cols] * cur - cp_ref[:, cols] * (left + right))
        cur, down, prev = ahead, ahead_down, up


def parts(v_ref, u0_ref, u3_ref, own):
    tiles, outer = v_ref.shape[1] // TILE, own // TILE

    def get(rows, t):
        if t < outer:
            return u0_ref[rows, t * TILE : (t + 1) * TILE]
        if t >= tiles - outer:
            t = t - (tiles - outer)
            return u3_ref[rows, t * TILE : (t + 1) * TILE]
        return v_ref[rows, t * TILE : (t + 1) * TILE]

    return get


def sweep_residual(r_ref, get, coefs, s_ref):
    rows, total = r_ref.shape

    def run(group):
        def emit(t, cur, image):
            cols = slice(t * TILE, (t + 1) * TILE)
            s_ref[group, cols] = (r_ref[group, cols] - image).astype(BF16)

        operator(lambda t: get(group, t), 0, total // TILE, 0, coefs, 0.0, 0.0, emit)

    by_rows(rows, run)


def pick(core_ref, a_ref, b_ref, left_ref, right_ref):
    @pl.when(core_ref[0] == 0)
    def _():
        left_ref[...] = b_ref[...]
        right_ref[...] = a_ref[...]

    @pl.when(core_ref[0] != 0)
    def _():
        left_ref[...] = a_ref[...]
        right_ref[...] = b_ref[...]


def first_edges(core_ref, r_hbm, cp_hbm, basis_hbm, ci_hbm, a_ref, b_ref,
                r_ref, cp_ref, basis_ref, ci_ref, left_ref, right_ref, sem):
    rows, total = r_hbm.shape
    subs, modes, own = basis_hbm.shape
    copies = []
    for k, (at, sub, tile_lo, cp_lo) in enumerate(
        ((0, 0, 0, 0), (total - CH, subs - 1, own - TILE, total - TILE))
    ):
        for n, (src, dst) in enumerate(
            (
                (r_hbm.at[:, pl.ds(at, CH)], r_ref.at[k]),
                (cp_hbm.at[:, pl.ds(cp_lo, TILE)], cp_ref.at[k]),
                (basis_hbm.at[sub, :, pl.ds(tile_lo, TILE)], basis_ref.at[k]),
                (ci_hbm.at[pl.ds(sub * modes, modes), :], ci_ref.at[k]),
            )
        ):
            copies.append(pltpu.make_async_copy(src, dst, sem.at[4 * k + n]))
    for c in copies:
        c.start()
    for c in copies:
        c.wait()
    lane = lane_of((modes, TILE))
    for k, (out, col, roll) in enumerate(((left_ref, 0, 2), (right_ref, TILE - 1, 3))):
        out[:, :CH] = r_ref[k].astype(BF16)
        one = cp_ref[k][:, col : col + 1]
        meta = spread(jnp.broadcast_to(one, (rows, 1))).astype(F32)
        weight = basis_ref[k].astype(F32)
        edge = pltpu.roll(weight, roll, 1) * one
        hi = edge.astype(BF16).astype(F32)
        lo = pltpu.roll(edge - hi, 1, 1)
        both = jnp.where(lane == 2, hi, jnp.where(lane == 3, lo, 0.0))
        out[:, CH : CH + TILE] = meta.astype(BF16)
        out[:modes, CH : CH + TILE] = (meta[:modes] + both).astype(BF16)
        line = jnp.sum(weight[:, col : col + 1] * ci_ref[k], axis=0, keepdims=True)
        count = line.shape[1] // TILE
        out[:, CH + TILE :] = jnp.zeros((rows, TILE), BF16)
        out[:count, CH + TILE :] = jnp.concatenate(
            [line[:, n * TILE : (n + 1) * TILE] for n in range(count)], axis=0
        ).astype(BF16)
    def send(even):
        a_ref[...] = (right_ref if even else left_ref)[...]
        b_ref[...] = (left_ref if even else right_ref)[...]

    by_side(core_ref, send)


def by_side(core_ref, run):
    pl.when(core_ref[0] == 0)(lambda: run(True))
    pl.when(core_ref[0] != 0)(lambda: run(False))


def lines_of(core_ref, ci_ref, a_ref, b_ref, out_ref, left_ref, right_ref):
    pick(core_ref, a_ref, b_ref, left_ref, right_ref)
    rows, width = ci_ref.shape
    out_ref[:rows, :] = ci_ref[...].astype(BF16)
    extra = []
    for ref in (left_ref, right_ref):
        block = ref[:, CH + TILE :].astype(F32)
        extra.append(
            jnp.concatenate([block[k : k + 1, :] for k in range(width // TILE)], axis=1)
        )
    extra.append(jnp.zeros((6, width), F32))
    out_ref[rows:, :] = jnp.concatenate(extra, axis=0).astype(BF16)


def weave(core_ref, mine_ref, other_ref, out_ref, all_ref):
    rows, half = mine_ref.shape
    low = core_ref[3] == 0

    @pl.when(low)
    def _():
        all_ref[:, TILE : TILE + half] = mine_ref[...].astype(F32)
        all_ref[:, TILE + half : TILE + 2 * half] = other_ref[...].astype(F32)

    @pl.when(jnp.logical_not(low))
    def _():
        all_ref[:, TILE : TILE + half] = other_ref[...].astype(F32)
        all_ref[:, TILE + half : TILE + 2 * half] = mine_ref[...].astype(F32)

    all_ref[:, :TILE] = all_ref[:, 2 * half : 2 * half + TILE]
    all_ref[:, 2 * half + TILE :] = all_ref[:, TILE : 2 * TILE]
    lane = lane_of((rows, TILE))
    core = core_ref[0]
    zero = jnp.zeros((rows, TILE), F32)

    def step(k, carry):
        at = pl.multiple_of(k * TILE, TILE)
        prev = all_ref[:, pl.ds(at, TILE)]
        tile = all_ref[:, pl.ds(pl.multiple_of(at + TILE, TILE), TILE)]
        after = all_ref[:, pl.ds(pl.multiple_of(at + 2 * TILE, TILE), TILE)]
        near = pltpu.roll(tile, 16, 1)
        even = jnp.where(lane < 64, tile, jnp.where(lane < 80, pltpu.roll(prev, 80, 1), near))
        odd = jnp.where(lane < 64, pltpu.roll(tile, 64, 1), jnp.where(lane < 80, near, pltpu.roll(after, 80, 1)))
        at = 2 * k * TILE
        out_ref[:, pl.ds(pl.multiple_of(at + core * TILE, TILE), TILE)] = jnp.where(
            lane < 96, even, zero
        ).astype(BF16)
        out_ref[:, pl.ds(pl.multiple_of(at + (1 - core) * TILE, TILE), TILE)] = jnp.where(
            lane < 96, odd, zero
        ).astype(BF16)
        return carry

    lax.fori_loop(0, 2 * half // TILE, step, 0, unroll=min(4, 2 * half // TILE))


def products(s_ref, L_ref, own, order, store, ready=None):
    total = s_ref.shape[1]
    margin = (order - own) // 2
    subs = L_ref.shape[0]
    part = own // 2
    quarter = own // 4

    def rows_at(k, part=part):
        return pl.ds(pl.multiple_of(k * part, part), part)

    def first(k, carry):
        p = dot_t(s_ref[:, TILE : order - margin], L_ref[0, rows_at(k, quarter), margin + TILE :])
        store(pl.multiple_of(k * quarter, quarter), quarter, p)
        return carry

    def last(k, carry):
        start = (subs - 1) * own - margin
        p = dot_t(
            s_ref[:, start : total - TILE],
            L_ref[subs - 1, rows_at(k), : total - TILE - start],
        )
        store(pl.multiple_of((subs - 1) * own + k * part, part), part, p)
        return carry

    def inner(n, carry):
        j, k = 1 + n // 2, n % 2
        if ready is not None:
            pl.when(k == 0)(lambda: ready(j))
        start = pl.multiple_of(j * own - margin, TILE)
        p = dot_t(s_ref[:, pl.ds(start, order)], L_ref[j, rows_at(k), :])
        store(pl.multiple_of(j * own + k * part, part), part, p)
        return carry

    if ready is not None:
        ready(0)
    lax.fori_loop(0, 4, first, 0)
    lax.fori_loop(0, 2 * (subs - 2), inner, 0)
    if ready is not None:
        ready(subs - 1)
    lax.fori_loop(0, 2, last, 0)


def middle_first(r_ref, L_hbm, v_ref, L_ref, s_ref, sem):
    subs, own, order = L_ref.shape

    def copy(j):
        return pltpu.make_async_copy(L_hbm.at[j], L_ref.at[j], sem.at[j])

    for j in range(subs):
        copy(j).start()
    s_ref[...] = r_ref[...].astype(BF16)

    def store(at, size, p):
        v_ref[:, pl.ds(at, size)] = p

    products(s_ref, L_ref, own, order, store, lambda j: copy(j).wait())


def complete(v_ref, near_l_ref, near_r_ref, wl_ref, wr_ref, L_ref, u0_ref, u3_ref):
    subs, own, order = L_ref.shape
    total, wide = v_ref.shape[1], wl_ref.shape[1]
    u0_ref[:, :wide] = near_l_ref[...]
    u0_ref[:, wide:] = v_ref[:, wide:own] + dot_t(wl_ref[...], L_ref[0, wide:, :wide])
    u3_ref[:, own - wide :] = near_r_ref[...]
    u3_ref[:, : own - wide] = v_ref[:, total - own : total - wide] + dot_t(
        wr_ref[...], L_ref[subs - 1, : own - wide, order - wide :]
    )


def middle_near(r_ref, v_ref, near_l_ref, near_r_ref, wl_ref, wr_ref, dg_ref, cp_ref, L_ref,
                out_ref, s_ref, u0_ref, u3_ref):
    complete(v_ref, near_l_ref, near_r_ref, wl_ref, wr_ref, L_ref, u0_ref, u3_ref)
    middle(r_ref, v_ref, u0_ref, u3_ref, dg_ref, cp_ref, L_ref, out_ref, s_ref)


def middle(r_ref, v_ref, u0_ref, u3_ref, dg_ref, cp_ref, L_ref, out_ref, s_ref):
    subs, own, order = L_ref.shape
    total = r_ref.shape[1]
    margin = (order - own) // 2
    sweep_residual(r_ref, parts(v_ref, u0_ref, u3_ref, own), (dg_ref, cp_ref), s_ref)

    for j, u_ref in ((0, u0_ref), (subs - 1, u3_ref)):
        at = j * own
        lo = at - margin
        a, b = max(lo, TILE), min(lo + order, total - TILE)
        out_ref[:, at : at + own] = u_ref[...] + dot_t(
            s_ref[:, a:b], L_ref[j, :, a - lo : b - lo]
        )

    def inner(j, carry):
        at = pl.multiple_of(j * own, own)
        p = dot_t(s_ref[:, pl.ds(pl.multiple_of(at - margin, TILE), order)], L_ref[j])
        out_ref[:, pl.ds(at, own)] = v_ref[:, pl.ds(at, own)] + p
        return carry

    lax.fori_loop(1, subs - 1, inner, 0)


def edge_sends(r_ref, dg_ref, cp_ref, u0_ref, u3_ref, left_ref, right_ref):
    rows, total = r_ref.shape
    own = u0_ref.shape[1]
    count, tiles = CH // TILE, own // TILE
    shift = total - own

    def run(group):
        def left(t, cur, image):
            cols = slice(t * TILE, (t + 1) * TILE)
            left_ref[group, cols] = (r_ref[group, cols] - image).astype(BF16)

        def right(t, cur, image):
            cols = slice(shift + t * TILE, shift + (t + 1) * TILE)
            k = (t - (tiles - count)) * TILE
            right_ref[group, k : k + TILE] = (r_ref[group, cols] - image).astype(BF16)

        read = lambda ref: lambda t: ref[group, t * TILE : (t + 1) * TILE]
        operator(read(u0_ref), 0, count, 0, (dg_ref, cp_ref), 0.0, None, left)
        operator(
            read(u3_ref), tiles - count, tiles, shift, (dg_ref, cp_ref), None, 0.0, right
        )

    by_rows(rows, run)
    left_ref[:, CH : CH + TILE] = spread(u0_ref[:, :1])
    right_ref[:, CH : CH + TILE] = spread(u3_ref[:, own - 1 :])


def edges(first, *refs):
    (core_ref, v_ref, gota_ref, gotb_ref, owna_ref, ownb_ref, metaa_ref, metab_ref) = refs[:8]
    (r_ref, dg_ref, cp_ref, L_ref, u0_ref, u3_ref, wl_ref, wr_ref) = refs[8:16]
    (senda_ref, sendb_ref, info_ref, sl_ref, sr_ref) = refs[16:]
    total = v_ref.shape[1]
    subs, own, order = L_ref.shape
    wide = CH + TILE
    spreads = slice(CH, wide)

    def gather(even):
        a, b = (gota_ref, owna_ref, metaa_ref), (gotb_ref, ownb_ref, metab_ref)
        (gl, ol, ml), (gr, orr, mr) = (b, a) if even else (a, b)
        wl_ref[:, :CH] = gl[:, :CH]
        wl_ref[:, CH:] = ol[:, :TILE]
        wr_ref[:, :TILE] = orr[:, CH - TILE : CH]
        wr_ref[:, TILE:] = gr[:, :CH]
        if not first:
            for k, ref in enumerate((gl, gr, ol, orr, ml, mr)):
                info_ref[k] = ref[:, spreads]

    by_side(core_ref, gather)
    if not first:
        rim_l, rim_r, mine_l, mine_r, coup_l, coup_r = (
            column(info_ref[k], 0) for k in range(6)
        )
        lane = lane_of((v_ref.shape[0], TILE))
        for ref, lo, at, y in (
            (wl_ref, CH, 0, cp_ref[:, :1] * rim_l),
            (wr_ref, 0, TILE - 1, cp_ref[:, total - 1 :] * rim_r),
            (wl_ref, CH - TILE, TILE - 1, coup_l * mine_l),
            (wr_ref, TILE, 0, coup_r * mine_r),
        ):
            x = ref[:, lo : lo + TILE].astype(F32)
            ref[:, lo : lo + TILE] = (x + jnp.where(lane == at, y, 0.0)).astype(BF16)
    u0_ref[...] = v_ref[:, :wide] + dot_t(wl_ref[...], L_ref[0, :wide, :wide])
    u3_ref[...] = v_ref[:, total - wide :] + dot_t(
        wr_ref[...], L_ref[subs - 1, own - wide :, order - wide :]
    )
    edge_sends(r_ref, dg_ref, cp_ref, u0_ref, u3_ref, sl_ref, sr_ref)

    def send(even):
        senda_ref[...] = (sr_ref if even else sl_ref)[...]
        sendb_ref[...] = (sl_ref if even else sr_ref)[...]

    by_side(core_ref, send)


def project(core_ref, v_ref, near_l_ref, near_r_ref, wl_ref, wr_ref, L_ref, r_ref, dg_ref, cp_ref,
            basis_ref, metaa_ref, metab_ref, unused_a, unused_b, out_ref, u0_ref, u3_ref,
            s_ref, metal_ref, metar_ref):
    complete(v_ref, near_l_ref, near_r_ref, wl_ref, wr_ref, L_ref, u0_ref, u3_ref)
    rows, total = r_ref.shape
    own = basis_ref.shape[2]
    modes = basis_ref.shape[1]
    get = parts(v_ref, u0_ref, u3_ref, own)
    lane = lane_of((rows, TILE))

    def meta_of(even):
        metal_ref[...] = (metab_ref if even else metaa_ref)[:modes, CH : CH + TILE]
        metar_ref[...] = (metaa_ref if even else metab_ref)[:modes, CH : CH + TILE]

    by_side(core_ref, meta_of)
    sweep_residual(r_ref, get, (dg_ref, cp_ref), s_ref)
    pieces = [
        dot_t(s_ref[:, j * own : (j + 1) * own], basis_ref[j]) for j in range(total // own)
    ]
    first, last = u0_ref[:, :1], u3_ref[:, own - 1 :]
    chosen = (lane == 2) | (lane == 3)
    for value, meta in ((first, metal_ref), (last, metar_ref)):
        hi, lo = split(value)
        coef = meta[...]
        pieces.append(
            dot_t(jnp.where(chosen, hi.astype(F32), 0.0).astype(BF16), coef)
            + dot_t(jnp.where(chosen, lo.astype(F32), 0.0).astype(BF16), coef)
        )
    rims = jnp.zeros((rows, 32), F32)
    lane32 = lane_of((rows, 32))
    for k, value in enumerate((first, last)):
        hi, lo = split(value)
        rims = jnp.where(lane32 == 2 * k, hi.astype(F32), rims)
        rims = jnp.where(lane32 == 2 * k + 1, lo.astype(F32), rims)
    chunk = jnp.concatenate(pieces + [rims], axis=1).astype(BF16)
    for d in range(out_ref.shape[0]):
        out_ref[d] = chunk


def coarse(core_ref, mine_ref, other_ref, W_ref, v_ref, u0_ref, u3_ref, r_ref, dg_ref, cp_ref,
           basis_ref, x_ref, image_ref, sums_ref, a_ref, b_ref, both_ref, rims_ref):
    rows, total = r_ref.shape
    own = basis_ref.shape[2]
    modes = basis_ref.shape[1]
    count = mine_ref.shape[0]
    group = min(8, count)
    c = None
    for k in range(0, count, group):
        tiles = []
        for d in range(k, k + group):
            tiles += [mine_ref[d], other_ref[d]]
        p = dot_t(
            jnp.concatenate(tiles, axis=1), W_ref[:, 2 * k * TILE : 2 * (k + group) * TILE]
        )
        c = p if c is None else c + p
    subs = total // own
    for j in range(subs):
        hi, lo = split(c[:, j * modes : (j + 1) * modes])
        both = jnp.concatenate([hi, lo], axis=1)
        at = j * own
        b = basis_ref[j]
        u = u0_ref[...] if j == 0 else u3_ref[...] if j == subs - 1 else v_ref[:, at : at + own]
        x_ref[:, at : at + own] = u + jnp.dot(
            both, jnp.concatenate([b, b], axis=0), preferred_element_type=F32
        )
    n = subs * modes
    before = other_ref[core_ref[1]]
    after = other_ref[core_ref[2]]
    rim_l = column(before, 98) + c[:, n : n + 1]
    rim_r = column(after, 96) + c[:, n + 1 : n + 2]
    rims_ref[0] = jnp.broadcast_to(rim_l, (rows, TILE))
    rims_ref[1] = jnp.broadcast_to(rim_r, (rows, TILE))

    def run(group):
        acc = [jnp.zeros((GROUP, TILE), F32)] * 2

        def emit(t, cur, image):
            cols = slice(t * TILE, (t + 1) * TILE)
            image_ref[group, cols] = image
            acc[0] = acc[0] + r_ref[group, cols] * image
            acc[1] = acc[1] + image * image

        operator(
            lambda t: x_ref[group, t * TILE : (t + 1) * TILE], 0, total // TILE, 0,
            (dg_ref, cp_ref), rims_ref[0, group, :], rims_ref[1, group, :], emit,
        )
        for k in range(2):
            both_ref[k, group, :] = jnp.broadcast_to(
                jnp.sum(acc[k], axis=1, keepdims=True), (GROUP, TILE)
            )

    by_rows(rows, run)
    flat = jnp.transpose(jnp.concatenate([both_ref[0], both_ref[1]], axis=0))
    sums_ref[...] = flat[: sums_ref.shape[0]]

    def send(even):
        (b_ref if even else a_ref)[...] = image_ref[:, :CH].astype(BF16)
        (a_ref if even else b_ref)[...] = image_ref[:, total - CH :].astype(BF16)

    by_side(core_ref, send)


def step_of(sums_ref, rows):
    s = jnp.sum(sums_ref[...], axis=0, keepdims=True)
    t = jnp.transpose(jnp.broadcast_to(s, (2 * rows, 2 * rows)))
    return t[:rows, :1] / (t[rows:, :1] + 1e-6)


def second(core_ref, sums_ref, x_ref, image_ref, r_ref, ha0_ref, hb0_ref, ha_ref, hb_ref,
           dg_ref, cp_ref, L_ref, sol_ref, res_ref, u_ref, u0_ref, u3_ref, a_ref, b_ref,
           s_ref, sl_ref, sr_ref):
    rows, total = r_ref.shape
    own, order = L_ref.shape[1], L_ref.shape[2]
    alpha = step_of(sums_ref, rows)

    def halo(even):
        for at, one in ((0, even), (CH + total, not even)):
            old, new = (hb0_ref, hb_ref) if one else (ha0_ref, ha_ref)
            s_ref[:, at : at + CH] = (
                old[:, :CH].astype(F32) - alpha * new[...].astype(F32)
            ).astype(BF16)

    by_side(core_ref, halo)
    for lo in range(0, total, TILE):
        cols = slice(lo, lo + TILE)
        r = r_ref[:, cols] - alpha * image_ref[:, cols]
        res_ref[:, cols] = r
        sol_ref[:, cols] = alpha * x_ref[:, cols]
        s_ref[:, CH + lo : CH + lo + TILE] = r.astype(BF16)
    subs = L_ref.shape[0]

    u0_ref[...] = dot_t(s_ref[:, :order], L_ref[0])
    u3_ref[...] = dot_t(s_ref[:, total - own :], L_ref[subs - 1])
    u_ref[:, :own] = u0_ref[...]
    u_ref[:, total - own :] = u3_ref[...]

    def step(j, carry):
        at = pl.multiple_of(j * own, own)
        u_ref[:, pl.ds(at, own)] = dot_t(s_ref[:, pl.ds(at, order)], L_ref[j])
        return carry

    lax.fori_loop(1, subs - 1, step, 0)
    edge_sends(res_ref, dg_ref, cp_ref, u0_ref, u3_ref, sl_ref, sr_ref)

    def send(even):
        a_ref[...] = (sr_ref if even else sl_ref)[...]
        b_ref[...] = (sl_ref if even else sr_ref)[...]

    by_side(core_ref, send)


def finish(sums_ref, x_ref, image_ref, r_ref, sol_in_ref, unused_a, unused_b, sol_ref, res_ref):
    rows, total = r_ref.shape
    alpha = step_of(sums_ref, rows)
    width = total // 4

    def half(k, carry):
        cols = pl.ds(pl.multiple_of(k * width, width), width)
        res_ref[:, cols] = r_ref[:, cols] - alpha * image_ref[:, cols]
        sol_ref[:, cols] = sol_in_ref[:, cols] + alpha * x_ref[:, cols]
        return carry

    lax.fori_loop(0, 4, half, 0)


def call(kernel, name, outs, args, scratch=(), limit=8, flops=0, smem=1, specs=None):
    vmem = pl.BlockSpec(memory_space=pltpu.VMEM)
    size = sum(a.size * a.dtype.itemsize for a in args)
    return pl.pallas_call(
        kernel,
        out_shape=outs,
        in_specs=specs
        or [pl.BlockSpec(memory_space=pltpu.SMEM)] * smem + [vmem] * (len(args) - smem),
        out_specs=jax.tree.map(lambda _: vmem, outs),
        scratch_shapes=list(scratch),
        compiler_params=pltpu.CompilerParams(vmem_limit_bytes=limit << 20),
        cost_estimate=pl.CostEstimate(flops=flops, bytes_accessed=size, transcendentals=0),
        name=name,
    )(*args)


def body(right_side, diagonal, coupling, local_inverse, coarse_basis, coarse_inverse):
    rows, total = right_side.shape
    subs, own, order = local_inverse.shape
    modes = coarse_basis.shape[1]
    sectors = lax.axis_size("sector")
    chip = [(i, i ^ 1) for i in range(sectors)]
    side = [(i, (i + 1 if i % 2 else i - 1) % sectors) for i in range(sectors)]
    planes = [[2 * k + c for k in range(sectors // 2)] for c in range(2)]
    here = lax.axis_index("sector")
    core = jnp.stack(
        [
            here % 2,
            (here + sectors - 1) % sectors // 2,
            (here + 1) % sectors // 2,
            lax.axis_index("lift"),
        ]
    ).astype(jnp.int32)
    L, basis = local_inverse, coarse_basis
    r = right_side
    dg, cp = diagonal.reshape(1, total), coupling.reshape(1, total)
    wide = CH + TILE
    shape = jax.ShapeDtypeStruct
    full = shape((rows, total), F32)
    sub = shape((rows, own), F32)
    near = shape((rows, wide), F32)
    send = shape((rows, wide), BF16)
    long = shape((rows, wide + TILE), BF16)
    s_scratch = pltpu.VMEM((rows, total), BF16)
    pair = lambda like: [pltpu.VMEM(like.shape, like.dtype)] * 2
    work = 2 * rows * subs * own * order

    def exchange(a, b):
        got_b = lax.ppermute(b, "sector", side)
        got_a = lax.ppermute(a, "sector", chip)
        return got_a, got_b

    hbm = pl.BlockSpec(memory_space=pltpu.HBM)
    sa, sb = call(
        first_edges, "first_edges", [long, long], [core, r, cp, basis, coarse_inverse],
        [
            pltpu.VMEM((2, rows, CH), F32),
            pltpu.VMEM((2, 1, TILE), F32),
            pltpu.VMEM((2, modes, TILE), BF16),
            pltpu.VMEM((2, modes, coarse_inverse.shape[1]), F32),
        ]
        + pair(long)
        + [pltpu.SemaphoreType.DMA((8,))],
        EDGE_LIMIT,
        specs=[pl.BlockSpec(memory_space=pltpu.SMEM)] + [hbm] * 4,
    )
    got_a0, got_b0 = exchange(sa, sb)
    v, L = call(
        middle_first, "middle_first", [full, shape(L.shape, L.dtype)], [r, L],
        [s_scratch, pltpu.SemaphoreType.DMA((subs,))],
        FIRST_LIMIT, work, specs=[pl.BlockSpec(memory_space=pltpu.VMEM), hbm],
    )
    weights = []

    def sweeps(v, u, sa, sb, start):
        for sweep in range(start, SWEEPS):
            last = sweep == SWEEPS - 1
            if sweep == 0:
                vv, ga, gb = v, got_a0, got_b0
            else:
                ga, gb = exchange(sa, sb)
                if len(u) == 2:
                    vv = call(
                        middle, "middle", full, [r, v, *u, dg, cp, L], [s_scratch], 8, work, 0
                    )
                else:
                    vv = call(
                        middle_near, "middle_near", full, [r, v, *u, dg, cp, L],
                        [s_scratch] + pair(sub), 8, work, 0,
                    )
            if sweep == 1 and not weights:
                ci, _ = lax.optimization_barrier((coarse_inverse, vv))
                lines = call(
                    lines_of, "lines", shape((ci.shape[0] + 8, ci.shape[1]), BF16),
                    [core, ci, got_a0, got_b0], pair(long),
                )
                other = lax.ppermute(lines, "lift", [(0, 1), (1, 0)])
                weights.append([lines, other])
            if last and len(weights) == 1:
                vv, *weights[0] = lax.optimization_barrier((vv, *weights[0]))
            first = sweep == 0
            *u, sa, sb = call(
                functools.partial(edges, first), "edges_first" if first else "edges",
                [near, near, send, send, send, send],
                [core, vv, ga, gb, sa, sb, got_a0, got_b0, r, dg, cp, L],
                [pltpu.VMEM((6, rows, TILE), BF16)] + pair(send),
                flops=work // 8,
            )
            v = vv
        return v, u, sa, sb

    edge = shape((rows, CH), BF16)

    def coarse_step(v, u, sa, sb):
        chunk, u0, u3 = call(
            project, "project", [shape((sectors // 2, rows, TILE), BF16), sub, sub],
            [core, v, *u, L, r, dg, cp, basis, got_a0, got_b0, sa, sb],
            [s_scratch] + [pltpu.VMEM((modes, TILE), BF16)] * 2,
        )
        mine = lax.all_to_all(
            chunk, "sector", 0, 0, axis_index_groups=planes, tiled=True
        )
        other = lax.ppermute(mine, "sector", chip)
        if len(weights) == 1:
            lines, swapped = weights[0]
            lines, swapped, _ = lax.optimization_barrier((lines, swapped, mine))
            weights.append(
                call(
                    weave, "weave", shape((lines.shape[0], sectors * TILE), BF16),
                    [core, lines, swapped],
                    [pltpu.VMEM((lines.shape[0], 2 * lines.shape[1] + 2 * TILE), F32)],
                    flops=1 << 26,
                )
            )
        W = weights[1]
        return call(
            coarse, "coarse", [full, full, shape((sectors, 2 * rows), F32), edge, edge],
            [core, mine, other, W, v, u0, u3, r, dg, cp, basis],
            [pltpu.VMEM((2, rows, TILE), F32)] * 2,
        )

    v, u, sa, sb = sweeps(v, None, sa, sb, 0)
    x, image, sums, ia, ib = coarse_step(v, u, sa, sb)
    halo_a, halo_b = exchange(ia, ib)
    sums = lax.all_to_all(sums, "sector", 0, 0, tiled=True)
    sol, r, v, u0, u3, sa, sb = call(
        second, "second", [full, full, full, sub, sub, send, send],
        [core, sums, x, image, r, got_a0, got_b0, halo_a, halo_b, dg, cp, L],
        [pltpu.VMEM((rows, total + 2 * CH), BF16)] + pair(send), 8, work,
    )
    v, u, sa, sb = sweeps(v, (u0, u3), sa, sb, 1)
    x, image, sums, ia, ib = coarse_step(v, u, sa, sb)
    sums = lax.all_to_all(sums, "sector", 0, 0, tiled=True)
    sol, res = call(finish, "finish", [full, full], [sums, x, image, r, sol, ia, ib], smem=0)
    return sol, res


def solution(mesh):
    in_specs = (
        P("lift", "sector"),
        P("sector"),
        P("sector"),
        P("sector", None, None),
        P("sector", None, None),
        P("sector", "lift"),
    )
    out_specs = (P("lift", "sector"), P("lift", "sector"))
    return jax.shard_map(body, mesh=mesh, in_specs=in_specs, out_specs=out_specs, check_vma=False)
```

```python
import functools

import jax
import jax.numpy as jnp
from jax import lax
from jax.experimental import pallas as pl
from jax.experimental.pallas import tpu as pltpu
from jax.sharding import PartitionSpec as P

SWEEPS = 4
F32, BF16 = jnp.float32, jnp.bfloat16
CH = 512
TILE = 128
EDGE_LIMIT = 57
FIRST_LIMIT = 20


def lane_of(shape):
    return lax.broadcasted_iota(jnp.int32, shape, 1)


def dot_t(a, b):
    return lax.dot_general(a, b, (((1,), (1,)), ((), ())), preferred_element_type=F32)


def split(x):
    hi = x.astype(BF16)
    return hi, (x - hi.astype(F32)).astype(BF16)


def spread(x):
    hi = x.astype(BF16).astype(F32)
    lo = (x - hi).astype(BF16).astype(F32)
    lane = lane_of((x.shape[0], TILE))
    return jnp.where(lane == 0, hi, jnp.where(lane == 1, lo, 0.0)).astype(BF16)


def column(tile, at):
    return tile[:, at : at + 1].astype(F32) + tile[:, at + 1 : at + 2].astype(F32)


GROUP = 16


def by_rows(rows, run):
    for at in range(0, rows, GROUP):
        run(slice(at, at + GROUP))


def operator(read, first, last, total, coefs, before, after, emit):
    dg_ref, cp_ref = coefs
    lane = lane_of((GROUP, TILE))
    cur = read(first)
    down = pltpu.roll(cur, TILE - 1, 1)
    prev = before if before is not None else pltpu.roll(read(first - 1), 1, 1)
    for t in range(first, last):
        up = pltpu.roll(cur, 1, 1)
        if t + 1 < last or after is None:
            ahead = read(t + 1)
            ahead_down = pltpu.roll(ahead, TILE - 1, 1)
        else:
            ahead, ahead_down = None, after
        left = jnp.where(lane == 0, prev, up)
        right = jnp.where(lane == TILE - 1, ahead_down, down)
        cols = slice(total + t * TILE, total + (t + 1) * TILE)
        emit(t, cur, dg_ref[:, cols] * cur - cp_ref[:, cols] * (left + right))
        cur, down, prev = ahead, ahead_down, up


def parts(v_ref, u0_ref, u3_ref, own):
    tiles, outer = v_ref.shape[1] // TILE, own // TILE

    def get(rows, t):
        if t < outer:
            return u0_ref[rows, t * TILE : (t + 1) * TILE]
        if t >= tiles - outer:
            t = t - (tiles - outer)
            return u3_ref[rows, t * TILE : (t + 1) * TILE]
        return v_ref[rows, t * TILE : (t + 1) * TILE]

    return get


def sweep_residual(r_ref, get, coefs, s_ref):
    rows, total = r_ref.shape

    def run(group):
        def emit(t, cur, image):
            cols = slice(t * TILE, (t + 1) * TILE)
            s_ref[group, cols] = (r_ref[group, cols] - image).astype(BF16)

        operator(lambda t: get(group, t), 0, total // TILE, 0, coefs, 0.0, 0.0, emit)

    by_rows(rows, run)


def pick(core_ref, a_ref, b_ref, left_ref, right_ref):
    @pl.when(core_ref[0] == 0)
    def _():
        left_ref[...] = b_ref[...]
        right_ref[...] = a_ref[...]

    @pl.when(core_ref[0] != 0)
    def _():
        left_ref[...] = a_ref[...]
        right_ref[...] = b_ref[...]


def first_edges(core_ref, r_hbm, cp_hbm, basis_hbm, ci_hbm, a_ref, b_ref,
                r_ref, cp_ref, basis_ref, ci_ref, left_ref, right_ref, sem):
    rows, total = r_hbm.shape
    subs, modes, own = basis_hbm.shape
    copies = []
    for k, (at, sub, tile_lo, cp_lo) in enumerate(
        ((0, 0, 0, 0), (total - CH, subs - 1, own - TILE, total - TILE))
    ):
        for n, (src, dst) in enumerate(
            (
                (r_hbm.at[:, pl.ds(at, CH)], r_ref.at[k]),
                (cp_hbm.at[:, pl.ds(cp_lo, TILE)], cp_ref.at[k]),
                (basis_hbm.at[sub, :, pl.ds(tile_lo, TILE)], basis_ref.at[k]),
                (ci_hbm.at[pl.ds(sub * modes, modes), :], ci_ref.at[k]),
            )
        ):
            copies.append(pltpu.make_async_copy(src, dst, sem.at[4 * k + n]))
    for c in copies:
        c.start()
    for c in copies:
        c.wait()
    lane = lane_of((modes, TILE))
    for k, (out, col, roll) in enumerate(((left_ref, 0, 2), (right_ref, TILE - 1, 3))):
        out[:, :CH] = r_ref[k].astype(BF16)
        one = cp_ref[k][:, col : col + 1]
        meta = spread(jnp.broadcast_to(one, (rows, 1))).astype(F32)
        weight = basis_ref[k].astype(F32)
        edge = pltpu.roll(weight, roll, 1) * one
        hi = edge.astype(BF16).astype(F32)
        lo = pltpu.roll(edge - hi, 1, 1)
        both = jnp.where(lane == 2, hi, jnp.where(lane == 3, lo, 0.0))
        out[:, CH : CH + TILE] = meta.astype(BF16)
        out[:modes, CH : CH + TILE] = (meta[:modes] + both).astype(BF16)
        line = jnp.sum(weight[:, col : col + 1] * ci_ref[k], axis=0, keepdims=True)
        count = line.shape[1] // TILE
        out[:, CH + TILE :] = jnp.zeros((rows, TILE), BF16)
        out[:count, CH + TILE :] = jnp.concatenate(
            [line[:, n * TILE : (n + 1) * TILE] for n in range(count)], axis=0
        ).astype(BF16)
    def send(even):
        a_ref[...] = (right_ref if even else left_ref)[...]
        b_ref[...] = (left_ref if even else right_ref)[...]

    by_side(core_ref, send)


def by_side(core_ref, run):
    pl.when(core_ref[0] == 0)(lambda: run(True))
    pl.when(core_ref[0] != 0)(lambda: run(False))


def lines_of(core_ref, ci_ref, a_ref, b_ref, out_ref, left_ref, right_ref):
    pick(core_ref, a_ref, b_ref, left_ref, right_ref)
    rows, width = ci_ref.shape
    out_ref[:rows, :] = ci_ref[...].astype(BF16)
    extra = []
    for ref in (left_ref, right_ref):
        block = ref[:, CH + TILE :].astype(F32)
        extra.append(
            jnp.concatenate([block[k : k + 1, :] for k in range(width // TILE)], axis=1)
        )
    extra.append(jnp.zeros((6, width), F32))
    out_ref[rows:, :] = jnp.concatenate(extra, axis=0).astype(BF16)


def weave(core_ref, mine_ref, other_ref, out_ref, all_ref):
    rows, half = mine_ref.shape
    low = core_ref[3] == 0

    @pl.when(low)
    def _():
        all_ref[:, TILE : TILE + half] = mine_ref[...].astype(F32)
        all_ref[:, TILE + half : TILE + 2 * half] = other_ref[...].astype(F32)

    @pl.when(jnp.logical_not(low))
    def _():
        all_ref[:, TILE : TILE + half] = other_ref[...].astype(F32)
        all_ref[:, TILE + half : TILE + 2 * half] = mine_ref[...].astype(F32)

    all_ref[:, :TILE] = all_ref[:, 2 * half : 2 * half + TILE]
    all_ref[:, 2 * half + TILE :] = all_ref[:, TILE : 2 * TILE]
    lane = lane_of((rows, TILE))
    core = core_ref[0]
    zero = jnp.zeros((rows, TILE), F32)

    def step(k, carry):
        at = pl.multiple_of(k * TILE, TILE)
        prev = all_ref[:, pl.ds(at, TILE)]
        tile = all_ref[:, pl.ds(pl.multiple_of(at + TILE, TILE), TILE)]
        after = all_ref[:, pl.ds(pl.multiple_of(at + 2 * TILE, TILE), TILE)]
        near = pltpu.roll(tile, 16, 1)
        even = jnp.where(lane < 64, tile, jnp.where(lane < 80, pltpu.roll(prev, 80, 1), near))
        odd = jnp.where(lane < 64, pltpu.roll(tile, 64, 1), jnp.where(lane < 80, near, pltpu.roll(after, 80, 1)))
        at = 2 * k * TILE
        out_ref[:, pl.ds(pl.multiple_of(at + core * TILE, TILE), TILE)] = jnp.where(
            lane < 96, even, zero
        ).astype(BF16)
        out_ref[:, pl.ds(pl.multiple_of(at + (1 - core) * TILE, TILE), TILE)] = jnp.where(
            lane < 96, odd, zero
        ).astype(BF16)
        return carry

    lax.fori_loop(0, 2 * half // TILE, step, 0, unroll=min(4, 2 * half // TILE))


def products(s_ref, L_ref, own, order, store, ready=None):
    total = s_ref.shape[1]
    margin = (order - own) // 2
    subs = L_ref.shape[0]
    part = own // 2
    quarter = own // 4

    def rows_at(k, part=part):
        return pl.ds(pl.multiple_of(k * part, part), part)

    def first(k, carry):
        p = dot_t(s_ref[:, TILE : order - margin], L_ref[0, rows_at(k, quarter), margin + TILE :])
        store(pl.multiple_of(k * quarter, quarter), quarter, p)
        return carry

    def last(k, carry):
        start = (subs - 1) * own - margin
        p = dot_t(
            s_ref[:, start : total - TILE],
            L_ref[subs - 1, rows_at(k), : total - TILE - start],
        )
        store(pl.multiple_of((subs - 1) * own + k * part, part), part, p)
        return carry

    def inner(n, carry):
        j, k = 1 + n // 2, n % 2
        if ready is not None:
            pl.when(k == 0)(lambda: ready(j))
        start = pl.multiple_of(j * own - margin, TILE)
        p = dot_t(s_ref[:, pl.ds(start, order)], L_ref[j, rows_at(k), :])
        store(pl.multiple_of(j * own + k * part, part), part, p)
        return carry

    if ready is not None:
        ready(0)
    lax.fori_loop(0, 4, first, 0)
    lax.fori_loop(0, 2 * (subs - 2), inner, 0)
    if ready is not None:
        ready(subs - 1)
    lax.fori_loop(0, 2, last, 0)


def middle_first(r_ref, L_hbm, v_ref, L_ref, s_ref, sem):
    subs, own, order = L_ref.shape

    def copy(j):
        return pltpu.make_async_copy(L_hbm.at[j], L_ref.at[j], sem.at[j])

    for j in range(subs):
        copy(j).start()
    s_ref[...] = r_ref[...].astype(BF16)

    def store(at, size, p):
        v_ref[:, pl.ds(at, size)] = p

    products(s_ref, L_ref, own, order, store, lambda j: copy(j).wait())


def complete(v_ref, near_l_ref, near_r_ref, wl_ref, wr_ref, L_ref, u0_ref, u3_ref):
    subs, own, order = L_ref.shape
    total, wide = v_ref.shape[1], wl_ref.shape[1]
    u0_ref[:, :wide] = near_l_ref[...]
    u0_ref[:, wide:] = v_ref[:, wide:own] + dot_t(wl_ref[...], L_ref[0, wide:, :wide])
    u3_ref[:, own - wide :] = near_r_ref[...]
    u3_ref[:, : own - wide] = v_ref[:, total - own : total - wide] + dot_t(
        wr_ref[...], L_ref[subs - 1, : own - wide, order - wide :]
    )


def middle_near(r_ref, v_ref, near_l_ref, near_r_ref, wl_ref, wr_ref, dg_ref, cp_ref, L_ref,
                out_ref, s_ref, u0_ref, u3_ref):
    complete(v_ref, near_l_ref, near_r_ref, wl_ref, wr_ref, L_ref, u0_ref, u3_ref)
    middle(r_ref, v_ref, u0_ref, u3_ref, dg_ref, cp_ref, L_ref, out_ref, s_ref)


def middle_second(r_ref, sin_ref, u0_ref, u3_ref, dg_ref, cp_ref, L_ref, out_ref, s_ref, v_ref):
    subs, own, order = L_ref.shape

    def step(j, carry):
        at = pl.multiple_of(j * own, own)
        v_ref[:, pl.ds(at, own)] = dot_t(sin_ref[:, pl.ds(at, order)], L_ref[j])
        return carry

    lax.fori_loop(1, subs - 1, step, 0)
    middle(r_ref, v_ref, u0_ref, u3_ref, dg_ref, cp_ref, L_ref, out_ref, s_ref)


def middle(r_ref, v_ref, u0_ref, u3_ref, dg_ref, cp_ref, L_ref, out_ref, s_ref):
    subs, own, order = L_ref.shape
    total = r_ref.shape[1]
    margin = (order - own) // 2
    sweep_residual(r_ref, parts(v_ref, u0_ref, u3_ref, own), (dg_ref, cp_ref), s_ref)

    for j, u_ref in ((0, u0_ref), (subs - 1, u3_ref)):
        at = j * own
        lo = at - margin
        a, b = max(lo, TILE), min(lo + order, total - TILE)
        out_ref[:, at : at + own] = u_ref[...] + dot_t(
            s_ref[:, a:b], L_ref[j, :, a - lo : b - lo]
        )

    def inner(j, carry):
        at = pl.multiple_of(j * own, own)
        p = dot_t(s_ref[:, pl.ds(pl.multiple_of(at - margin, TILE), order)], L_ref[j])
        out_ref[:, pl.ds(at, own)] = v_ref[:, pl.ds(at, own)] + p
        return carry

    lax.fori_loop(1, subs - 1, inner, 0)


def edge_sends(r_ref, dg_ref, cp_ref, u0_ref, u3_ref, left_ref, right_ref):
    rows, total = r_ref.shape
    own = u0_ref.shape[1]
    count, tiles = CH // TILE, own // TILE
    shift = total - own

    def run(group):
        def left(t, cur, image):
            cols = slice(t * TILE, (t + 1) * TILE)
            left_ref[group, cols] = (r_ref[group, cols] - image).astype(BF16)

        def right(t, cur, image):
            cols = slice(shift + t * TILE, shift + (t + 1) * TILE)
            k = (t - (tiles - count)) * TILE
            right_ref[group, k : k + TILE] = (r_ref[group, cols] - image).astype(BF16)

        read = lambda ref: lambda t: ref[group, t * TILE : (t + 1) * TILE]
        operator(read(u0_ref), 0, count, 0, (dg_ref, cp_ref), 0.0, None, left)
        operator(
            read(u3_ref), tiles - count, tiles, shift, (dg_ref, cp_ref), None, 0.0, right
        )

    by_rows(rows, run)
    left_ref[:, CH : CH + TILE] = spread(u0_ref[:, :1])
    right_ref[:, CH : CH + TILE] = spread(u3_ref[:, own - 1 :])


def edges(first, *refs):
    (core_ref, v_ref, gota_ref, gotb_ref, owna_ref, ownb_ref, metaa_ref, metab_ref) = refs[:8]
    (r_ref, dg_ref, cp_ref, L_ref, u0_ref, u3_ref, wl_ref, wr_ref) = refs[8:16]
    (senda_ref, sendb_ref, info_ref, sl_ref, sr_ref) = refs[16:]
    total = v_ref.shape[1]
    subs, own, order = L_ref.shape
    wide = CH + TILE
    spreads = slice(CH, wide)

    def gather(even):
        a, b = (gota_ref, owna_ref, metaa_ref), (gotb_ref, ownb_ref, metab_ref)
        (gl, ol, ml), (gr, orr, mr) = (b, a) if even else (a, b)
        wl_ref[:, :CH] = gl[:, :CH]
        wl_ref[:, CH:] = ol[:, :TILE]
        wr_ref[:, :TILE] = orr[:, CH - TILE : CH]
        wr_ref[:, TILE:] = gr[:, :CH]
        if not first:
            for k, ref in enumerate((gl, gr, ol, orr, ml, mr)):
                info_ref[k] = ref[:, spreads]

    by_side(core_ref, gather)
    if not first:
        rim_l, rim_r, mine_l, mine_r, coup_l, coup_r = (
            column(info_ref[k], 0) for k in range(6)
        )
        lane = lane_of((v_ref.shape[0], TILE))
        for ref, lo, at, y in (
            (wl_ref, CH, 0, cp_ref[:, :1] * rim_l),
            (wr_ref, 0, TILE - 1, cp_ref[:, total - 1 :] * rim_r),
            (wl_ref, CH - TILE, TILE - 1, coup_l * mine_l),
            (wr_ref, TILE, 0, coup_r * mine_r),
        ):
            x = ref[:, lo : lo + TILE].astype(F32)
            ref[:, lo : lo + TILE] = (x + jnp.where(lane == at, y, 0.0)).astype(BF16)
    u0_ref[...] = v_ref[:, :wide] + dot_t(wl_ref[...], L_ref[0, :wide, :wide])
    u3_ref[...] = v_ref[:, total - wide :] + dot_t(
        wr_ref[...], L_ref[subs - 1, own - wide :, order - wide :]
    )
    edge_sends(r_ref, dg_ref, cp_ref, u0_ref, u3_ref, sl_ref, sr_ref)

    def send(even):
        senda_ref[...] = (sr_ref if even else sl_ref)[...]
        sendb_ref[...] = (sl_ref if even else sr_ref)[...]

    by_side(core_ref, send)


def project(core_ref, v_ref, near_l_ref, near_r_ref, wl_ref, wr_ref, L_ref, r_ref, dg_ref, cp_ref,
            basis_ref, metaa_ref, metab_ref, unused_a, unused_b, out_ref, u0_ref, u3_ref,
            s_ref, metal_ref, metar_ref):
    complete(v_ref, near_l_ref, near_r_ref, wl_ref, wr_ref, L_ref, u0_ref, u3_ref)
    rows, total = r_ref.shape
    own = basis_ref.shape[2]
    modes = basis_ref.shape[1]
    get = parts(v_ref, u0_ref, u3_ref, own)
    lane = lane_of((rows, TILE))

    def meta_of(even):
        metal_ref[...] = (metab_ref if even else metaa_ref)[:modes, CH : CH + TILE]
        metar_ref[...] = (metaa_ref if even else metab_ref)[:modes, CH : CH + TILE]

    by_side(core_ref, meta_of)
    sweep_residual(r_ref, get, (dg_ref, cp_ref), s_ref)
    pieces = [
        dot_t(s_ref[:, j * own : (j + 1) * own], basis_ref[j]) for j in range(total // own)
    ]
    first, last = u0_ref[:, :1], u3_ref[:, own - 1 :]
    chosen = (lane == 2) | (lane == 3)
    for value, meta in ((first, metal_ref), (last, metar_ref)):
        hi, lo = split(value)
        coef = meta[...]
        pieces.append(
            dot_t(jnp.where(chosen, hi.astype(F32), 0.0).astype(BF16), coef)
            + dot_t(jnp.where(chosen, lo.astype(F32), 0.0).astype(BF16), coef)
        )
    rims = jnp.zeros((rows, 32), F32)
    lane32 = lane_of((rows, 32))
    for k, value in enumerate((first, last)):
        hi, lo = split(value)
        rims = jnp.where(lane32 == 2 * k, hi.astype(F32), rims)
        rims = jnp.where(lane32 == 2 * k + 1, lo.astype(F32), rims)
    chunk = jnp.concatenate(pieces + [rims], axis=1).astype(BF16)
    for d in range(out_ref.shape[0]):
        out_ref[d] = chunk


def coarse(core_ref, mine_ref, other_ref, W_ref, v_ref, u0_ref, u3_ref, r_ref, dg_ref, cp_ref,
           basis_ref, x_ref, image_ref, sums_ref, a_ref, b_ref, both_ref, rims_ref):
    rows, total = r_ref.shape
    own = basis_ref.shape[2]
    modes = basis_ref.shape[1]
    count = mine_ref.shape[0]
    group = min(8, count)
    c = None
    for k in range(0, count, group):
        tiles = []
        for d in range(k, k + group):
            tiles += [mine_ref[d], other_ref[d]]
        p = dot_t(
            jnp.concatenate(tiles, axis=1), W_ref[:, 2 * k * TILE : 2 * (k + group) * TILE]
        )
        c = p if c is None else c + p
    subs = total // own
    for j in range(subs):
        hi, lo = split(c[:, j * modes : (j + 1) * modes])
        both = jnp.concatenate([hi, lo], axis=1)
        at = j * own
        b = basis_ref[j]
        u = u0_ref[...] if j == 0 else u3_ref[...] if j == subs - 1 else v_ref[:, at : at + own]
        x_ref[:, at : at + own] = u + jnp.dot(
            both, jnp.concatenate([b, b], axis=0), preferred_element_type=F32
        )
    n = subs * modes
    before = other_ref[core_ref[1]]
    after = other_ref[core_ref[2]]
    rim_l = column(before, 98) + c[:, n : n + 1]
    rim_r = column(after, 96) + c[:, n + 1 : n + 2]
    rims_ref[0] = jnp.broadcast_to(rim_l, (rows, TILE))
    rims_ref[1] = jnp.broadcast_to(rim_r, (rows, TILE))

    def run(group):
        acc = [jnp.zeros((GROUP, TILE), F32)] * 2

        def emit(t, cur, image):
            cols = slice(t * TILE, (t + 1) * TILE)
            image_ref[group, cols] = image
            acc[0] = acc[0] + r_ref[group, cols] * image
            acc[1] = acc[1] + image * image

        operator(
            lambda t: x_ref[group, t * TILE : (t + 1) * TILE], 0, total // TILE, 0,
            (dg_ref, cp_ref), rims_ref[0, group, :], rims_ref[1, group, :], emit,
        )
        for k in range(2):
            both_ref[k, group, :] = jnp.broadcast_to(
                jnp.sum(acc[k], axis=1, keepdims=True), (GROUP, TILE)
            )

    by_rows(rows, run)
    flat = jnp.transpose(jnp.concatenate([both_ref[0], both_ref[1]], axis=0))
    sums_ref[...] = flat[: sums_ref.shape[0]]

    def send(even):
        (b_ref if even else a_ref)[...] = image_ref[:, :CH].astype(BF16)
        (a_ref if even else b_ref)[...] = image_ref[:, total - CH :].astype(BF16)

    by_side(core_ref, send)


def step_of(sums_ref, rows):
    s = jnp.sum(sums_ref[...], axis=0, keepdims=True)
    t = jnp.transpose(jnp.broadcast_to(s, (2 * rows, 2 * rows)))
    return t[:rows, :1] / (t[rows:, :1] + 1e-6)


def second(core_ref, sums_ref, x_ref, image_ref, r_ref, ha0_ref, hb0_ref, ha_ref, hb_ref,
           dg_ref, cp_ref, L_ref, sol_ref, res_ref, s_ref, u0_ref, u3_ref, a_ref, b_ref,
           sl_ref, sr_ref):
    rows, total = r_ref.shape
    own, order = L_ref.shape[1], L_ref.shape[2]
    alpha = step_of(sums_ref, rows)

    def halo(even):
        for at, one in ((0, even), (CH + total, not even)):
            old, new = (hb0_ref, hb_ref) if one else (ha0_ref, ha_ref)
            s_ref[:, at : at + CH] = (
                old[:, :CH].astype(F32) - alpha * new[...].astype(F32)
            ).astype(BF16)

    by_side(core_ref, halo)
    for lo in range(0, total, TILE):
        cols = slice(lo, lo + TILE)
        r = r_ref[:, cols] - alpha * image_ref[:, cols]
        res_ref[:, cols] = r
        sol_ref[:, cols] = alpha * x_ref[:, cols]
        s_ref[:, CH + lo : CH + lo + TILE] = r.astype(BF16)
    subs = L_ref.shape[0]

    u0_ref[...] = dot_t(s_ref[:, :order], L_ref[0])
    u3_ref[...] = dot_t(s_ref[:, total - own :], L_ref[subs - 1])
    edge_sends(res_ref, dg_ref, cp_ref, u0_ref, u3_ref, sl_ref, sr_ref)

    def send(even):
        a_ref[...] = (sr_ref if even else sl_ref)[...]
        b_ref[...] = (sl_ref if even else sr_ref)[...]

    by_side(core_ref, send)


def finish(sums_ref, x_ref, image_ref, r_ref, sol_in_ref, unused_a, unused_b, sol_ref, res_ref):
    rows, total = r_ref.shape
    alpha = step_of(sums_ref, rows)
    width = total // 4

    def half(k, carry):
        cols = pl.ds(pl.multiple_of(k * width, width), width)
        res_ref[:, cols] = r_ref[:, cols] - alpha * image_ref[:, cols]
        sol_ref[:, cols] = sol_in_ref[:, cols] + alpha * x_ref[:, cols]
        return carry

    lax.fori_loop(0, 4, half, 0)


def call(kernel, name, outs, args, scratch=(), limit=8, flops=0, smem=1, specs=None):
    vmem = pl.BlockSpec(memory_space=pltpu.VMEM)
    size = sum(a.size * a.dtype.itemsize for a in args)
    return pl.pallas_call(
        kernel,
        out_shape=outs,
        in_specs=specs
        or [pl.BlockSpec(memory_space=pltpu.SMEM)] * smem + [vmem] * (len(args) - smem),
        out_specs=jax.tree.map(lambda _: vmem, outs),
        scratch_shapes=list(scratch),
        compiler_params=pltpu.CompilerParams(vmem_limit_bytes=limit << 20),
        cost_estimate=pl.CostEstimate(flops=flops, bytes_accessed=size, transcendentals=0),
        name=name,
    )(*args)


def body(right_side, diagonal, coupling, local_inverse, coarse_basis, coarse_inverse):
    rows, total = right_side.shape
    subs, own, order = local_inverse.shape
    modes = coarse_basis.shape[1]
    sectors = lax.axis_size("sector")
    chip = [(i, i ^ 1) for i in range(sectors)]
    side = [(i, (i + 1 if i % 2 else i - 1) % sectors) for i in range(sectors)]
    planes = [[2 * k + c for k in range(sectors // 2)] for c in range(2)]
    here = lax.axis_index("sector")
    core = jnp.stack(
        [
            here % 2,
            (here + sectors - 1) % sectors // 2,
            (here + 1) % sectors // 2,
            lax.axis_index("lift"),
        ]
    ).astype(jnp.int32)
    L, basis = local_inverse, coarse_basis
    r = right_side
    dg, cp = diagonal.reshape(1, total), coupling.reshape(1, total)
    wide = CH + TILE
    shape = jax.ShapeDtypeStruct
    full = shape((rows, total), F32)
    sub = shape((rows, own), F32)
    near = shape((rows, wide), F32)
    send = shape((rows, wide), BF16)
    long = shape((rows, wide + TILE), BF16)
    s_scratch = pltpu.VMEM((rows, total), BF16)
    pair = lambda like: [pltpu.VMEM(like.shape, like.dtype)] * 2
    work = 2 * rows * subs * own * order

    def exchange(a, b):
        got_b = lax.ppermute(b, "sector", side)
        got_a = lax.ppermute(a, "sector", chip)
        return got_a, got_b

    hbm = pl.BlockSpec(memory_space=pltpu.HBM)
    sa, sb = call(
        first_edges, "first_edges", [long, long], [core, r, cp, basis, coarse_inverse],
        [
            pltpu.VMEM((2, rows, CH), F32),
            pltpu.VMEM((2, 1, TILE), F32),
            pltpu.VMEM((2, modes, TILE), BF16),
            pltpu.VMEM((2, modes, coarse_inverse.shape[1]), F32),
        ]
        + pair(long)
        + [pltpu.SemaphoreType.DMA((8,))],
        EDGE_LIMIT,
        specs=[pl.BlockSpec(memory_space=pltpu.SMEM)] + [hbm] * 4,
    )
    got_a0, got_b0 = exchange(sa, sb)
    v, L = call(
        middle_first, "middle_first", [full, shape(L.shape, L.dtype)], [r, L],
        [s_scratch, pltpu.SemaphoreType.DMA((subs,))],
        FIRST_LIMIT, work, specs=[pl.BlockSpec(memory_space=pltpu.VMEM), hbm],
    )
    weights = []

    def sweeps(v, u, sa, sb, start):
        for sweep in range(start, SWEEPS):
            last = sweep == SWEEPS - 1
            if sweep == 0:
                vv, ga, gb = v, got_a0, got_b0
            else:
                ga, gb = exchange(sa, sb)
                if len(u) == 2:
                    vv = call(
                        middle_second, "middle_second", full, [r, v, *u, dg, cp, L],
                        [s_scratch, pltpu.VMEM((rows, total), F32)], 8, work, 0,
                    )
                else:
                    vv = call(
                        middle_near, "middle_near", full, [r, v, *u, dg, cp, L],
                        [s_scratch] + pair(sub), 8, work, 0,
                    )
            if sweep == 1 and not weights:
                ci, _ = lax.optimization_barrier((coarse_inverse, vv))
                lines = call(
                    lines_of, "lines", shape((ci.shape[0] + 8, ci.shape[1]), BF16),
                    [core, ci, got_a0, got_b0], pair(long),
                )
                other = lax.ppermute(lines, "lift", [(0, 1), (1, 0)])
                weights.append([lines, other])
            if last and len(weights) == 1:
                vv, *weights[0] = lax.optimization_barrier((vv, *weights[0]))
            first = sweep == 0
            *u, sa, sb = call(
                functools.partial(edges, first), "edges_first" if first else "edges",
                [near, near, send, send, send, send],
                [core, vv, ga, gb, sa, sb, got_a0, got_b0, r, dg, cp, L],
                [pltpu.VMEM((6, rows, TILE), BF16)] + pair(send),
                flops=work // 8,
            )
            v = vv
        return v, u, sa, sb

    edge = shape((rows, CH), BF16)

    def coarse_step(v, u, sa, sb):
        chunk, u0, u3 = call(
            project, "project", [shape((sectors // 2, rows, TILE), BF16), sub, sub],
            [core, v, *u, L, r, dg, cp, basis, got_a0, got_b0, sa, sb],
            [s_scratch] + [pltpu.VMEM((modes, TILE), BF16)] * 2,
        )
        mine = lax.all_to_all(
            chunk, "sector", 0, 0, axis_index_groups=planes, tiled=True
        )
        other = lax.ppermute(mine, "sector", chip)
        if len(weights) == 1:
            lines, swapped = weights[0]
            lines, swapped, _ = lax.optimization_barrier((lines, swapped, mine))
            weights.append(
                call(
                    weave, "weave", shape((lines.shape[0], sectors * TILE), BF16),
                    [core, lines, swapped],
                    [pltpu.VMEM((lines.shape[0], 2 * lines.shape[1] + 2 * TILE), F32)],
                    flops=1 << 26,
                )
            )
        W = weights[1]
        return call(
            coarse, "coarse", [full, full, shape((sectors, 2 * rows), F32), edge, edge],
            [core, mine, other, W, v, u0, u3, r, dg, cp, basis],
            [pltpu.VMEM((2, rows, TILE), F32)] * 2,
        )

    v, u, sa, sb = sweeps(v, None, sa, sb, 0)
    x, image, sums, ia, ib = coarse_step(v, u, sa, sb)
    halo_a, halo_b = exchange(ia, ib)
    sums = lax.all_to_all(sums, "sector", 0, 0, tiled=True)
    sol, r, v, u0, u3, sa, sb = call(
        second, "second", [full, full, shape((rows, total + 2 * CH), BF16), sub, sub, send, send],
        [core, sums, x, image, r, got_a0, got_b0, halo_a, halo_b, dg, cp, L],
        pair(send), 8, work,
    )
    v, u, sa, sb = sweeps(v, (u0, u3), sa, sb, 1)
    x, image, sums, ia, ib = coarse_step(v, u, sa, sb)
    sums = lax.all_to_all(sums, "sector", 0, 0, tiled=True)
    sol, res = call(finish, "finish", [full, full], [sums, x, image, r, sol, ia, ib], smem=0)
    return sol, res


def solution(mesh):
    in_specs = (
        P("lift", "sector"),
        P("sector"),
        P("sector"),
        P("sector", None, None),
        P("sector", None, None),
        P("sector", "lift"),
    )
    out_specs = (P("lift", "sector"), P("lift", "sector"))
    return jax.shard_map(body, mesh=mesh, in_specs=in_specs, out_specs=out_specs, check_vma=False)
```
